32 devices in a mesh: dp: 2 (over y), ctx: 16 (over z, x, core).
Axes of the slice: x: 2, y: 2, z: 4, core: 2. Of those that a mesh axis runs over, the one named last changes fastest.
Arguments:
- inputs: bfloat16 [4, 2048, 768], P('dp', 'ctx'), may hold values from -6 to 6
- w_query: bfloat16 [768, 768], P(('dp', 'ctx')), may hold values from -0.0546875 to 0.0546875
- w_key: bfloat16 [768, 768], P(('dp', 'ctx')), may hold values from -0.21875 to 0.21875
- w_value: bfloat16 [768, 768], P(('dp', 'ctx')), may hold values from -0.21875 to 0.21875
- w_output: bfloat16 [768, 768], P(('dp', 'ctx')), may hold values from -1.25 to 1.25
- w_gate: bfloat16 [768, 2048], P(('dp', 'ctx')), may hold values from -0.21875 to 0.21875
- w_upper: bfloat16 [768, 2048], P(('dp', 'ctx')), may hold values from -0.21875 to 0.21875
- w_down: bfloat16 [2048, 768], P(('dp', 'ctx')), may hold values from -0.125 to 0.125
- gain_one: bfloat16 [768], P(('dp', 'ctx')), may hold values from 0.099609375 to 1.8984375
- gain_two: bfloat16 [768], P(('dp', 'ctx')), may hold values from 0.099609375 to 1.8984375
- bias_table: bfloat16 [384], P(('dp', 'ctx')), may hold values from -4 to 4
- buckets: int32 [4095], replicated, may hold values from 0 to 31
- cotangent: bfloat16 [4, 2048, 768], P('dp', 'ctx'), may hold values from -6 to 6
Outputs:
- outputs: bfloat16 [4, 2048, 768], P('dp', 'ctx')
- input_grad: float32 [4, 2048, 768], P('dp', 'ctx')
- grad_w_query: float32 [768, 768], P(('dp', 'ctx'))
- grad_w_key: float32 [768, 768], P(('dp', 'ctx'))
- grad_w_value: float32 [768, 768], P(('dp', 'ctx'))
- grad_w_output: float32 [768, 768], P(('dp', 'ctx'))
- grad_w_gate: float32 [768, 2048], P(('dp', 'ctx'))
- grad_w_upper: float32 [768, 2048], P(('dp', 'ctx'))
- grad_w_down: float32 [2048, 768], P(('dp', 'ctx'))
- grad_gain_one: float32 [768], P(('dp', 'ctx'))
- grad_gain_two: float32 [768], P(('dp', 'ctx'))
- grad_bias_table: float32 [384], P(('dp', 'ctx'))
The draws below stay inside these ranges and needn't reach their ends.
Inputs may be any that keep to these rules, and one draw needn't show every extreme that they name: `buckets`: each entry names a bucket of the bias table.
All inputs are finite; a program needn't handle non-finite values.
Results may differ from the reference program's by a relative error of at most 0.025.
Values may be sent and summed in bfloat16 or wider, within the bound.
No kernel may reach another device: no remote copies, remote signals or barrier semaphores. Data moves between devices by JAX's collectives and lax.ppermute only.
A program may use at most 320 MiB of HBM per device.

```python
import jax
import jax.numpy as jnp
from jax import lax

D = 768
H = 12
HD = 64
FF = 2048
BUCKETS = 32
LENGTH = 2048
SEQS = 4


def place_ends(array, own_key, low, top_value):
    longest = array.shape.index(max(array.shape))
    spots = []
    for shift in (0, 1):
        where = [jax.random.randint(jax.random.fold_in(own_key, axis), (), 0, length) for axis, length in enumerate(array.shape)]
        where[longest] = (where[longest] + shift) % array.shape[longest]
        spots.append(tuple(where))
    return array.at[spots[0]].set(low).at[spots[1]].set(top_value)


def levels(rng, extent, pieces, smallest, high):
    loudness = 1.0
    for dim, shards_of in pieces:
        heights = jax.random.uniform(jax.random.fold_in(jax.random.fold_in(rng, 6), dim), (shards_of,), jnp.float32, smallest / len(pieces), high / len(pieces))
        loudness = loudness * jnp.repeat(jnp.exp(heights), extent[dim] // shards_of).reshape((-1,) + (1,) * (len(extent) - 1 - dim))
    return loudness


def normal_values(own_key, shape, deviation, most, split=(), held_as=jnp.bfloat16):
    values = deviation * jax.random.normal(own_key, shape, jnp.float32)
    if split:
        values = values * levels(own_key, shape, split, -0.22, 0.18)
    return jnp.clip(values, -most, most).astype(held_as)


def setup_inputs(seed: int = 0) -> dict:
    key_list = jax.random.split(jax.random.key(seed), 14)
    inputs = normal_values(key_list[0], (SEQS, LENGTH, D), 1.0, 6.0, ((0, 2), (1, 16)))
    w_query = normal_values(key_list[1], (D, D), (D * HD // 4) ** -0.5, 0.0546875, ((0, 32),))
    w_key = normal_values(key_list[2], (D, D), D ** -0.5, 0.21875, ((0, 32),))
    w_value = normal_values(key_list[3], (D, D), D ** -0.5, 0.21875, ((0, 32),))
    w_output = normal_values(key_list[4], (D, D), (D // 32) ** -0.5, 1.25, ((0, 32),))
    w_gate = normal_values(key_list[5], (D, FF), D ** -0.5, 0.21875, ((0, 32),))
    w_upper = normal_values(key_list[6], (D, FF), D ** -0.5, 0.21875, ((0, 32),))
    w_down = normal_values(key_list[7], (FF, D), FF ** -0.5, 0.125, ((0, 32),))
    gain_one = jnp.clip(1.0 + 0.18 * jax.random.normal(key_list[8], (D,), jnp.float32), 0.099609375, 1.8984375).astype(jnp.bfloat16)
    gain_two = jnp.clip(1.0 + 0.18 * jax.random.normal(key_list[9], (D,), jnp.float32), 0.099609375, 1.8984375).astype(jnp.bfloat16)
    bias_table = normal_values(key_list[10], (BUCKETS * H,), 1.0, 4.0, ((0, 32),))
    buckets = place_ends(jax.random.randint(key_list[11], (2 * LENGTH - 1,), 0, BUCKETS), jax.random.fold_in(key_list[11], 1), 0, BUCKETS - 1).astype(jnp.int32)
    cotangent = normal_values(key_list[12], (SEQS, LENGTH, D), 1.0, 6.0, ((0, 2), (1, 16)))
    return {"inputs": inputs, "w_query": w_query, "w_key": w_key, "w_value": w_value, "w_output": w_output, "w_gate": w_gate, "w_upper": w_upper, "w_down": w_down, "gain_one": gain_one, "gain_two": gain_two, "bias_table": bias_table, "buckets": buckets, "cotangent": cotangent}


@jax.custom_vjp
def low(v):
    return lax.optimization_barrier(v.astype(jnp.bfloat16)).astype(jnp.float32)

@jax.custom_vjp
def low_back(v):
    return v

def low_keep(v):
    return (low(v), None)

def low_pass(kept, grad):
    return (grad,)

def back_keep(v):
    return (v, None)

def back_low(kept, grad):
    return (low(grad),)
low.defvjp(low_keep, low_pass)
low_back.defvjp(back_keep, back_low)
exactly = lax.Precision.HIGHEST

def rms_scale(values, gain_vec):
    return values * lax.rsqrt(lax.optimization_barrier(jnp.mean(values * values, axis=-1, keepdims=True)) + 1e-06) * gain_vec

def attention(queries, key_proj, value_proj, offset_bias):
    seq_length = queries.shape[0]
    block_rows = 512 if seq_length % 512 == 0 else seq_length
    query_heads = queries.reshape(seq_length, H, HD)
    key_heads = key_proj.reshape(seq_length, H, HD)
    value_heads = value_proj.reshape(seq_length, H, HD)
    positions = jnp.arange(seq_length, dtype=jnp.int32)

    def attend(first_row):
        block_queries = lax.dynamic_slice_in_dim(query_heads, first_row, block_rows, 0)
        offsets = positions[None, :] - (first_row + jnp.arange(block_rows, dtype=jnp.int32))[:, None] + seq_length - 1
        bias_block = jnp.transpose(offset_bias[offsets], (2, 0, 1))
        scores = low_back(jnp.einsum('qhd,khd->hqk', block_queries, key_heads, precision=exactly) + bias_block)
        lse_rows = jax.nn.logsumexp(scores, axis=-1, keepdims=True)
        probabilities = low(jnp.exp(scores - lse_rows))
        mixed_rows = jnp.einsum('hqk,khd->qhd', probabilities, value_heads, precision=exactly)
        return mixed_rows.reshape(block_rows, H * HD)
    starts = jnp.arange(seq_length // block_rows, dtype=jnp.int32) * block_rows
    return lax.map(jax.checkpoint(attend), starts).reshape(seq_length, H * HD)

def encoder_layer(token_rows, w_query, w_key, w_value, w_output, w_gate, w_upper, w_down, gain_one, gain_two, bias_table, buckets):
    normed = low(rms_scale(token_rows, gain_one))
    queries = low_back(low(jnp.dot(normed, w_query, precision=exactly)))
    key_proj = low_back(low(jnp.dot(normed, w_key, precision=exactly)))
    value_proj = low_back(low(jnp.dot(normed, w_value, precision=exactly)))
    offset_bias = bias_table.reshape(BUCKETS, H)[buckets]
    context = low_back(low(attention(queries, key_proj, value_proj, offset_bias)))
    residual = token_rows + low_back(jnp.dot(context, w_output, precision=exactly))
    normed_two = low(rms_scale(residual, gain_two))
    gate_pre = low_back(jnp.dot(normed_two, w_gate, precision=exactly))
    up_pre = low_back(jnp.dot(normed_two, w_upper, precision=exactly))
    hidden = low(jax.nn.gelu(gate_pre, approximate=True) * up_pre)
    return residual + low_back(jnp.dot(hidden, w_down, precision=exactly))

def reference(inputs, w_query, w_key, w_value, w_output, w_gate, w_upper, w_down, gain_one, gain_two, bias_table, buckets, cotangent):
    weights = tuple((weight.astype(jnp.float32) for weight in (w_query, w_key, w_value, w_output, w_gate, w_upper, w_down, gain_one, gain_two, bias_table)))

    def one_sequence(grad_totals, seq_pair):
        seq_rows, seq_grad = seq_pair

        def forward(seq_float, *params):
            return encoder_layer(seq_float, *params, buckets)
        result, pullback = jax.vjp(forward, seq_rows.astype(jnp.float32), *weights)
        gradients = pullback(seq_grad.astype(jnp.float32))
        grad_totals = tuple((earlier + update for earlier, update in zip(grad_totals, gradients[1:])))
        return (grad_totals, (result.astype(jnp.bfloat16), gradients[0]))
    zeros = tuple((jnp.zeros(weight.shape, jnp.float32) for weight in weights))
    totals, (outputs, input_grad) = lax.scan(one_sequence, zeros, (inputs, cotangent))
    return (outputs, input_grad, totals[0], totals[1], totals[2], totals[3], totals[4], totals[5], totals[6], totals[7], totals[8], totals[9])
```

```python
import functools

import jax
import jax.numpy as jnp
from jax import lax
from jax.experimental import pallas as pl
from jax.experimental.pallas import tpu as pltpu
from jax.sharding import Mesh
from jax.sharding import PartitionSpec as P

H = 12
BUCKETS = 32
GROUPS = 4
CORES = 2
BLOCK = 128

epsilon = 1e-06
exactly = lax.Precision.HIGHEST
bf16 = jnp.bfloat16
f32 = jnp.float32
everyone = ("dp", "a", "z", "x", "c")


def rms_scale(values, gain_vec):
    return (
        values * lax.rsqrt(jnp.mean(values * values, axis=-1, keepdims=True) + epsilon) * gain_vec
    )


def gelu_product(gate_in, up_in):
    return jax.nn.gelu(gate_in, approximate=True) * up_in


def inner_rows(first_op, second_op):
    return lax.dot_general(
        first_op, second_op, (((0,), (0,)), ((), ())), preferred_element_type=f32
    )


def outer_rows(first_op, second_op):
    return lax.dot_general(
        first_op, second_op, (((1,), (1,)), ((), ())), preferred_element_type=f32
    )


def vmem_limit(mib):
    return pltpu.CompilerParams(vmem_limit_bytes=mib * 1024 * 1024)


def project_kernel(heads, token_ref, gain_ref, weight_ref, normed_ref, query_ref, pair_ref):
    rows = token_ref[...].astype(f32)
    scale = lax.rsqrt(jnp.mean(rows * rows, axis=-1, keepdims=True) + epsilon)
    normed = (rows * scale * gain_ref[...]).astype(bf16)
    normed_ref[...] = normed
    width = query_ref.shape[2]
    mixed = jnp.dot(
        normed, weight_ref[:, : 3 * heads * width], preferred_element_type=f32
    ).astype(bf16)
    for k in range(heads):
        query_ref[k] = mixed[:, k * width : (k + 1) * width]
    for k in range(2 * heads):
        pair_ref[k] = mixed[:, (heads + k) * width : (heads + k + 1) * width]


def project(tokens, gain_row, weight, heads, width):
    rows, model = tokens.shape
    tile = 256
    return pl.pallas_call(
        functools.partial(project_kernel, heads),
        grid=(rows // tile,),
        in_specs=[
            pl.BlockSpec((tile, model), lambda i: (i, 0)),
            pl.BlockSpec((1, model), lambda i: (0, 0)),
            pl.BlockSpec(weight.shape, lambda i: (0, 0)),
        ],
        out_specs=[
            pl.BlockSpec((tile, model), lambda i: (i, 0)),
            pl.BlockSpec((heads, tile, width), lambda i: (0, i, 0)),
            pl.BlockSpec((2 * heads, tile, width), lambda i: (0, i, 0)),
        ],
        out_shape=[
            jax.ShapeDtypeStruct((rows, model), bf16),
            jax.ShapeDtypeStruct((heads, rows, width), bf16),
            jax.ShapeDtypeStruct((2 * heads, rows, width), bf16),
        ],
        compiler_params=vmem_limit(40),
        cost_estimate=pl.CostEstimate(
            flops=2 * rows * model * 3 * heads * width,
            bytes_accessed=8 * rows * model,
            transcendentals=0,
        ),
        name="project",
    )(tokens, gain_row, weight)


def skew_rows(vector_ref, table_ref, row_scratch):
    span = vector_ref.shape[-1]
    for r in range(8):
        row_scratch[r : r + 1, :] = pltpu.roll(vector_ref[0], r, 1) if r else vector_ref[0]
    eight = row_scratch[...]
    for group in range(BLOCK // 8):
        turned = pltpu.roll(eight, 8 * group, 1) if group else eight
        table_ref[8 * group : 8 * group + 8, :] = turned[:, BLOCK:span]


def interleave(scratch, own_ref, other_ref, parity):
    for k in range(own_ref.shape[1] // BLOCK):
        rows = slice(k * BLOCK, (k + 1) * BLOCK)
        first = pl.multiple_of((2 * k + parity) * BLOCK, BLOCK)
        second = pl.multiple_of((2 * k + 1 - parity) * BLOCK, BLOCK)
        scratch[pl.ds(first, BLOCK), :] = own_ref[0, rows, :]
        scratch[pl.ds(second, BLOCK), :] = other_ref[0, rows, :]


def attend_kernel(
    tile,
    chunk,
    place_ref,
    query_ref,
    key_own,
    key_other,
    value_own,
    value_other,
    vector_ref,
    context_ref,
    probs_ref,
    kept_ref,
    keys,
    values,
    table,
    scores,
    row_scratch,
):
    head, step = pl.program_id(0), pl.program_id(1)
    first_block, parity = place_ref[0], place_ref[1]
    key_count, width = keys.shape
    blocks = key_count // BLOCK

    @pl.when(step == 0)
    def prepare():
        skew_rows(vector_ref, table, row_scratch)
        interleave(keys, key_own, key_other, parity)
        interleave(values, value_own, value_other, parity)

    query = query_ref[0]
    starts = []
    for sub in range(tile // BLOCK):
        block = 2 * (first_block + step * (tile // BLOCK) + sub) + parity
        starts.append((blocks - 1 - block) * BLOCK)
    lane_max = None
    for part in range(key_count // chunk):
        product = lax.dot_general(
            query,
            keys[part * chunk : (part + 1) * chunk, :],
            (((1,), (1,)), ((), ())),
            preferred_element_type=f32,
        )
        for sub in range(tile // BLOCK):
            rows = slice(sub * BLOCK, (sub + 1) * BLOCK)
            offset = pl.multiple_of(starts[sub] + part * chunk, BLOCK)
            scores[rows, part * chunk : (part + 1) * chunk] = (
                product[rows] + table[:, pl.ds(offset, chunk)]
            )
        piece = scores[:, part * chunk : (part + 1) * chunk]
        for k in range(chunk // BLOCK):
            lanes = piece[:, k * BLOCK : (k + 1) * BLOCK]
            lane_max = lanes if lane_max is None else jnp.maximum(lane_max, lanes)
    row_max = jnp.max(lane_max, axis=-1, keepdims=True)
    lane_sum = jnp.zeros((tile, BLOCK), f32)
    mixed = jnp.zeros((tile, width), f32)
    for part in range(key_count // chunk):
        cols = slice(part * chunk, (part + 1) * chunk)
        weights = jnp.exp(scores[:, cols] - row_max)
        for k in range(chunk // BLOCK):
            lane_sum = lane_sum + weights[:, k * BLOCK : (k + 1) * BLOCK]
        low = weights.astype(bf16)
        probs_ref[0, :, cols] = low
        mixed = mixed + jnp.dot(low, values[cols, :], preferred_element_type=f32)
    inverse = 1.0 / jnp.sum(lane_sum, axis=-1, keepdims=True)
    mixed = mixed * inverse
    kept_ref[0, :, :width] = mixed
    kept_ref[0, :, width:] = jnp.broadcast_to(inverse, (tile, width))
    low = mixed.astype(bf16)
    rows = pl.ds(pl.multiple_of(step * tile, tile), tile)
    for k in range(context_ref.shape[1] // width):

        @pl.when(head == k)
        def store():
            context_ref[rows, k * width : (k + 1) * width] = low


def attend(place, query, own, other, vectors):
    heads, rows, width = query.shape
    own_rows = own.shape[1]
    key_count = 2 * own_rows
    span = vectors.shape[-1]
    tile, chunk = 256, 512
    half = lambda shift: pl.BlockSpec((1, own_rows, width), lambda h, i, s: (h + shift, 0, 0))
    return pl.pallas_call(
        functools.partial(attend_kernel, tile, chunk),
        grid_spec=pltpu.PrefetchScalarGridSpec(
            num_scalar_prefetch=1,
            grid=(heads, rows // tile),
            in_specs=[
                pl.BlockSpec((1, tile, width), lambda h, i, s: (h, i, 0)),
                half(0),
                half(0),
                half(heads),
                half(heads),
                pl.BlockSpec((1, 1, span), lambda h, i, s: (h, 0, 0)),
            ],
            out_specs=[
                pl.BlockSpec((rows, heads * width), lambda h, i, s: (0, 0)),
                pl.BlockSpec((1, tile, key_count), lambda h, i, s: (h, i, 0)),
                pl.BlockSpec((1, tile, 2 * width), lambda h, i, s: (h, i, 0)),
            ],
            scratch_shapes=[
                pltpu.VMEM((key_count, width), bf16),
                pltpu.VMEM((key_count, width), bf16),
                pltpu.VMEM((BLOCK, span - BLOCK), f32),
                pltpu.VMEM((tile, key_count), f32),
                pltpu.VMEM((8, span), f32),
            ],
        ),
        out_shape=[
            jax.ShapeDtypeStruct((rows, heads * width), bf16),
            jax.ShapeDtypeStruct((heads, rows, key_count), bf16),
            jax.ShapeDtypeStruct((heads, rows, 2 * width), f32),
        ],
        compiler_params=vmem_limit(60),
        cost_estimate=pl.CostEstimate(
            flops=16 * heads * rows * key_count * width,
            bytes_accessed=2 * heads * rows * key_count,
            transcendentals=heads * rows * key_count,
        ),
        name="attend",
    )(place, query, own, other, own, other, vectors)


def attend_back_kernel(
    tile,
    chunk,
    place_ref,
    grad_ref,
    kept_ref,
    probs_ref,
    query_ref,
    key_own,
    key_other,
    value_own,
    value_other,
    query_grad_ref,
    own_grad_ref,
    other_grad_ref,
    offset_ref,
    keys,
    values,
    diagonals,
    key_sums,
    value_sums,
    head_grad,
):
    head, step = pl.program_id(0), pl.program_id(1)
    first_block, parity = place_ref[0], place_ref[1]
    key_count, width = keys.shape
    heads = grad_ref.shape[1] // width
    blocks = key_count // BLOCK

    @pl.when(step == 0)
    def prepare():
        interleave(keys, key_own, key_other, parity)
        interleave(values, value_own, value_other, parity)
        diagonals[...] = jnp.zeros_like(diagonals)
        key_sums[...] = jnp.zeros_like(key_sums)
        value_sums[...] = jnp.zeros_like(value_sums)

    for k in range(heads):

        @pl.when(head == k)
        def load():
            head_grad[...] = grad_ref[:, k * width : (k + 1) * width]

    scaled = (head_grad[...].astype(f32) * kept_ref[0, :, width:]).astype(bf16)
    delta = jnp.sum(scaled.astype(f32) * kept_ref[0, :, :width], axis=-1, keepdims=True)
    query_turned = query_ref[0].astype(f32).T.astype(bf16)
    grad_turned = scaled.astype(f32).T.astype(bf16)
    starts = []
    for sub in range(tile // BLOCK):
        block = 2 * (first_block + step * (tile // BLOCK) + sub) + parity
        starts.append((blocks - 1 - block) * BLOCK)
    query_grad = jnp.zeros((tile, width), f32)
    for part in range(key_count // chunk):
        cols = slice(part * chunk, (part + 1) * chunk)
        prob_grad = lax.dot_general(
            scaled, values[cols, :], (((1,), (1,)), ((), ())), preferred_element_type=f32
        )
        low = probs_ref[0, :, cols]
        score_grad = low.astype(f32) * (prob_grad - delta)
        for sub in range(tile // BLOCK):
            rows = slice(sub * BLOCK, (sub + 1) * BLOCK)
            offset = pl.multiple_of(starts[sub] + part * chunk, BLOCK)
            diagonals[:, pl.ds(offset, chunk)] += score_grad[rows]
        score_low = score_grad.astype(bf16)
        query_grad = query_grad + jnp.dot(score_low, keys[cols, :], preferred_element_type=f32)
        key_sums[:, cols] += jnp.dot(query_turned, score_low, preferred_element_type=f32)
        value_sums[:, cols] += jnp.dot(grad_turned, low, preferred_element_type=f32)
    rows = pl.ds(pl.multiple_of(step * tile, tile), tile)
    for k in range(heads):

        @pl.when(head == k)
        def store():
            query_grad_ref[rows, k * width : (k + 1) * width] = query_grad.astype(bf16)

    @pl.when(step == pl.num_programs(1) - 1)
    def finish():
        span = diagonals.shape[1]
        eight = diagonals[0:8, :]
        for group in range(1, BLOCK // 8):
            eight = eight + pltpu.roll(
                diagonals[8 * group : 8 * group + 8, :], span - 8 * group, 1
            )
        total = eight[0:1, :]
        for r in range(1, 8):
            total = total + pltpu.roll(eight[r : r + 1, :], span - r, 1)
        offset_ref[0] = pltpu.roll(total, BLOCK - 1, 1)
        for k in range(heads):

            @pl.when(head == k)
            def store_pairs():
                for sums, shift in ((key_sums, 0), (value_sums, heads)):
                    lanes = slice((shift + k) * width, (shift + k + 1) * width)
                    for b in range(blocks // 2):
                        near = pl.multiple_of((2 * b + parity) * BLOCK, BLOCK)
                        far = pl.multiple_of((2 * b + 1 - parity) * BLOCK, BLOCK)
                        out = slice(b * BLOCK, (b + 1) * BLOCK)
                        own_grad_ref[out, lanes] = sums[:, pl.ds(near, BLOCK)].T
                        other_grad_ref[out, lanes] = sums[:, pl.ds(far, BLOCK)].T.astype(bf16)


def attend_back(place, grad, kept, probs, query, own, other):
    heads, rows, width = query.shape
    own_rows = own.shape[1]
    key_count = 2 * own_rows
    span = key_count * 2
    tile, chunk = 256, 512
    half = lambda shift: pl.BlockSpec((1, own_rows, width), lambda h, i, s: (h + shift, 0, 0))
    return pl.pallas_call(
        functools.partial(attend_back_kernel, tile, chunk),
        grid_spec=pltpu.PrefetchScalarGridSpec(
            num_scalar_prefetch=1,
            grid=(heads, rows // tile),
            in_specs=[
                pl.BlockSpec((tile, heads * width), lambda h, i, s: (i, 0)),
                pl.BlockSpec((1, tile, 2 * width), lambda h, i, s: (h, i, 0)),
                pl.BlockSpec((1, tile, key_count), lambda h, i, s: (h, i, 0)),
                pl.BlockSpec((1, tile, width), lambda h, i, s: (h, i, 0)),
                half(0),
                half(0),
                half(heads),
                half(heads),
            ],
            out_specs=[
                pl.BlockSpec((rows, heads * width), lambda h, i, s: (0, 0)),
                pl.BlockSpec((own_rows, 2 * heads * width), lambda h, i, s: (0, 0)),
                pl.BlockSpec((own_rows, 2 * heads * width), lambda h, i, s: (0, 0)),
                pl.BlockSpec((1, 1, span), lambda h, i, s: (h, 0, 0)),
            ],
            scratch_shapes=[
                pltpu.VMEM((key_count, width), bf16),
                pltpu.VMEM((key_count, width), bf16),
                pltpu.VMEM((BLOCK, span), f32),
                pltpu.VMEM((width, key_count), f32),
                pltpu.VMEM((width, key_count), f32),
                pltpu.VMEM((tile, width), bf16),
            ],
        ),
        out_shape=[
            jax.ShapeDtypeStruct((rows, heads * width), bf16),
            jax.ShapeDtypeStruct((own_rows, 2 * heads * width), f32),
            jax.ShapeDtypeStruct((own_rows, 2 * heads * width), bf16),
            jax.ShapeDtypeStruct((heads, 1, span), f32),
        ],
        compiler_params=vmem_limit(60),
        cost_estimate=pl.CostEstimate(
            flops=32 * heads * rows * key_count * width,
            bytes_accessed=2 * heads * rows * key_count,
            transcendentals=0,
        ),
        name="attend_back",
    )(place, grad, kept, probs, query, own, other, own, other)


def project_back_kernel(
    query_grad_ref,
    own_ref,
    received_ref,
    normed_ref,
    token_ref,
    weight_ref,
    rows_ref,
    weight_grad_ref,
    gain_ref,
    mixed,
):
    step = pl.program_id(0)
    part = query_grad_ref.shape[1]
    mixed[:, :part] = query_grad_ref[...]
    mixed[:, part:] = (own_ref[...] + received_ref[...].astype(f32)).astype(bf16)
    grads = mixed[...]
    normed_grad = lax.dot_general(
        grads,
        weight_ref[:, : 3 * part],
        (((1,), (1,)), ((), ())),
        preferred_element_type=f32,
    )
    rows_ref[...] = normed_grad.astype(bf16)
    tokens = token_ref[...].astype(f32)
    scale = lax.rsqrt(jnp.mean(tokens * tokens, axis=-1, keepdims=True) + epsilon)
    gain = jnp.sum(normed_grad * (tokens * scale), axis=0, keepdims=True)
    update = lax.dot_general(
        normed_ref[...], grads, (((0,), (0,)), ((), ())), preferred_element_type=f32
    )

    @pl.when(step == 0)
    def start():
        weight_grad_ref[...] = update
        gain_ref[...] = gain

    @pl.when(step != 0)
    def more():
        weight_grad_ref[...] += update
        gain_ref[...] += gain


def project_back(query_grad, own, received, normed, tokens, weight):
    rows, model = tokens.shape
    part = query_grad.shape[1]
    tile = 256
    by_rows = lambda size: pl.BlockSpec((tile, size), lambda i: (i, 0))
    whole = lambda shape: pl.BlockSpec(shape, lambda i: (0, 0))
    return pl.pallas_call(
        project_back_kernel,
        grid=(rows // tile,),
        in_specs=[
            by_rows(part),
            by_rows(2 * part),
            by_rows(2 * part),
            by_rows(model),
            by_rows(model),
            whole(weight.shape),
        ],
        out_specs=[by_rows(model), whole((model, 3 * part)), whole((1, model))],
        out_shape=[
            jax.ShapeDtypeStruct((rows, model), bf16),
            jax.ShapeDtypeStruct((model, 3 * part), f32),
            jax.ShapeDtypeStruct((1, model), f32),
        ],
        scratch_shapes=[pltpu.VMEM((tile, 3 * part), bf16)],
        compiler_params=vmem_limit(40),
        cost_estimate=pl.CostEstimate(
            flops=12 * rows * model * part, bytes_accessed=12 * rows * model, transcendentals=0
        ),
        name="project_back",
    )(query_grad, own, received, normed, tokens, weight)


def swap(value, axis):
    return lax.ppermute(value, axis, [(0, 1), (1, 0)])


def pick(pair, index, axis):
    return lax.dynamic_index_in_dim(pair, index, axis, keepdims=False)


def in_order(mine, theirs, index, axis):
    return jnp.where(
        index == 0, jnp.stack([mine, theirs], axis), jnp.stack([theirs, mine], axis)
    )


def halve(value, index, name, axis):
    sent = swap(pick(value, 1 - index, axis), name)
    return (pick(value, index, axis).astype(f32) + sent.astype(f32)).astype(bf16)


def body(
    inputs,
    w_query,
    w_key,
    w_value,
    w_output,
    w_gate,
    w_upper,
    w_down,
    gain_one,
    gain_two,
    bias_table,
    buckets,
    cotangent,
    sizes,
):
    along_dp, along_a = sizes
    z, x, c = lax.axis_index("z"), lax.axis_index("x"), lax.axis_index("c")
    a = lax.axis_index("a")
    seqs, local_rows, model = inputs.shape
    length = buckets.shape[0] // 2 + 1
    width = model // H
    heads = H // GROUPS
    part = heads * width
    weight_rows = w_query.shape[0]
    hidden_units = w_gate.shape[1]

    packed = jnp.concatenate(
        [w_output, w_gate, w_upper, w_down.reshape(weight_rows, hidden_units)], axis=1
    )
    everything = lax.all_gather(packed, everyone, axis=0, tiled=True)

    mine, theirs = pick(inputs, x, 0), swap(pick(inputs, 1 - x, 0), "x")
    near = in_order(mine, theirs, x, 0)
    gathered = jnp.zeros((GROUPS, *near.shape), bf16)
    gathered = lax.dynamic_update_index_in_dim(gathered, near, z, 0)
    for shift in range(1, GROUPS):
        came = lax.ppermute(near, "z", [(i, (i + shift) % GROUPS) for i in range(GROUPS)])
        gathered = lax.dynamic_update_index_in_dim(gathered, came, (z - shift) % GROUPS, 0)
    own_count = GROUPS * 2 * local_rows
    tokens_own = gathered.reshape(own_count, model)

    blocks = [
        jnp.transpose(w.reshape(weight_rows, GROUPS, part), (1, 0, 2))
        for w in (w_query, w_key, w_value)
    ]
    table_column = jnp.pad(bias_table, (0, weight_rows - bias_table.shape[0]))
    extra = jnp.stack([gain_one, gain_two, table_column], axis=1)
    extra = jnp.pad(extra, ((0, 0), (0, BLOCK - extra.shape[1])))
    extra = jnp.broadcast_to(extra[None], (GROUPS, weight_rows, BLOCK))
    columns = lax.all_to_all(jnp.concatenate([*blocks, extra], axis=2), "z", 0, 0, tiled=True)
    columns = in_order(columns, swap(columns, "x"), x, 1)
    if along_a > 1:
        columns = lax.all_gather(columns, "a", axis=0)
    else:
        columns = columns[None]
    dp = lax.axis_index("dp")
    columns = in_order(columns, swap(columns, "dp"), dp, 0)
    columns = in_order(columns, swap(columns, "c"), c, 4)
    columns = columns.reshape(model, 3 * part + BLOCK)
    gain_a = columns[:, 3 * part].astype(f32)
    gain_b = columns[:, 3 * part + 1].astype(f32)
    table = columns[:, 3 * part + 2].reshape(model // weight_rows, weight_rows)
    table = table[:, : bias_table.shape[0]].reshape(BUCKETS, H)
    one_hot = (buckets[:, None] == jnp.arange(BUCKETS, dtype=jnp.int32)[None, :]).astype(bf16)
    own_table = lax.dynamic_slice_in_dim(table, z * heads, heads, 1)
    offset_bias = lax.dot_general(
        own_table, one_hot, (((0,), (1,)), ((), ())), preferred_element_type=f32
    )
    vectors = jnp.pad(offset_bias, ((0, 0), (1, 0))).reshape(heads, 1, 2 * length)

    if along_a > 1:
        tokens_all = lax.all_gather(tokens_own, "a", axis=0, tiled=True)
    else:
        tokens_all = tokens_own
    normed, query, own = project(tokens_all, gain_a.reshape(1, model), columns, heads, width)
    if along_a > 1:
        query = lax.dynamic_slice_in_dim(query, a * own_count, own_count, 1)
        normed = lax.dynamic_slice_in_dim(normed, a * own_count, own_count, 0)
    other = swap(own, "c")
    place = jnp.stack([a * (own_count // BLOCK), c]).astype(jnp.int32)
    context_own, probs, kept = attend(place, query, own, other, vectors)
    context = lax.all_to_all(
        context_own.reshape(GROUPS * 2, local_rows, part), ("z", "x"), 0, 0, tiled=True
    )
    context = jnp.transpose(
        context.reshape(GROUPS, 2, local_rows, part), (1, 2, 0, 3)
    ).reshape(2 * local_rows, model)

    output_w = everything[:, :model]
    gate_w = everything[:, model : model + hidden_units]
    upper_w = everything[:, model + hidden_units : model + 2 * hidden_units]
    down_w = everything[:, model + 2 * hidden_units :].reshape(hidden_units, model)

    token_rows = inputs.reshape(seqs * local_rows, model).astype(f32)
    residual = token_rows + jnp.dot(context, output_w, preferred_element_type=f32)
    second_low = rms_scale(residual, gain_b).astype(bf16)
    gate_pre = jnp.dot(second_low, gate_w, preferred_element_type=f32)
    up_pre = jnp.dot(second_low, upper_w, preferred_element_type=f32)
    hidden = gelu_product(gate_pre, up_pre).astype(bf16)
    outputs = (residual + jnp.dot(hidden, down_w, preferred_element_type=f32)).astype(bf16)

    down_grad = cotangent.reshape(seqs * local_rows, model)
    hidden_grad = outer_rows(down_grad, down_w)
    unused, gelu_pull = jax.vjp(gelu_product, gate_pre, up_pre)
    gate_grad, up_grad = gelu_pull(hidden_grad)
    gate_low = gate_grad.astype(bf16)
    up_low = up_grad.astype(bf16)
    norm_grad = outer_rows(gate_low, gate_w) + outer_rows(up_low, upper_w)
    unused, norm_pull = jax.vjp(rms_scale, residual, gain_b)
    residual_part, gain_b_grad = norm_pull(norm_grad)
    residual_grad = down_grad.astype(f32) + residual_part
    attn_low = residual_grad.astype(bf16)
    context_low = outer_rows(attn_low, output_w).astype(bf16)
    sent = jnp.transpose(
        context_low.reshape(2, local_rows, GROUPS, part), (2, 0, 1, 3)
    ).reshape(GROUPS * 2, local_rows, part)
    context_grad = lax.all_to_all(sent, ("z", "x"), 0, 0, tiled=True).reshape(own_count, part)

    big_grads = jnp.concatenate(
        [
            inner_rows(context, attn_low).astype(bf16),
            inner_rows(second_low, gate_low).astype(bf16),
            inner_rows(second_low, up_low).astype(bf16),
            inner_rows(hidden, down_grad).astype(bf16).reshape(model, hidden_units),
        ],
        axis=1,
    )
    big_owned = lax.psum_scatter(big_grads, everyone, scatter_dimension=0, tiled=True)
    big_owned = big_owned.astype(f32)

    query_grad, own_grad, other_grad, offset_grad = attend_back(
        place, context_grad, kept, probs, query, own, other
    )
    if along_a > 1:
        own_grad = lax.psum_scatter(own_grad, "a", scatter_dimension=0, tiled=True)
        other_grad = lax.psum_scatter(other_grad, "a", scatter_dimension=0, tiled=True)
    received = swap(other_grad, "c")
    rows_grad, weight_grad, gain_a_grad = project_back(
        query_grad, own_grad, received, normed, tokens_own, columns
    )

    rows_grad = rows_grad.reshape(GROUPS, 2, local_rows, model)
    total = pick(rows_grad, z, 0).astype(f32)
    for shift in range(1, GROUPS):
        sent = pick(rows_grad, (z + shift) % GROUPS, 0)
        came = lax.ppermute(sent, "z", [(i, (i + shift) % GROUPS) for i in range(GROUPS)])
        total = total + came.astype(f32)
    from_pair = swap(pick(total, 1 - x, 0).astype(bf16), "x").astype(f32)
    normed_grad = in_order(pick(total, x, 0), from_pair, x, 0).reshape(seqs * local_rows, model)
    scale = lax.rsqrt(jnp.mean(token_rows * token_rows, axis=-1, keepdims=True) + epsilon)
    weighted = normed_grad * gain_a
    inner = jnp.mean(weighted * token_rows, axis=-1, keepdims=True)
    input_grad = residual_grad + scale * weighted - token_rows * (scale * scale * scale * inner)

    table_part = lax.dot_general(
        offset_grad.reshape(heads, 2 * length)[:, : 2 * length - 1],
        one_hot.astype(f32),
        (((1,), (0,)), ((), ())),
        precision=exactly,
    )
    table_grad = lax.dynamic_update_slice_in_dim(
        jnp.zeros((BUCKETS, H), f32), jnp.transpose(table_part), z * heads, 1
    )
    per_owner = bias_table.shape[0]
    table_grad = jnp.pad(
        table_grad.reshape(BUCKETS * H // per_owner, per_owner),
        ((0, 0), (0, weight_rows - per_owner)),
    )
    extra_grad = jnp.stack(
        [gain_a_grad.reshape(model), gain_b_grad, table_grad.reshape(model)], axis=1
    )
    extra_grad = jnp.pad(extra_grad.astype(bf16), ((0, 0), (0, BLOCK - extra_grad.shape[1])))
    terms = jnp.concatenate([weight_grad.astype(bf16), extra_grad], axis=1)
    terms = terms.reshape(along_dp, along_a, GROUPS, 2, CORES, weight_rows, 3 * part + BLOCK)
    terms = halve(terms, c, "c", 4)
    terms = halve(terms, x, "x", 3)
    terms = halve(terms, dp, "dp", 0)
    if along_a > 1:
        terms = lax.psum_scatter(terms, "a", scatter_dimension=0, tiled=True)
    terms = lax.all_to_all(terms[0], "z", 0, 0, tiled=True).astype(f32)
    owned = [
        jnp.transpose(terms[:, :, k * part : (k + 1) * part], (1, 0, 2)).reshape(
            weight_rows, model
        )
        for k in range(3)
    ]
    extras = jnp.sum(terms[:, :, 3 * part : 3 * part + 3], axis=0)
    return (
        outputs.reshape(seqs, local_rows, model),
        input_grad.reshape(seqs, local_rows, model),
        owned[0],
        owned[1],
        owned[2],
        big_owned[:, :model],
        big_owned[:, model : model + hidden_units],
        big_owned[:, model + hidden_units : model + 2 * hidden_units],
        big_owned[:, model + 2 * hidden_units :].reshape(w_down.shape),
        extras[:, 0],
        extras[:, 1],
        extras[:per_owner, 2],
    )


def solution(mesh):
    along_dp, along_ctx = mesh.shape["dp"], mesh.shape["ctx"]
    along_a = along_ctx // (GROUPS * 2 * CORES)
    fine = Mesh(mesh.devices.reshape(along_dp, along_a, GROUPS, 2, CORES), everyone)
    rows = P("dp", ("a", "z", "x", "c"), None)
    owned = P(everyone, None)
    vector = P(everyone)
    in_specs = (rows, *[owned] * 7, *[vector] * 3, P(), rows)
    out_specs = (rows, rows, *[owned] * 7, *[vector] * 3)
    return jax.shard_map(
        functools.partial(body, sizes=(along_dp, along_a)),
        mesh=fine,
        in_specs=in_specs,
        out_specs=out_specs,
        check_vma=False,
    )
```

```python
import functools

import jax
import jax.numpy as jnp
from jax import lax
from jax.experimental import pallas as pl
from jax.experimental.pallas import tpu as pltpu
from jax.sharding import Mesh
from jax.sharding import PartitionSpec as P

H = 12
BUCKETS = 32
GROUPS = 4
CORES = 2
BLOCK = 128

epsilon = 1e-06
exactly = lax.Precision.HIGHEST
bf16 = jnp.bfloat16
f32 = jnp.float32
everyone = ("dp", "a", "zh", "zl", "x", "c")
chips = ("dp", "zh", "zl", "x")
PANEL = 256


def rms_scale(values, gain_vec):
    return (
        values * lax.rsqrt(jnp.mean(values * values, axis=-1, keepdims=True) + epsilon) * gain_vec
    )


def vmem_limit(mib):
    return pltpu.CompilerParams(vmem_limit_bytes=mib * 1024 * 1024)


def project_kernel(heads, token_ref, gain_ref, weight_ref, normed_ref, query_ref, pair_ref):
    rows = token_ref[...].astype(f32)
    scale = lax.rsqrt(jnp.mean(rows * rows, axis=-1, keepdims=True) + epsilon)
    normed = (rows * scale * gain_ref[...]).astype(bf16)
    normed_ref[...] = normed
    width = query_ref.shape[2]
    mixed = jnp.dot(
        normed, weight_ref[:, : 3 * heads * width], preferred_element_type=f32
    ).astype(bf16)
    for k in range(heads):
        query_ref[k] = mixed[:, k * width : (k + 1) * width]
        for side in range(2):
            first = (heads * (side + 1) + k) * width
            pair_ref[k, :, side * width : (side + 1) * width] = mixed[:, first : first + width]


def project(tokens, gain_row, weight, heads, width):
    rows, model = tokens.shape
    tile = 256
    return pl.pallas_call(
        functools.partial(project_kernel, heads),
        grid=(rows // tile,),
        in_specs=[
            pl.BlockSpec((tile, model), lambda i: (i, 0)),
            pl.BlockSpec((1, model), lambda i: (0, 0)),
            pl.BlockSpec(weight.shape, lambda i: (0, 0)),
        ],
        out_specs=[
            pl.BlockSpec((tile, model), lambda i: (i, 0)),
            pl.BlockSpec((heads, tile, width), lambda i: (0, i, 0)),
            pl.BlockSpec((heads, tile, 2 * width), lambda i: (0, i, 0)),
        ],
        out_shape=[
            jax.ShapeDtypeStruct((rows, model), bf16),
            jax.ShapeDtypeStruct((heads, rows, width), bf16),
            jax.ShapeDtypeStruct((heads, rows, 2 * width), bf16),
        ],
        compiler_params=vmem_limit(12),
        cost_estimate=pl.CostEstimate(
            flops=2 * rows * model * 3 * heads * width,
            bytes_accessed=8 * rows * model,
            transcendentals=0,
        ),
        name="project",
    )(tokens, gain_row, weight)


def skew_kernel(vector_ref, table_ref, row_scratch):
    span = vector_ref.shape[-1]
    for r in range(8):
        row_scratch[r : r + 1, :] = pltpu.roll(vector_ref[0], r, 1) if r else vector_ref[0]
    eight = row_scratch[...]
    rows = []
    for group in range(BLOCK // 8):
        turned = pltpu.roll(eight, 8 * group, 1) if group else eight
        rows.append(turned[:, BLOCK:span])
    for pair in range(BLOCK // 16):
        both = jnp.concatenate(rows[2 * pair : 2 * pair + 2], axis=0)
        table_ref[0, 16 * pair : 16 * pair + 16, :] = both.astype(bf16)


def skew(vectors):
    heads, unused, span = vectors.shape
    return pl.pallas_call(
        skew_kernel,
        grid=(heads,),
        in_specs=[pl.BlockSpec((1, 1, span), lambda h: (h, 0, 0))],
        out_specs=pl.BlockSpec((1, BLOCK, span - BLOCK), lambda h: (h, 0, 0)),
        out_shape=jax.ShapeDtypeStruct((heads, BLOCK, span - BLOCK), bf16),
        scratch_shapes=[pltpu.VMEM((8, span), f32)],
        compiler_params=vmem_limit(10),
        cost_estimate=pl.CostEstimate(
            flops=0, bytes_accessed=2 * heads * BLOCK * span, transcendentals=0
        ),
        name="skew",
    )(vectors)


def interleave(keys, values, own_ref, other_ref, parity, fill):
    width = keys.shape[1]
    for k in range(own_ref.shape[1] // BLOCK):
        rows = slice(k * BLOCK, (k + 1) * BLOCK)
        for source, spot in ((own_ref, parity), (other_ref, 1 - parity)):
            into = pl.ds(pl.multiple_of((2 * k + spot) * BLOCK, BLOCK), BLOCK)
            keys[into, :] = source[0, rows, :width]
            values[into, :width] = source[0, rows, width:]
            if fill:
                values[into, width:] = jnp.ones((BLOCK, width), bf16)


def table_starts(tile, step, first_block, parity, blocks):
    starts = []
    for sub in range(tile // BLOCK):
        block = 2 * (first_block + step * (tile // BLOCK) + sub) + parity
        starts.append((blocks - 1 - block) * BLOCK)
    return starts


def attend_kernel(
    tile,
    chunk,
    place_ref,
    query_ref,
    pair_own,
    pair_other,
    table,
    context_ref,
    probs_ref,
    kept_ref,
    inverse_ref,
    keys,
    values,
    scores,
):
    head, step = pl.program_id(0), pl.program_id(1)
    first_block, parity = place_ref[0], place_ref[1]
    key_count, width = keys.shape
    blocks = key_count // BLOCK
    subs = tile // BLOCK
    table = table.at[0]

    @pl.when(step == 0)
    def prepare():
        interleave(keys, values, pair_own, pair_other, parity, True)

    query = query_ref[0]
    starts = table_starts(tile, step, first_block, parity, blocks)
    lane_max = None
    for part in range(key_count // chunk):
        cols = slice(part * chunk, (part + 1) * chunk)
        product = lax.dot_general(
            query, keys[cols, :], (((1,), (1,)), ((), ())), preferred_element_type=f32
        )
        pieces = []
        for sub in range(subs):
            rows = slice(sub * BLOCK, (sub + 1) * BLOCK)
            offset = pl.multiple_of(starts[sub] + part * chunk, BLOCK)
            piece = product[rows] + table[:, pl.ds(offset, chunk)].astype(f32)
            scores[rows, cols] = piece
            for k in range(chunk // BLOCK):
                lanes = piece[:, k * BLOCK : (k + 1) * BLOCK]
                top = lanes if k == 0 else jnp.maximum(top, lanes)
            pieces.append(top)
        pieces = jnp.concatenate(pieces, axis=0)
        lane_max = pieces if lane_max is None else jnp.maximum(lane_max, pieces)
    row_max = jnp.max(lane_max, axis=-1, keepdims=True)
    total = jnp.zeros((tile, 2 * width), f32)
    for part in range(key_count // chunk):
        cols = slice(part * chunk, (part + 1) * chunk)
        low = jnp.exp(scores[:, cols] - row_max).astype(bf16)
        probs_ref[0, :, cols] = low
        total = total + jnp.dot(low, values[cols, :], preferred_element_type=f32)
    inverse = 1.0 / total[:, width:]
    value = total[:, :width] * inverse
    kept_ref[0, :, :width] = value
    kept_ref[0, :, width:] = inverse
    turned = value.T.astype(bf16)
    inverse_turned = inverse.T
    for sub in range(subs):
        lanes = slice(sub * BLOCK, (sub + 1) * BLOCK)
        rows = pl.ds(pl.multiple_of(head * width, width), width)
        context_ref[step * subs + sub, rows, :] = turned[:, lanes]
        inverse_ref[0, sub] = inverse_turned[0:1, lanes]


def attend(place, query, own, other, table):
    heads, rows, width = query.shape
    own_rows = own.shape[1]
    key_count = 2 * own_rows
    tile, chunk = 256, 512
    pairs = pl.BlockSpec((1, own_rows, 2 * width), lambda h, i, s: (h, 0, 0))
    return pl.pallas_call(
        functools.partial(attend_kernel, tile, chunk),
        grid_spec=pltpu.PrefetchScalarGridSpec(
            num_scalar_prefetch=1,
            grid=(heads, rows // tile),
            in_specs=[
                pl.BlockSpec((1, tile, width), lambda h, i, s: (h, i, 0)),
                pairs,
                pairs,
                pl.BlockSpec((1, *table.shape[1:]), lambda h, i, s: (h, 0, 0)),
            ],
            out_specs=[
                pl.BlockSpec((rows // BLOCK, heads * width, BLOCK), lambda h, i, s: (0, 0, 0)),
                pl.BlockSpec((1, tile, key_count), lambda h, i, s: (h, i, 0)),
                pl.BlockSpec((1, tile, 2 * width), lambda h, i, s: (h, i, 0)),
                pl.BlockSpec((1, tile // BLOCK, 1, BLOCK), lambda h, i, s: (h, i, 0, 0)),
            ],
            scratch_shapes=[
                pltpu.VMEM((key_count, width), bf16),
                pltpu.VMEM((key_count, 2 * width), bf16),
                pltpu.VMEM((tile, key_count), f32),
            ],
        ),
        out_shape=[
            jax.ShapeDtypeStruct((rows // BLOCK, heads * width, BLOCK), bf16),
            jax.ShapeDtypeStruct((heads, rows, key_count), bf16),
            jax.ShapeDtypeStruct((heads, rows, 2 * width), f32),
            jax.ShapeDtypeStruct((heads, rows // BLOCK, 1, BLOCK), f32),
        ],
        compiler_params=vmem_limit(54),
        cost_estimate=pl.CostEstimate(
            flops=16 * heads * rows * key_count * width,
            bytes_accessed=2 * heads * rows * key_count,
            transcendentals=heads * rows * key_count,
        ),
        name="attend",
    )(place, query, own, other, table)


def attend_back_kernel(
    tile,
    chunk,
    place_ref,
    grad_ref,
    kept_ref,
    inverse_ref,
    probs_ref,
    query_ref,
    pair_own,
    pair_other,
    hot_ref,
    query_grad_ref,
    own_grad_ref,
    other_grad_ref,
    offset_ref,
    keys,
    values,
    diagonals,
    key_sums,
    value_sums,
):
    step = pl.program_id(1)
    first_block, parity = place_ref[0], place_ref[1]
    key_count, width = keys.shape
    blocks = key_count // BLOCK
    subs = tile // BLOCK

    @pl.when(step == 0)
    def prepare():
        interleave(keys, values, pair_own, pair_other, parity, False)
        diagonals[...] = jnp.zeros_like(diagonals)
        key_sums[...] = jnp.zeros_like(key_sums)
        value_sums[...] = jnp.zeros_like(value_sums)

    turned = jnp.concatenate(
        [grad_ref[sub].astype(f32) * inverse_ref[0, sub] for sub in range(subs)], axis=1
    )
    grad_turned = turned.astype(bf16)
    scaled = grad_turned.astype(f32).T
    delta = jnp.sum(scaled * kept_ref[0, :, :width], axis=-1, keepdims=True)
    scaled = scaled.astype(bf16)
    query_turned = query_ref[0].astype(f32).T.astype(bf16)
    starts = table_starts(tile, step, first_block, parity, blocks)
    query_grad = jnp.zeros((tile, width), f32)
    for part in range(key_count // chunk):
        cols = slice(part * chunk, (part + 1) * chunk)
        prob_grad = lax.dot_general(
            scaled, values[cols, :], (((1,), (1,)), ((), ())), preferred_element_type=f32
        )
        low = probs_ref[0, :, cols]
        score_grad = low.astype(f32) * (prob_grad - delta)
        for sub in range(subs):
            rows = slice(sub * BLOCK, (sub + 1) * BLOCK)
            offset = pl.multiple_of(starts[sub] + part * chunk, BLOCK)
            diagonals[:, pl.ds(offset, chunk)] += score_grad[rows]
        score_low = score_grad.astype(bf16)
        query_grad = query_grad + jnp.dot(score_low, keys[cols, :], preferred_element_type=f32)
        key_sums[:, cols] += jnp.dot(query_turned, score_low, preferred_element_type=f32)
        value_sums[:, cols] += jnp.dot(grad_turned, low, preferred_element_type=f32)
    query_grad_ref[0] = query_grad.astype(bf16)

    @pl.when(step == pl.num_programs(1) - 1)
    def finish():
        span = diagonals.shape[1]
        eight = diagonals[0:8, :]
        for group in range(1, BLOCK // 8):
            eight = eight + pltpu.roll(
                diagonals[8 * group : 8 * group + 8, :], span - 8 * group, 1
            )
        total = eight[0:1, :]
        for r in range(1, 8):
            total = total + pltpu.roll(eight[r : r + 1, :], span - r, 1)
        total = pltpu.roll(total, BLOCK - 1, 1)
        bucket_sums = None
        for unused in range(3):
            low = total.astype(bf16)
            total = total - low.astype(f32)
            more = jnp.dot(low, hot_ref[...], preferred_element_type=f32)
            bucket_sums = more if bucket_sums is None else bucket_sums + more
        offset_ref[0] = bucket_sums
        for sums, rows in ((key_sums, slice(0, width)), (value_sums, slice(width, 2 * width))):
            for b in range(blocks // 2):
                near = pl.multiple_of((2 * b + parity) * BLOCK, BLOCK)
                far = pl.multiple_of((2 * b + 1 - parity) * BLOCK, BLOCK)
                lanes = slice(b * BLOCK, (b + 1) * BLOCK)
                own_grad_ref[0, rows, lanes] = sums[:, pl.ds(near, BLOCK)]
                other_grad_ref[0, rows, lanes] = sums[:, pl.ds(far, BLOCK)].astype(bf16)


def attend_back(place, grad, kept, inverse, probs, query, own, other, hot, first, count):
    unused, rows, width = query.shape
    own_rows = own.shape[1]
    key_count = 2 * own_rows
    span = key_count * 2
    tile, chunk = 512, 512
    pairs = pl.BlockSpec((1, own_rows, 2 * width), lambda h, i, s: (h + first, 0, 0))
    return pl.pallas_call(
        functools.partial(attend_back_kernel, tile, chunk),
        grid_spec=pltpu.PrefetchScalarGridSpec(
            num_scalar_prefetch=1,
            grid=(count, rows // tile),
            in_specs=[
                pl.BlockSpec(
                    (tile // BLOCK, width, BLOCK), lambda h, i, s: (i, h + first, 0)
                ),
                pl.BlockSpec((1, tile, 2 * width), lambda h, i, s: (h + first, i, 0)),
                pl.BlockSpec((1, tile // BLOCK, 1, BLOCK), lambda h, i, s: (h + first, i, 0, 0)),
                pl.BlockSpec((1, tile, key_count), lambda h, i, s: (h + first, i, 0)),
                pl.BlockSpec((1, tile, width), lambda h, i, s: (h + first, i, 0)),
                pairs,
                pairs,
                pl.BlockSpec(hot.shape, lambda h, i, s: (0, 0)),
            ],
            out_specs=[
                pl.BlockSpec((1, tile, width), lambda h, i, s: (h, i, 0)),
                pl.BlockSpec((1, 2 * width, own_rows), lambda h, i, s: (h, 0, 0)),
                pl.BlockSpec((1, 2 * width, own_rows), lambda h, i, s: (h, 0, 0)),
                pl.BlockSpec((1, 1, hot.shape[1]), lambda h, i, s: (h, 0, 0)),
            ],
            scratch_shapes=[
                pltpu.VMEM((key_count, width), bf16),
                pltpu.VMEM((key_count, width), bf16),
                pltpu.VMEM((BLOCK, span), f32),
                pltpu.VMEM((width, key_count), f32),
                pltpu.VMEM((width, key_count), f32),
            ],
        ),
        out_shape=[
            jax.ShapeDtypeStruct((count, rows, width), bf16),
            jax.ShapeDtypeStruct((count, 2 * width, own_rows), f32),
            jax.ShapeDtypeStruct((count, 2 * width, own_rows), bf16),
            jax.ShapeDtypeStruct((count, 1, hot.shape[1]), f32),
        ],
        compiler_params=vmem_limit(54),
        cost_estimate=pl.CostEstimate(
            flops=32 * count * rows * key_count * width,
            bytes_accessed=2 * count * rows * key_count,
            transcendentals=0,
        ),
        name="attend_back",
    )(place, grad, kept, inverse, probs, query, own, other, hot)


def project_back_kernel(splits, place_ref, normed_ref, token_ref, weight_ref, *refs):
    extra_ref, given = refs[0], refs[1:-9]
    rows_refs, kept_ref, sent_ref, turned, sums, gains = (*[refs[-9:-5]], *refs[-5:])
    step = pl.program_id(0)
    query_grads = given[: len(splits)]
    owns = given[len(splits) : 2 * len(splits)]
    came = given[2 * len(splits) :]
    heads = sum(splits)
    width = query_grads[0].shape[2]
    part = heads * width
    head = 0
    for k, count in enumerate(splits):
        for h in range(count):
            turned[head * width : (head + 1) * width, :] = (
                query_grads[k][h].astype(f32).T.astype(bf16)
            )
            both = (owns[k][h] + came[k][h].astype(f32)).astype(bf16)
            for side in range(2):
                at = part * (side + 1) + head * width
                turned[at : at + width, :] = both[side * width : (side + 1) * width]
            head += 1
    grads = turned[...]
    normed_grad = lax.dot_general(
        grads,
        weight_ref[:, : 3 * part],
        (((0,), (1,)), ((), ())),
        preferred_element_type=f32,
    )
    low = normed_grad.astype(bf16)
    half, model = low.shape[0] // 2, low.shape[1]
    for k in range(2):

        @pl.when(place_ref[0] == k)
        def store():
            for share in range(2):
                lanes = slice(share * model // 2, (share + 1) * model // 2)
                rows_refs[share][0] = low[k * half : (k + 1) * half, lanes]
                rows_refs[2 + share][0] = low[(1 - k) * half : (2 - k) * half, lanes]

    tokens = token_ref[...].astype(f32)
    scale = lax.rsqrt(jnp.mean(tokens * tokens, axis=-1, keepdims=True) + epsilon)
    gain = jnp.sum(normed_grad * (tokens * scale), axis=0, keepdims=True)
    update = jnp.dot(grads, normed_ref[...], preferred_element_type=f32)

    @pl.when(step == 0)
    def start():
        sums[...] = update
        gains[...] = extra_ref[...]

    @pl.when(step != 0)
    def more():
        sums[...] += update

    gains[0:1, :] += gain

    @pl.when(step == pl.num_programs(0) - 1)
    def finish():
        update = sums[...].T
        extras = jnp.concatenate(
            [gains[...], jnp.zeros((BLOCK - gains.shape[0], model), f32)], axis=0
        ).T
        owners, rows, columns = kept_ref.shape
        for k in range(2):

            @pl.when(place_ref[1] == k)
            def pack():
                for owner in range(owners):
                    for ref, core in ((kept_ref, k), (sent_ref, 1 - k)):
                        at = slice((2 * owner + core) * rows, (2 * owner + core + 1) * rows)
                        ref[owner, :, : 3 * part] = update[at].astype(bf16)
                        ref[owner, :, 3 * part :] = extras[at].astype(bf16)


def project_back(place, query_grads, owns, came, normed, tokens, weight, extra, weight_rows):
    rows, model = tokens.shape
    splits = tuple(value.shape[0] for value in query_grads)
    width = query_grads[0].shape[2]
    part = sum(splits) * width
    tile = 2 * BLOCK
    steps = rows // tile
    by_rows = pl.BlockSpec((tile, model), lambda i, s: (i, 0))
    whole = lambda shape: pl.BlockSpec(shape, lambda i, s: (0, 0))
    pairs = [pl.BlockSpec((count, 2 * width, tile), lambda i, s: (0, 0, i)) for count in splits]
    share = (1, BLOCK, model // 2)
    packed = (model // (2 * weight_rows), weight_rows, 3 * part + BLOCK)
    return pl.pallas_call(
        functools.partial(project_back_kernel, splits),
        grid_spec=pltpu.PrefetchScalarGridSpec(
            num_scalar_prefetch=1,
            grid=(steps,),
            in_specs=[by_rows, by_rows, whole(weight.shape), whole(extra.shape)]
            + [pl.BlockSpec((count, tile, width), lambda i, s: (0, i, 0)) for count in splits]
            + pairs
            + pairs,
            out_specs=[pl.BlockSpec(share, lambda i, s: (i, 0, 0))] * 4
            + [pl.BlockSpec(packed, lambda i, s: (0, 0, 0))] * 2,
            scratch_shapes=[
                pltpu.VMEM((3 * part, tile), bf16),
                pltpu.VMEM((3 * part, model), f32),
                pltpu.VMEM(extra.shape, f32),
            ],
        ),
        out_shape=[jax.ShapeDtypeStruct((steps, *share[1:]), bf16)] * 4
        + [jax.ShapeDtypeStruct(packed, bf16)] * 2,
        compiler_params=vmem_limit(60),
        cost_estimate=pl.CostEstimate(
            flops=12 * rows * model * part, bytes_accessed=12 * rows * model, transcendentals=0
        ),
        name="project_back",
    )(place, normed, tokens, weight, extra, *query_grads, *owns, *came)


def rows_kernel(place_ref, token_ref, residual_ref, gain_ref, *refs):
    terms, grad_ref = refs[:-1], refs[-1]
    per_share = len(terms) // 2
    seqs, local_rows, model = token_ref.shape
    for seq in range(seqs):
        shares = []
        for share in range(2):
            total = jnp.zeros((local_rows, model // 2), f32)
            for shift in range(per_share):
                term = terms[share * per_share + shift][...].astype(f32)
                total = total + jnp.where(place_ref[shift] == seq, term, 0.0)
            shares.append(total)
        weighted = jnp.concatenate(shares, axis=1) * gain_ref[...]
        tokens = token_ref[seq].astype(f32)
        scale = lax.rsqrt(jnp.mean(tokens * tokens, axis=-1, keepdims=True) + epsilon)
        inner = jnp.mean(weighted * tokens, axis=-1, keepdims=True)
        rows = slice(seq * local_rows, (seq + 1) * local_rows)
        grad_ref[seq] = (
            residual_ref[rows] + scale * weighted - tokens * (scale * scale * scale * inner)
        )


def rows_stage(place, tokens, residual_grad, gain_row, terms):
    whole = lambda array: pl.BlockSpec(array.shape, lambda i, s: (0,) * array.ndim)
    given = (tokens, residual_grad, gain_row, *terms)
    return pl.pallas_call(
        rows_kernel,
        grid_spec=pltpu.PrefetchScalarGridSpec(
            num_scalar_prefetch=1,
            grid=(1,),
            in_specs=[whole(array) for array in given],
            out_specs=whole(tokens),
        ),
        out_shape=jax.ShapeDtypeStruct(tokens.shape, f32),
        compiler_params=vmem_limit(16),
        cost_estimate=pl.CostEstimate(
            flops=20 * tokens.size, bytes_accessed=16 * tokens.size, transcendentals=0
        ),
        name="rows_stage",
    )(place, *given)


def output_kernel(context_ref, token_ref, gain_ref, *refs):
    weights, (residual_ref, normed_ref) = refs[:-2], refs[-2:]
    seqs, local_rows, model = token_ref.shape
    groups = context_ref.shape[0] // seqs
    part = context_ref.shape[1]
    for seq in range(seqs):
        rows = slice(seq * local_rows, (seq + 1) * local_rows)
        for p, weight_ref in enumerate(weights):
            lanes = slice(p * PANEL, (p + 1) * PANEL)
            weight = weight_ref[...].reshape(model, PANEL)
            total = token_ref[seq, :, lanes].astype(f32)
            for group in range(groups):
                total = total + lax.dot_general(
                    context_ref[seq * groups + group],
                    weight[group * part : (group + 1) * part],
                    (((0,), (0,)), ((), ())),
                    preferred_element_type=f32,
                )
            residual_ref[rows, lanes] = total
    normed_ref[...] = rms_scale(residual_ref[...], gain_ref[...]).astype(bf16)


def output_stage(context, tokens, gain_row, everything, shape):
    seqs, local_rows, model = tokens.shape
    whole = lambda array: pl.BlockSpec(array.shape, lambda i: (0,) * array.ndim)
    return pl.pallas_call(
        output_kernel,
        grid=(1,),
        in_specs=[whole(context), whole(tokens), whole(gain_row)] + shape.output_specs(),
        out_specs=[pl.BlockSpec((seqs * local_rows, model), lambda i: (0, 0))] * 2,
        out_shape=[
            jax.ShapeDtypeStruct((seqs * local_rows, model), f32),
            jax.ShapeDtypeStruct((seqs * local_rows, model), bf16),
        ],
        compiler_params=vmem_limit(60),
        cost_estimate=pl.CostEstimate(
            flops=2 * seqs * local_rows * model * model,
            bytes_accessed=2 * model * model,
            transcendentals=0,
        ),
        name="output_stage",
    )(context, tokens, gain_row, *[everything] * len(shape.output_specs()))


def hidden_kernel(
    shape, place_ref, normed_own, normed_other, down_own, down_other, gate_w, upper_w, *refs
):
    panels = shape.model // PANEL
    down_w = refs[:panels]
    out_own, out_other, norm_own, norm_other = refs[panels : panels + 4]
    grad_refs, (normed, downs, outs, norms) = refs[panels + 4 : -4], refs[-4:]
    step = pl.program_id(0)
    x, dp = place_ref[0], place_ref[1]
    half = normed_own.shape[0]

    @pl.when(step == 0)
    def gather():
        normed[:half] = normed_own[...]
        normed[half:] = normed_other[...]
        downs[:half] = down_own[...]
        downs[half:] = down_other[...]

    rows, grad = normed[...], downs[...]
    gate = gate_w[...].reshape(shape.model, PANEL)
    upper = upper_w[...].reshape(shape.model, PANEL)
    gate_pre = jnp.dot(rows, gate, preferred_element_type=f32)
    up_pre = jnp.dot(rows, upper, preferred_element_type=f32)
    hidden_grad = None
    for p in range(panels):
        product = lax.dot_general(
            grad[:, p * PANEL : (p + 1) * PANEL],
            down_w[p][...].reshape(PANEL, PANEL),
            (((1,), (1,)), ((), ())),
            preferred_element_type=f32,
        )
        hidden_grad = product if hidden_grad is None else hidden_grad + product
    slope = 0.7978845608028654
    square = gate_pre * gate_pre
    bend = jnp.tanh(slope * gate_pre * (1.0 + 0.044715 * square))
    share = 0.5 * (1.0 + bend)
    curved = gate_pre * share
    hidden = (curved * up_pre).astype(bf16)
    steep = share + 0.5 * gate_pre * (1.0 - bend * bend) * (
        slope * (1.0 + 3.0 * 0.044715 * square)
    )
    gate_low = (hidden_grad * up_pre * steep).astype(bf16)
    up_low = (hidden_grad * curved).astype(bf16)
    across = (((1,), (1,)), ((), ()))
    norm_part = lax.dot_general(gate_low, gate, across, preferred_element_type=f32)
    norm_part += lax.dot_general(up_low, upper, across, preferred_element_type=f32)

    @pl.when(step == 0)
    def first():
        norms[...] = norm_part

    @pl.when(step != 0)
    def later():
        norms[...] += norm_part

    along = (((0,), (0,)), ((), ()))
    for p in range(panels):
        lanes = slice(p * PANEL, (p + 1) * PANEL)
        product = jnp.dot(
            hidden, down_w[p][...].reshape(PANEL, PANEL), preferred_element_type=f32
        )

        @pl.when(step == 0)
        def first_out():
            outs[:, lanes] = product

        @pl.when(step != 0)
        def later_out():
            outs[:, lanes] += product

        shape.store_down(
            grad_refs,
            step,
            p,
            lax.dot_general(hidden, grad[:, lanes], along, preferred_element_type=f32),
            x,
            dp,
        )
    for side, low in enumerate((gate_low, up_low)):
        shape.store_side(
            grad_refs,
            step,
            side,
            lax.dot_general(rows, low, along, preferred_element_type=f32),
            x,
            dp,
        )

    @pl.when(step == shape.steps - 1)
    def finish():
        out_own[...] = outs[:half]
        out_other[...] = outs[half:].astype(bf16)
        norm_own[...] = norms[:half]
        norm_other[...] = norms[half:].astype(bf16)


class PackedWeights:
    def __init__(self, model, hidden_half, pieces):
        self.model, self.pieces = model, pieces
        self.side = model // pieces
        self.deep = hidden_half // pieces
        self.steps = hidden_half // PANEL
        self.panels = model // PANEL
        self.side_rows = 2 * self.steps * self.side
        self.grad_rows = self.side_rows + self.panels * self.deep

    def side_spec(self, shift):
        return pl.BlockSpec((self.pieces, self.side, PANEL), lambda j: (0, j + shift, 0))

    def down_specs(self):
        if self.pieces == 1:
            first = self.side_rows // PANEL
            each = self.deep // PANEL
            return [
                pl.BlockSpec((1, PANEL, PANEL), lambda j, p=p: (0, first + p * each + j, 0))
                for p in range(self.panels)
            ]
        first = self.side_rows // self.deep
        some = self.pieces // self.steps
        return [
            pl.BlockSpec((some, self.deep, PANEL), lambda j, p=p: (j, first + p, 0))
            for p in range(self.panels)
        ]

    def output_specs(self):
        first = self.grad_rows // self.side
        return [
            pl.BlockSpec((self.pieces, self.side, PANEL), lambda j, p=p: (0, first + p, 0))
            for p in range(self.panels)
        ]

    def grad_shapes(self):
        if self.pieces == 1:
            return [(1, self.grad_rows, PANEL)]
        side = self.steps * self.side
        first = (self.pieces // 2, side + self.deep, PANEL)
        second = (self.pieces // 2, side + (self.panels - 1) * self.deep, PANEL)
        return [first, first, second, second]

    def store_side(self, refs, step, side, value, x, dp):
        low = value.astype(bf16).reshape(self.pieces, self.side, PANEL)
        if self.pieces == 1:
            start = pl.multiple_of((step + side * self.steps) * self.side, 16)
            refs[0][:, pl.ds(start, self.side), :] = low
            return
        rows = pl.ds(pl.multiple_of(step * self.side, 16), self.side)
        half = self.pieces // 2
        if side:
            for k in range(2):

                @pl.when(dp == k)
                def store_upper():
                    refs[2][:, rows, :] = low[k * half : (k + 1) * half]
                    refs[3][:, rows, :] = low[(1 - k) * half : (2 - k) * half]
        else:
            pairs = low.reshape(half, 2, self.side, PANEL)
            for k in range(2):

                @pl.when(x == k)
                def store_gate():
                    refs[0][:, rows, :] = pairs[:, k]
                    refs[1][:, rows, :] = pairs[:, 1 - k]

    def store_down(self, refs, step, p, value, x, dp):
        low = value.astype(bf16)
        if self.pieces == 1:
            start = pl.multiple_of(self.side_rows + p * self.deep + step * PANEL, PANEL)
            refs[0][0, pl.ds(start, PANEL), :] = low
            return
        some = self.pieces // self.steps
        first = self.steps * self.side
        if p == 0:
            pairs = low.reshape(some // 2, 2, self.deep, PANEL)
            spots = pl.ds(step * (some // 2), some // 2)
            for k in range(2):

                @pl.when(x == k)
                def store_first():
                    refs[0][spots, first : first + self.deep, :] = pairs[:, k]
                    refs[1][spots, first : first + self.deep, :] = pairs[:, 1 - k]
        else:
            pieces = low.reshape(some, self.deep, PANEL)
            per_half = self.steps // 2
            spots = pl.ds((step % per_half) * some, some)
            first += (p - 1) * self.deep
            for slot, mine in ((2, step // per_half == dp), (3, step // per_half != dp)):

                @pl.when(mine)
                def store_other():
                    refs[slot][spots, first : first + self.deep, :] = pieces


def hidden_stage(place, normed, normed_other, down, down_other, everything, shape):
    half, model = normed.shape
    whole = pl.BlockSpec((half, model), lambda j, s: (0, 0))
    with_place = lambda spec: pl.BlockSpec(
        spec.block_shape, lambda j, s, spec=spec: spec.index_map(j)
    )
    grads = shape.grad_shapes()
    weights = [shape.side_spec(0), shape.side_spec(shape.steps)] + shape.down_specs()
    return pl.pallas_call(
        functools.partial(hidden_kernel, shape),
        grid_spec=pltpu.PrefetchScalarGridSpec(
            num_scalar_prefetch=1,
            grid=(shape.steps,),
            in_specs=[whole] * 4 + [with_place(spec) for spec in weights],
            out_specs=[whole] * 4 + [pl.BlockSpec(size, lambda j, s: (0, 0, 0)) for size in grads],
            scratch_shapes=[
                pltpu.VMEM((2 * half, model), bf16),
                pltpu.VMEM((2 * half, model), bf16),
                pltpu.VMEM((2 * half, model), f32),
                pltpu.VMEM((2 * half, model), f32),
            ],
        ),
        out_shape=[
            jax.ShapeDtypeStruct((half, model), f32),
            jax.ShapeDtypeStruct((half, model), bf16),
            jax.ShapeDtypeStruct((half, model), f32),
            jax.ShapeDtypeStruct((half, model), bf16),
        ]
        + [jax.ShapeDtypeStruct(size, bf16) for size in grads],
        compiler_params=vmem_limit(60),
        cost_estimate=pl.CostEstimate(
            flops=18 * 2 * half * model * shape.steps * PANEL,
            bytes_accessed=12 * model * shape.steps * PANEL,
            transcendentals=0,
        ),
        name="hidden_stage",
    )(place, normed, normed_other, down, down_other, *[everything] * (2 + shape.panels))


def output_back_kernel(norm_own, norm_other, residual_ref, down_ref, gain_ref, context_ref, *refs):
    weights = refs[:-4]
    rows_ref, gain_grad_ref, context_grad_ref, weight_grad_ref = refs[-4:]
    residual, gain = residual_ref[...], gain_ref[...]
    norm_grad = norm_own[...] + norm_other[...].astype(f32)
    scale = lax.rsqrt(jnp.mean(residual * residual, axis=-1, keepdims=True) + epsilon)
    gain_grad_ref[...] = jnp.sum(norm_grad * (residual * scale), axis=0, keepdims=True)
    weighted = norm_grad * gain
    inner = jnp.mean(weighted * residual, axis=-1, keepdims=True)
    rows_grad = (
        down_ref[...].astype(f32)
        + scale * weighted
        - residual * (scale * scale * scale * inner)
    )
    rows_ref[...] = rows_grad
    low = rows_grad.astype(bf16)
    blocks, part, local_rows = context_ref.shape
    seqs = rows_grad.shape[0] // local_rows
    groups = blocks // seqs
    model = residual.shape[1]
    for group in range(groups):
        columns = slice(group * part, (group + 1) * part)
        product = None
        for p, weight_ref in enumerate(weights):
            more = lax.dot_general(
                weight_ref[...].reshape(model, PANEL)[columns],
                low[:, p * PANEL : (p + 1) * PANEL],
                (((1,), (1,)), ((), ())),
                preferred_element_type=f32,
            )
            product = more if product is None else product + more
        turned = product.astype(bf16)
        total = None
        for seq in range(seqs):
            rows = slice(seq * local_rows, (seq + 1) * local_rows)
            context_grad_ref[seq * groups + group] = turned[:, rows]
            more = jnp.dot(
                context_ref[seq * groups + group], low[rows], preferred_element_type=f32
            )
            total = more if total is None else total + more
        weight_grad_ref[columns, :] = total.astype(bf16)


def output_back(norm_own, norm_other, residual, down, gain_row, context, everything, shape):
    rows, model = residual.shape
    whole = lambda array: pl.BlockSpec(array.shape, lambda i: (0,) * array.ndim)
    given = (norm_own, norm_other, residual, down, gain_row, context)
    out_shape = [
        jax.ShapeDtypeStruct((rows, model), f32),
        jax.ShapeDtypeStruct((1, model), f32),
        jax.ShapeDtypeStruct(context.shape, bf16),
        jax.ShapeDtypeStruct((model, model), bf16),
    ]
    return pl.pallas_call(
        output_back_kernel,
        grid=(1,),
        in_specs=[whole(array) for array in given] + shape.output_specs(),
        out_specs=[whole(array) for array in out_shape],
        out_shape=out_shape,
        compiler_params=vmem_limit(60),
        cost_estimate=pl.CostEstimate(
            flops=4 * rows * model * model, bytes_accessed=4 * model * model, transcendentals=0
        ),
        name="output_back",
    )(*given, *[everything] * shape.panels)


def owned_kernel(part, term_ref, *refs):
    groups, rows, columns = term_ref.shape
    model = refs[0].shape[1]
    total = None
    for group in range(groups):
        term = term_ref[group].astype(f32)
        for k in range(3):
            first = model + k * part
            refs[k][:, group * part : (group + 1) * part] = term[:, first : first + part]
        total = term if total is None else total + term
    refs[3][...] = total[:, :model]
    extras = total[:, model + 3 * part :]
    short = jnp.zeros((BLOCK - rows, BLOCK), f32)
    refs[4][...] = jnp.concatenate([extras, short], axis=0).T[:8]


def owned_stage(terms, model, part):
    groups, rows, columns = terms.shape
    whole = lambda array: pl.BlockSpec(array.shape, lambda i: (0,) * array.ndim)
    out_shape = [jax.ShapeDtypeStruct((rows, model), f32)] * 4 + [
        jax.ShapeDtypeStruct((8, BLOCK), f32)
    ]
    return pl.pallas_call(
        functools.partial(owned_kernel, part),
        grid=(1,),
        in_specs=[whole(terms)],
        out_specs=[whole(array) for array in out_shape],
        out_shape=out_shape,
        compiler_params=vmem_limit(16),
        cost_estimate=pl.CostEstimate(
            flops=terms.size, bytes_accessed=4 * terms.size, transcendentals=0
        ),
        name="owned_stage",
    )(terms)


def swap(value, axis):
    return lax.ppermute(value, axis, [(0, 1), (1, 0)])


def pick(pair, index, axis):
    return lax.dynamic_index_in_dim(pair, index, axis, keepdims=False)


def in_order(mine, theirs, index, axis):
    return jnp.where(
        index == 0, jnp.stack([mine, theirs], axis), jnp.stack([theirs, mine], axis)
    )


def plus(mine, came):
    return (mine.astype(f32) + came.astype(f32)).astype(bf16)


def halve(value, index, name, axis):
    return plus(pick(value, index, axis), swap(pick(value, 1 - index, axis), name))


def turn(value, shift):
    count = 2 * 2
    return lax.ppermute(value, ("zh", "zl"), [(i, (i + shift) % count) for i in range(count)])


def exchange(value, axes, index, axis):
    count = value.shape[axis]
    result = value
    for mask in range(1, count):
        came = lax.ppermute(
            pick(value, index ^ mask, axis), axes, [(i, i ^ mask) for i in range(count)]
        )
        result = lax.dynamic_update_index_in_dim(result, came, index ^ mask, axis)
    return result


def columns_in_panels(weight):
    rows, cols = weight.shape
    return jnp.transpose(weight.reshape(rows, cols // PANEL, PANEL), (1, 0, 2)).reshape(
        rows * cols // PANEL, PANEL
    )


def own_half(weight, each, c):
    rows, cols = weight.shape
    return pick(weight.reshape(rows, cols // (2 * each), 2, each), c, 2).reshape(rows, cols // 2)


def body(
    inputs,
    w_query,
    w_key,
    w_value,
    w_output,
    w_gate,
    w_upper,
    w_down,
    gain_one,
    gain_two,
    bias_table,
    buckets,
    cotangent,
    sizes,
):
    along_dp, along_a = sizes
    dp, a, x, c = (lax.axis_index(name) for name in ("dp", "a", "x", "c"))
    zh, zl = lax.axis_index("zh"), lax.axis_index("zl")
    z, group = 2 * zh + zl, 2 * zl + x
    depth = 4
    seqs, local_rows, model = inputs.shape
    length = buckets.shape[0] // 2 + 1
    width = model // H
    heads = H // GROUPS
    part = heads * width
    weight_rows, hidden_units = w_gate.shape
    each = w_down.shape[0]
    own_count = depth * 2 * local_rows
    token_count = seqs * local_rows

    column = jnp.zeros((depth, local_rows, model), bf16)
    column = lax.dynamic_update_index_in_dim(column, pick(inputs, zh, 0), z, 0)
    for shift in range(1, depth):
        arriving = turn(pick(inputs, (z + shift) % depth // 2, 0), shift)
        column = lax.dynamic_update_index_in_dim(column, arriving, (z - shift) % depth, 0)
    tokens_own = in_order(column, swap(column, "x"), x, 1).reshape(own_count, model)

    blocks = [
        jnp.transpose(w.reshape(weight_rows, GROUPS, part), (1, 0, 2))
        for w in (w_query, w_key, w_value)
    ]
    table_column = jnp.pad(bias_table, (0, weight_rows - bias_table.shape[0]))
    extra = jnp.stack([gain_one, gain_two, table_column], axis=1)
    extra = jnp.pad(extra, ((0, 0), (0, BLOCK - extra.shape[1])))
    extra = jnp.broadcast_to(extra[None], (GROUPS, weight_rows, BLOCK))
    columns = lax.all_to_all(
        jnp.concatenate([*blocks, extra], axis=2), ("zl", "x"), 0, 0, tiled=True
    )
    columns = in_order(columns, swap(columns, "zh"), zh, 0)
    if along_a > 1:
        columns = lax.all_gather(columns, "a", axis=0)
    columns = in_order(columns, swap(columns, "dp"), dp, 0)
    columns = in_order(columns, swap(columns, "c"), c, columns.ndim - 2)
    columns = columns.reshape(model, 3 * part + BLOCK)
    gain_a = columns[:, 3 * part].astype(f32).reshape(1, model)
    gain_b = columns[:, 3 * part + 1].astype(f32).reshape(1, model)
    table = columns[:, 3 * part + 2].reshape(model // weight_rows, weight_rows)
    table = table[:, : bias_table.shape[0]].reshape(BUCKETS, H)
    padded = jnp.pad(buckets, (0, 1), constant_values=BLOCK)
    hot = (padded[:, None] == jnp.arange(BLOCK, dtype=jnp.int32)[None, :]).astype(bf16)
    own_table = lax.dynamic_slice_in_dim(table, group * heads, heads, 1)
    own_table = jnp.pad(own_table, ((0, BLOCK - BUCKETS), (0, 0)))
    ahead = jnp.pad(buckets, (1, 0), constant_values=BLOCK)
    hot_ahead = (ahead[None, :] == jnp.arange(BLOCK, dtype=jnp.int32)[:, None]).astype(bf16)
    vectors = lax.dot_general(
        own_table, hot_ahead, (((0,), (0,)), ((), ())), preferred_element_type=f32
    ).reshape(heads, 1, 2 * length)

    if along_a == 1:
        sent = [own_half(w, each, 1 - c) for w in (w_gate, w_upper)] + [w_output]
        came = swap(jnp.concatenate(sent, axis=1), "c")
        kept = [own_half(w, each, c) for w in (w_gate, w_upper)] + [w_output]
        both = in_order(jnp.concatenate(kept, axis=1), came, c, 0).reshape(2 * weight_rows, -1)
        packed = jnp.concatenate(
            [
                columns_in_panels(both[:, :hidden_units]),
                columns_in_panels(w_down),
                columns_in_panels(both[:, hidden_units:]),
            ],
            axis=0,
        )
        pieces = along_dp * depth * 2
        everything = lax.all_gather(packed, chips, axis=0, tiled=True)
        everything = everything.reshape(pieces, packed.shape[0], PANEL)
    else:
        pieces = 1
        gate_all, upper_all, down_all, output_all = (
            lax.all_gather(w, everyone, axis=0, tiled=True)
            for w in (w_gate, w_upper, w_down, w_output)
        )
        down_half = pick(down_all.reshape(-1, 2, each, model), c, 1).reshape(-1, model)
        everything = jnp.concatenate(
            [
                columns_in_panels(own_half(gate_all, each, c)),
                columns_in_panels(own_half(upper_all, each, c)),
                columns_in_panels(down_half),
                columns_in_panels(output_all),
            ],
            axis=0,
        )[None]
    shape = PackedWeights(model, hidden_units // 2, pieces)

    if along_a > 1:
        tokens_all = lax.all_gather(tokens_own, "a", axis=0, tiled=True)
    else:
        tokens_all = tokens_own
    normed, query, own = project(tokens_all, gain_a, columns, heads, width)
    if along_a > 1:
        query = lax.dynamic_slice_in_dim(query, a * own_count, own_count, 1)
        normed = lax.dynamic_slice_in_dim(normed, a * own_count, own_count, 0)
    other = swap(own, "c")
    biases = skew(vectors)
    place = jnp.stack([a * (own_count // BLOCK), c]).astype(jnp.int32)
    context_own, probs, kept, inverse = attend(place, query, own, other, biases)
    owners = ("zh", "zl", "x")
    context = lax.all_to_all(context_own, owners, 0, 0, tiled=True)

    down_grad = cotangent.reshape(token_count, model)
    down_other = swap(down_grad, "c")
    residual, second = output_stage(context, inputs, gain_b, everything, shape)
    second_other = swap(second, "c")
    sides_place = jnp.stack([x, dp]).astype(jnp.int32)
    out_own, out_other, norm_own, norm_other, *big_grads = hidden_stage(
        sides_place, second, second_other, down_grad, down_other, everything, shape
    )
    norm_came = swap(norm_other, "c")
    out_came = swap(out_other, "c")
    outputs = (residual + out_own + out_came.astype(f32)).astype(bf16)
    residual_grad, gain_b_grad, context_sent, output_grad = output_back(
        norm_own, norm_came, residual, down_grad, gain_b, context, everything, shape
    )
    context_grad = lax.all_to_all(context_sent, owners, 0, 0, tiled=True)
    if along_a == 1:
        first_terms, first_sent, second_terms, second_sent = big_grads
        first_came = swap(first_sent, "x")
        second_came = swap(second_sent, "dp")
    output_terms = output_grad.reshape(
        along_dp, along_a, 2, GROUPS, CORES, weight_rows, model
    )
    output_terms = halve(output_terms, c, "c", 4)

    if along_a == 1:
        context_grad, first_came, second_came = lax.optimization_barrier(
            (context_grad, first_came, second_came)
        )
        first_terms = plus(first_terms, first_came).reshape(along_dp, depth, -1, PANEL)
        second_terms = plus(second_terms, second_came).reshape(depth, 2, -1, PANEL)
        first_terms, second_terms, context_grad, output_terms = lax.optimization_barrier(
            (first_terms, second_terms, context_grad, output_terms)
        )
        first_came = swap(pick(first_terms, 1 - dp, 0), "dp")
        second_came = swap(pick(second_terms, 1 - x, 1), "x")
    output_came = swap(pick(output_terms, 1 - dp, 0), "dp")

    query_grads, owns, came, offset_grads = [], [], [], []
    for first, count in ((0, 1), (1, heads - 1)):
        query_grad, own_grad, other_grad, offset_grad = attend_back(
            place, context_grad, kept, inverse, probs, query, own, other, hot, first, count
        )
        if along_a > 1:
            own_grad, other_grad = (
                lax.psum_scatter(value, "a", scatter_dimension=2, tiled=True)
                for value in (own_grad, other_grad)
            )
        elif first == 0:
            first_came, second_came, output_came, query_grad, own_grad, other_grad, offset_grad = (
                lax.optimization_barrier(
                    (
                        first_came,
                        second_came,
                        output_came,
                        query_grad,
                        own_grad,
                        other_grad,
                        offset_grad,
                    )
                )
            )
            terms = jnp.concatenate(
                [
                    plus(pick(first_terms, dp, 0), first_came),
                    plus(pick(second_terms, x, 1), second_came),
                ],
                axis=1,
            )
            output_terms = plus(pick(output_terms, dp, 0), output_came)
            terms, output_terms, context_grad = lax.optimization_barrier(
                (terms, output_terms, context_grad)
            )
            column_came = [
                turn(pick(terms, (z + shift) % depth, 0), shift) for shift in range(1, depth)
            ]
        else:
            *column_came, query_grad, own_grad, other_grad, offset_grad = (
                lax.optimization_barrier(
                    (*column_came, query_grad, own_grad, other_grad, offset_grad)
                )
            )
        query_grads.append(query_grad)
        owns.append(own_grad)
        came.append(swap(other_grad, "c"))
        offset_grads.append(offset_grad)
    if along_a > 1:
        output_terms = plus(pick(output_terms, dp, 0), output_came)
    per_owner = bias_table.shape[0]
    bucket_sums = jnp.concatenate(offset_grads, axis=0)[:, 0, :BUCKETS]
    spot = jnp.arange(model, dtype=jnp.int32)
    entry = spot // weight_rows * per_owner + spot % weight_rows
    entry = jnp.where(spot % weight_rows < per_owner, entry, -1)
    spread = (entry[None, :] // H == jnp.arange(BUCKETS, dtype=jnp.int32)[:, None]).astype(bf16)
    table_rows = jnp.dot(bucket_sums.astype(bf16), spread, preferred_element_type=f32)
    own_heads = group * heads + jnp.arange(heads, dtype=jnp.int32)
    table_row = jnp.sum(
        jnp.where(entry[None, :] % H == own_heads[:, None], table_rows, 0.0), axis=0
    )
    extra = jnp.stack(
        [jnp.zeros((model,), f32), gain_b_grad.reshape(model), table_row]
        + [jnp.zeros((model,), f32)] * 5
    )
    core_place = jnp.stack([x, c]).astype(jnp.int32)
    *rows_grads, mixed, sent_c = project_back(
        core_place, query_grads, owns, came, normed, tokens_own, columns, extra, weight_rows
    )

    by_owner = (along_dp, along_a, 2, GROUPS, weight_rows, mixed.shape[2])
    mixed, sent_c, sent = mixed.reshape(by_owner), sent_c.reshape(by_owner), rows_grads[2:]
    came_x = [swap(value, "x") for value in sent]
    came_c = swap(sent_c, "c")
    mixed = plus(mixed, came_c)
    sent_dp, mixed, came_x[0] = lax.optimization_barrier(
        (pick(mixed, 1 - dp, 0), pick(mixed, dp, 0), came_x[0])
    )
    came_dp = swap(sent_dp, "dp")
    arrived = []

    def along_column(k):
        share = plus(rows_grads[k], came_x[k])
        return [pick(share, (z + shift) % depth, 0) for shift in range(depth)]

    def turned(parts):
        return [part if shift == 0 else turn(part, shift) for shift, part in enumerate(parts)]

    *parts, came_dp = lax.optimization_barrier((*along_column(0), came_dp))
    arrived += turned(parts)
    mixed = jnp.concatenate([output_terms, plus(mixed, came_dp)], axis=4)
    sent_zh, mixed, came_x[1] = lax.optimization_barrier(
        (pick(mixed, 1 - zh, 1), pick(mixed, zh, 1), came_x[1])
    )
    came_zh = swap(sent_zh, "zh")
    *parts, came_zh = lax.optimization_barrier((*along_column(1), came_zh))
    arrived += turned(parts)
    mixed = plus(mixed, came_zh)
    if along_a > 1:
        mixed = lax.psum_scatter(mixed, "a", scatter_dimension=0, tiled=True)
    *early, terms_owned = lax.optimization_barrier((*arrived[:depth], mixed[0]))
    arrived = early + arrived[depth:]
    terms_owned = lax.all_to_all(terms_owned, ("zl", "x"), 0, 0, tiled=True)
    origins = jnp.stack([(z - shift) % depth // 2 for shift in range(depth)]).astype(jnp.int32)
    input_grad = rows_stage(origins, inputs, residual_grad, gain_a, arrived)

    if along_a == 1:
        total = pick(terms, z, 0).astype(f32)
        for arriving in column_came:
            total = total + arriving.astype(f32)
        side, deep = shape.steps * shape.side, shape.deep
        sides = jnp.concatenate([total[:side], total[side + deep : 2 * side + deep]], axis=0)
        sides = sides.astype(bf16).reshape(-1, 2, weight_rows, PANEL)
        sides = in_order(pick(sides, c, 1), swap(pick(sides, 1 - c, 1), "c"), c, 0)
        sides = sides.reshape(2, 2, shape.steps, weight_rows, PANEL)
        sides = jnp.transpose(
            sides.reshape(2, 2, shape.steps, weight_rows, PANEL // each, each), (1, 3, 2, 4, 0, 5)
        ).reshape(2, weight_rows, hidden_units)
        gate_owned, upper_owned = sides[0].astype(f32), sides[1].astype(f32)
        down_owned = jnp.transpose(
            jnp.concatenate([total[side : side + deep], total[2 * side + deep :]], axis=0).reshape(
                shape.panels, each, PANEL
            ),
            (1, 0, 2),
        ).reshape(each, model)
    else:
        side = shape.steps * model
        gate_half, upper_half = (
            jnp.transpose(
                big_grads[0][0, k * side : (k + 1) * side].reshape(shape.steps, model, PANEL),
                (1, 0, 2),
            ).reshape(model, -1, 1, each)
            for k in range(2)
        )
        down_half = jnp.transpose(
            big_grads[0][0, 2 * side :].reshape(shape.panels, -1, PANEL), (1, 0, 2)
        ).reshape(-1, 1, each, model)
        zero = jnp.zeros_like
        gate_owned, upper_owned = (
            lax.psum_scatter(
                in_order(half, zero(half), c, 2).reshape(model, hidden_units),
                everyone,
                scatter_dimension=0,
                tiled=True,
            ).astype(f32)
            for half in (gate_half, upper_half)
        )
        down_owned = lax.psum_scatter(
            in_order(down_half, zero(down_half), c, 1).reshape(hidden_units, model),
            everyone,
            scatter_dimension=0,
            tiled=True,
        ).astype(f32)

    *owned, extras = owned_stage(terms_owned, model, part)
    return (
        outputs.reshape(seqs, local_rows, model),
        input_grad,
        *owned,
        gate_owned,
        upper_owned,
        down_owned,
        extras[0, :weight_rows],
        extras[1, :weight_rows],
        extras[2, :per_owner],
    )


def solution(mesh):
    along_dp, along_ctx = mesh.shape["dp"], mesh.shape["ctx"]
    along_a = along_ctx // (4 * 2 * CORES)
    fine = Mesh(mesh.devices.reshape(along_dp, along_a, 2, 2, 2, CORES), everyone)
    rows = P("dp", ("a", "zh", "zl", "x", "c"), None)
    owned = P(everyone, None)
    vector = P(everyone)
    in_specs = (rows, *[owned] * 7, *[vector] * 3, P(), rows)
    out_specs = (rows, rows, *[owned] * 7, *[vector] * 3)
    return jax.shard_map(
        functools.partial(body, sizes=(along_dp, along_a)),
        mesh=fine,
        in_specs=in_specs,
        out_specs=out_specs,
        check_vma=False,
    )
```

```python
import functools

import jax
import jax.numpy as jnp
from jax import lax
from jax.experimental import pallas as pl
from jax.experimental.pallas import tpu as pltpu
from jax.sharding import Mesh
from jax.sharding import PartitionSpec as P

H = 12
BUCKETS = 32
GROUPS = 4
CORES = 2
BLOCK = 128

epsilon = 1e-06
exactly = lax.Precision.HIGHEST
bf16 = jnp.bfloat16
f32 = jnp.float32
everyone = ("dp", "a", "zh", "zl", "x", "c")
chips = ("dp", "zh", "zl", "x")
PANEL = 256


def rms_scale(values, gain_vec):
    return (
        values * lax.rsqrt(jnp.mean(values * values, axis=-1, keepdims=True) + epsilon) * gain_vec
    )


def vmem_limit(mib):
    return pltpu.CompilerParams(vmem_limit_bytes=mib * 1024 * 1024)


def project_kernel(heads, token_ref, gain_ref, weight_ref, normed_ref, query_ref, pair_ref):
    rows = token_ref[...].astype(f32)
    scale = lax.rsqrt(jnp.mean(rows * rows, axis=-1, keepdims=True) + epsilon)
    normed = (rows * scale * gain_ref[...]).astype(bf16)
    normed_ref[...] = normed
    width = query_ref.shape[2]
    mixed = jnp.dot(
        normed, weight_ref[:, : 3 * heads * width], preferred_element_type=f32
    ).astype(bf16)
    for k in range(heads):
        query_ref[k] = mixed[:, k * width : (k + 1) * width]
        for side in range(2):
            first = (heads * (side + 1) + k) * width
            pair_ref[k, :, side * width : (side + 1) * width] = mixed[:, first : first + width]


def project(tokens, gain_row, weight, heads, width):
    rows, model = tokens.shape
    tile = 256
    return pl.pallas_call(
        functools.partial(project_kernel, heads),
        grid=(rows // tile,),
        in_specs=[
            pl.BlockSpec((tile, model), lambda i: (i, 0)),
            pl.BlockSpec((1, model), lambda i: (0, 0)),
            pl.BlockSpec(weight.shape, lambda i: (0, 0)),
        ],
        out_specs=[
            pl.BlockSpec((tile, model), lambda i: (i, 0)),
            pl.BlockSpec((heads, tile, width), lambda i: (0, i, 0)),
            pl.BlockSpec((heads, tile, 2 * width), lambda i: (0, i, 0)),
        ],
        out_shape=[
            jax.ShapeDtypeStruct((rows, model), bf16),
            jax.ShapeDtypeStruct((heads, rows, width), bf16),
            jax.ShapeDtypeStruct((heads, rows, 2 * width), bf16),
        ],
        compiler_params=vmem_limit(12),
        cost_estimate=pl.CostEstimate(
            flops=2 * rows * model * 3 * heads * width,
            bytes_accessed=8 * rows * model,
            transcendentals=0,
        ),
        name="project",
    )(tokens, gain_row, weight)


def skew_kernel(vector_ref, table_ref, row_scratch):
    span = vector_ref.shape[-1]
    for r in range(8):
        row_scratch[r : r + 1, :] = pltpu.roll(vector_ref[0], r, 1) if r else vector_ref[0]
    eight = row_scratch[...]
    rows = []
    for group in range(BLOCK // 8):
        turned = pltpu.roll(eight, 8 * group, 1) if group else eight
        rows.append(turned[:, BLOCK:span])
    for pair in range(BLOCK // 16):
        both = jnp.concatenate(rows[2 * pair : 2 * pair + 2], axis=0)
        table_ref[0, 16 * pair : 16 * pair + 16, :] = both.astype(bf16)


def skew(vectors):
    heads, unused, span = vectors.shape
    return pl.pallas_call(
        skew_kernel,
        grid=(heads,),
        in_specs=[pl.BlockSpec((1, 1, span), lambda h: (h, 0, 0))],
        out_specs=pl.BlockSpec((1, BLOCK, span - BLOCK), lambda h: (h, 0, 0)),
        out_shape=jax.ShapeDtypeStruct((heads, BLOCK, span - BLOCK), bf16),
        scratch_shapes=[pltpu.VMEM((8, span), f32)],
        compiler_params=vmem_limit(10),
        cost_estimate=pl.CostEstimate(
            flops=0, bytes_accessed=2 * heads * BLOCK * span, transcendentals=0
        ),
        name="skew",
    )(vectors)


def interleave(keys, values, own_ref, other_ref, parity, fill):
    width = keys.shape[1]
    for k in range(own_ref.shape[1] // BLOCK):
        rows = slice(k * BLOCK, (k + 1) * BLOCK)
        for source, spot in ((own_ref, parity), (other_ref, 1 - parity)):
            into = pl.ds(pl.multiple_of((2 * k + spot) * BLOCK, BLOCK), BLOCK)
            keys[into, :] = source[0, rows, :width]
            values[into, :width] = source[0, rows, width:]
            if fill:
                values[into, width:] = jnp.ones((BLOCK, width), bf16)


def table_starts(tile, step, first_block, parity, blocks):
    starts = []
    for sub in range(tile // BLOCK):
        block = 2 * (first_block + step * (tile // BLOCK) + sub) + parity
        starts.append((blocks - 1 - block) * BLOCK)
    return starts


def attend_kernel(
    tile,
    chunk,
    place_ref,
    query_ref,
    pair_own,
    pair_other,
    table,
    context_ref,
    probs_ref,
    kept_ref,
    inverse_ref,
    keys,
    values,
    scores,
):
    head, step = pl.program_id(0), pl.program_id(1)
    first_block, parity = place_ref[0], place_ref[1]
    key_count, width = keys.shape
    blocks = key_count // BLOCK
    subs = tile // BLOCK
    table = table.at[0]

    @pl.when(step == 0)
    def prepare():
        interleave(keys, values, pair_own, pair_other, parity, True)

    query = query_ref[0]
    starts = table_starts(tile, step, first_block, parity, blocks)
    lane_max = None
    for part in range(key_count // chunk):
        cols = slice(part * chunk, (part + 1) * chunk)
        product = lax.dot_general(
            query, keys[cols, :], (((1,), (1,)), ((), ())), preferred_element_type=f32
        )
        pieces = []
        for sub in range(subs):
            rows = slice(sub * BLOCK, (sub + 1) * BLOCK)
            offset = pl.multiple_of(starts[sub] + part * chunk, BLOCK)
            piece = product[rows] + table[:, pl.ds(offset, chunk)].astype(f32)
            scores[rows, cols] = piece
            for k in range(chunk // BLOCK):
                lanes = piece[:, k * BLOCK : (k + 1) * BLOCK]
                top = lanes if k == 0 else jnp.maximum(top, lanes)
            pieces.append(top)
        pieces = jnp.concatenate(pieces, axis=0)
        lane_max = pieces if lane_max is None else jnp.maximum(lane_max, pieces)
    row_max = jnp.max(lane_max, axis=-1, keepdims=True)
    total = jnp.zeros((tile, 2 * width), f32)
    for part in range(key_count // chunk):
        cols = slice(part * chunk, (part + 1) * chunk)
        low = jnp.exp(scores[:, cols] - row_max).astype(bf16)
        probs_ref[0, :, cols] = low
        total = total + jnp.dot(low, values[cols, :], preferred_element_type=f32)
    inverse = 1.0 / total[:, width:]
    value = total[:, :width] * inverse
    kept_ref[0, :, :width] = value
    kept_ref[0, :, width:] = inverse
    turned = value.T.astype(bf16)
    inverse_turned = inverse.T
    for sub in range(subs):
        lanes = slice(sub * BLOCK, (sub + 1) * BLOCK)
        rows = pl.ds(pl.multiple_of(head * width, width), width)
        context_ref[step * subs + sub, rows, :] = turned[:, lanes]
        inverse_ref[0, sub] = inverse_turned[0:1, lanes]


def attend(place, query, own, other, table):
    heads, rows, width = query.shape
    own_rows = own.shape[1]
    key_count = 2 * own_rows
    tile, chunk = 256, 512
    pairs = pl.BlockSpec((1, own_rows, 2 * width), lambda h, i, s: (h, 0, 0))
    return pl.pallas_call(
        functools.partial(attend_kernel, tile, chunk),
        grid_spec=pltpu.PrefetchScalarGridSpec(
            num_scalar_prefetch=1,
            grid=(heads, rows // tile),
            in_specs=[
                pl.BlockSpec((1, tile, width), lambda h, i, s: (h, i, 0)),
                pairs,
                pairs,
                pl.BlockSpec((1, *table.shape[1:]), lambda h, i, s: (h, 0, 0)),
            ],
            out_specs=[
                pl.BlockSpec((rows // BLOCK, heads * width, BLOCK), lambda h, i, s: (0, 0, 0)),
                pl.BlockSpec((1, tile, key_count), lambda h, i, s: (h, i, 0)),
                pl.BlockSpec((1, tile, 2 * width), lambda h, i, s: (h, i, 0)),
                pl.BlockSpec((1, tile // BLOCK, 1, BLOCK), lambda h, i, s: (h, i, 0, 0)),
            ],
            scratch_shapes=[
                pltpu.VMEM((key_count, width), bf16),
                pltpu.VMEM((key_count, 2 * width), bf16),
                pltpu.VMEM((tile, key_count), f32),
            ],
        ),
        out_shape=[
            jax.ShapeDtypeStruct((rows // BLOCK, heads * width, BLOCK), bf16),
            jax.ShapeDtypeStruct((heads, rows, key_count), bf16),
            jax.ShapeDtypeStruct((heads, rows, 2 * width), f32),
            jax.ShapeDtypeStruct((heads, rows // BLOCK, 1, BLOCK), f32),
        ],
        compiler_params=vmem_limit(54),
        cost_estimate=pl.CostEstimate(
            flops=16 * heads * rows * key_count * width,
            bytes_accessed=2 * heads * rows * key_count,
            transcendentals=heads * rows * key_count,
        ),
        name="attend",
    )(place, query, own, other, table)


def attend_back_kernel(
    tile,
    chunk,
    place_ref,
    grad_ref,
    kept_ref,
    inverse_ref,
    probs_ref,
    query_ref,
    pair_own,
    pair_other,
    hot_ref,
    query_grad_ref,
    own_grad_ref,
    other_grad_ref,
    offset_ref,
    keys,
    values,
    diagonals,
    key_sums,
    value_sums,
):
    step = pl.program_id(1)
    first_block, parity = place_ref[0], place_ref[1]
    key_count, width = keys.shape
    blocks = key_count // BLOCK
    subs = tile // BLOCK

    @pl.when(step == 0)
    def prepare():
        interleave(keys, values, pair_own, pair_other, parity, False)
        diagonals[...] = jnp.zeros_like(diagonals)
        key_sums[...] = jnp.zeros_like(key_sums)
        value_sums[...] = jnp.zeros_like(value_sums)

    turned = jnp.concatenate(
        [grad_ref[sub].astype(f32) * inverse_ref[0, sub] for sub in range(subs)], axis=1
    )
    grad_turned = turned.astype(bf16)
    scaled = grad_turned.astype(f32).T
    delta = jnp.sum(scaled * kept_ref[0, :, :width], axis=-1, keepdims=True)
    scaled = scaled.astype(bf16)
    query_turned = query_ref[0].astype(f32).T.astype(bf16)
    starts = table_starts(tile, step, first_block, parity, blocks)
    query_grad = jnp.zeros((tile, width), f32)
    for part in range(key_count // chunk):
        cols = slice(part * chunk, (part + 1) * chunk)
        prob_grad = lax.dot_general(
            scaled, values[cols, :], (((1,), (1,)), ((), ())), preferred_element_type=f32
        )
        low = probs_ref[0, :, cols]
        score_grad = low.astype(f32) * (prob_grad - delta)
        for sub in range(subs):
            rows = slice(sub * BLOCK, (sub + 1) * BLOCK)
            offset = pl.multiple_of(starts[sub] + part * chunk, BLOCK)
            diagonals[:, pl.ds(offset, chunk)] += score_grad[rows]
        score_low = score_grad.astype(bf16)
        query_grad = query_grad + jnp.dot(score_low, keys[cols, :], preferred_element_type=f32)
        key_sums[:, cols] += jnp.dot(query_turned, score_low, preferred_element_type=f32)
        value_sums[:, cols] += jnp.dot(grad_turned, low, preferred_element_type=f32)
    query_grad_ref[0] = query_grad.astype(bf16)

    @pl.when(step == pl.num_programs(1) - 1)
    def finish():
        span = diagonals.shape[1]
        eight = diagonals[0:8, :]
        for group in range(1, BLOCK // 8):
            eight = eight + pltpu.roll(
                diagonals[8 * group : 8 * group + 8, :], span - 8 * group, 1
            )
        total = eight[0:1, :]
        for r in range(1, 8):
            total = total + pltpu.roll(eight[r : r + 1, :], span - r, 1)
        total = pltpu.roll(total, BLOCK - 1, 1)
        bucket_sums = None
        for unused in range(3):
            low = total.astype(bf16)
            total = total - low.astype(f32)
            more = jnp.dot(low, hot_ref[...], preferred_element_type=f32)
            bucket_sums = more if bucket_sums is None else bucket_sums + more
        offset_ref[0] = bucket_sums
        for sums, rows in ((key_sums, slice(0, width)), (value_sums, slice(width, 2 * width))):
            for b in range(blocks // 2):
                near = pl.multiple_of((2 * b + parity) * BLOCK, BLOCK)
                far = pl.multiple_of((2 * b + 1 - parity) * BLOCK, BLOCK)
                lanes = slice(b * BLOCK, (b + 1) * BLOCK)
                own_grad_ref[0, rows, lanes] = sums[:, pl.ds(near, BLOCK)].astype(bf16)
                other_grad_ref[0, rows, lanes] = sums[:, pl.ds(far, BLOCK)].astype(bf16)


def attend_back(place, grad, kept, inverse, probs, query, own, other, hot):
    count, rows, width = query.shape
    own_rows = own.shape[1]
    key_count = 2 * own_rows
    span = key_count * 2
    tile, chunk = 512, 512
    pairs = pl.BlockSpec((1, own_rows, 2 * width), lambda h, i, s: (h, 0, 0))
    return pl.pallas_call(
        functools.partial(attend_back_kernel, tile, chunk),
        grid_spec=pltpu.PrefetchScalarGridSpec(
            num_scalar_prefetch=1,
            grid=(count, rows // tile),
            in_specs=[
                pl.BlockSpec(
                    (tile // BLOCK, width, BLOCK), lambda h, i, s: (i, h, 0)
                ),
                pl.BlockSpec((1, tile, 2 * width), lambda h, i, s: (h, i, 0)),
                pl.BlockSpec((1, tile // BLOCK, 1, BLOCK), lambda h, i, s: (h, i, 0, 0)),
                pl.BlockSpec((1, tile, key_count), lambda h, i, s: (h, i, 0)),
                pl.BlockSpec((1, tile, width), lambda h, i, s: (h, i, 0)),
                pairs,
                pairs,
                pl.BlockSpec(hot.shape, lambda h, i, s: (0, 0)),
            ],
            out_specs=[
                pl.BlockSpec((1, tile, width), lambda h, i, s: (h, i, 0)),
                pl.BlockSpec((1, 2 * width, own_rows), lambda h, i, s: (h, 0, 0)),
                pl.BlockSpec((1, 2 * width, own_rows), lambda h, i, s: (h, 0, 0)),
                pl.BlockSpec((1, 1, hot.shape[1]), lambda h, i, s: (h, 0, 0)),
            ],
            scratch_shapes=[
                pltpu.VMEM((key_count, width), bf16),
                pltpu.VMEM((key_count, width), bf16),
                pltpu.VMEM((BLOCK, span), f32),
                pltpu.VMEM((width, key_count), f32),
                pltpu.VMEM((width, key_count), f32),
            ],
        ),
        out_shape=[
            jax.ShapeDtypeStruct((count, rows, width), bf16),
            jax.ShapeDtypeStruct((count, 2 * width, own_rows), bf16),
            jax.ShapeDtypeStruct((count, 2 * width, own_rows), bf16),
            jax.ShapeDtypeStruct((count, 1, hot.shape[1]), f32),
        ],
        compiler_params=vmem_limit(54),
        cost_estimate=pl.CostEstimate(
            flops=32 * count * rows * key_count * width,
            bytes_accessed=2 * count * rows * key_count,
            transcendentals=0,
        ),
        name="attend_back",
    )(place, grad, kept, inverse, probs, query, own, other, hot)


def project_back_kernel(
    place_ref,
    normed_ref,
    weight_ref,
    extra_ref,
    query_grad_ref,
    own_ref,
    came_ref,
    kept_rows,
    sent_rows,
    kept_ref,
    sent_ref,
    turned,
    sums,
    gains,
):
    step = pl.program_id(0)
    heads, unused, width = query_grad_ref.shape
    part = heads * width
    for head in range(heads):
        turned[head * width : (head + 1) * width, :] = query_grad_ref[head].T
        both = (own_ref[head].astype(f32) + came_ref[head].astype(f32)).astype(bf16)
        for side in range(2):
            at = part * (side + 1) + head * width
            turned[at : at + width, :] = both[side * width : (side + 1) * width]
    grads = turned[...]
    normed_grad = lax.dot_general(
        grads,
        weight_ref[:, : 3 * part],
        (((0,), (1,)), ((), ())),
        preferred_element_type=f32,
    )
    low = normed_grad.astype(bf16)
    half = low.shape[0] // 2
    for k in range(2):

        @pl.when(place_ref[0] == k)
        def store():
            kept_rows[0] = low[k * half : (k + 1) * half]
            sent_rows[0] = low[(1 - k) * half : (2 - k) * half]

    gain = jnp.sum(normed_grad * normed_ref[...].astype(f32), axis=0, keepdims=True)
    update = jnp.dot(grads, normed_ref[...], preferred_element_type=f32)

    @pl.when(step == 0)
    def start():
        sums[...] = update
        gains[...] = extra_ref[...]

    @pl.when(step != 0)
    def more():
        sums[...] += update

    gains[0:1, :] += gain / extra_ref[3:4, :]

    @pl.when(step == pl.num_programs(0) - 1)
    def finish():
        update = sums[...].T
        model = update.shape[0]
        extras = jnp.concatenate(
            [gains[...], jnp.zeros((BLOCK - gains.shape[0], model), f32)], axis=0
        ).T
        owners, rows, columns = kept_ref.shape
        for k in range(2):

            @pl.when(place_ref[1] == k)
            def pack():
                for owner in range(owners):
                    for ref, core in ((kept_ref, k), (sent_ref, 1 - k)):
                        at = slice((2 * owner + core) * rows, (2 * owner + core + 1) * rows)
                        ref[owner, :, : 3 * part] = update[at].astype(bf16)
                        ref[owner, :, 3 * part :] = extras[at].astype(bf16)


def project_back(place, query_grad, own, came, normed, weight, extra, weight_rows):
    rows, model = normed.shape
    heads, unused, width = query_grad.shape
    part = heads * width
    tile = 2 * BLOCK
    steps = rows // tile
    whole = lambda shape: pl.BlockSpec(shape, lambda i, s: (0, 0))
    pairs = pl.BlockSpec((heads, 2 * width, tile), lambda i, s: (0, 0, i))
    share = pl.BlockSpec((1, BLOCK, model), lambda i, s: (i, 0, 0))
    packed = (model // (2 * weight_rows), weight_rows, 3 * part + BLOCK)
    return pl.pallas_call(
        project_back_kernel,
        grid_spec=pltpu.PrefetchScalarGridSpec(
            num_scalar_prefetch=1,
            grid=(steps,),
            in_specs=[
                pl.BlockSpec((tile, model), lambda i, s: (i, 0)),
                whole(weight.shape),
                whole(extra.shape),
                pl.BlockSpec((heads, tile, width), lambda i, s: (0, i, 0)),
                pairs,
                pairs,
            ],
            out_specs=[share] * 2 + [pl.BlockSpec(packed, lambda i, s: (0, 0, 0))] * 2,
            scratch_shapes=[
                pltpu.VMEM((3 * part, tile), bf16),
                pltpu.VMEM((3 * part, model), f32),
                pltpu.VMEM(extra.shape, f32),
            ],
        ),
        out_shape=[jax.ShapeDtypeStruct((steps, BLOCK, model), bf16)] * 2
        + [jax.ShapeDtypeStruct(packed, bf16)] * 2,
        compiler_params=vmem_limit(60),
        cost_estimate=pl.CostEstimate(
            flops=12 * rows * model * part, bytes_accessed=12 * rows * model, transcendentals=0
        ),
        name="project_back",
    )(place, normed, weight, extra, query_grad, own, came)


def rows_kernel(place_ref, token_ref, residual_ref, gain_ref, own_ref, other_ref, grad_ref):
    seqs, local_rows, model = token_ref.shape
    for k, normed_ref in enumerate((own_ref, other_ref)):
        seq = place_ref[0] ^ k
        weighted = normed_ref[...].astype(f32) * gain_ref[...]
        tokens = token_ref[seq].astype(f32)
        scale = lax.rsqrt(jnp.mean(tokens * tokens, axis=-1, keepdims=True) + epsilon)
        inner = jnp.mean(weighted * tokens, axis=-1, keepdims=True)
        rows = pl.ds(pl.multiple_of(seq * local_rows, local_rows), local_rows)
        grad_ref[seq] = (
            residual_ref[rows] + scale * weighted - tokens * (scale * scale * scale * inner)
        )


def rows_stage(place, tokens, residual_grad, gain_row, own, other):
    whole = lambda array: pl.BlockSpec(array.shape, lambda i, s: (0,) * array.ndim)
    given = (tokens, residual_grad, gain_row, own, other)
    return pl.pallas_call(
        rows_kernel,
        grid_spec=pltpu.PrefetchScalarGridSpec(
            num_scalar_prefetch=1,
            grid=(1,),
            in_specs=[whole(array) for array in given],
            out_specs=whole(tokens),
        ),
        out_shape=jax.ShapeDtypeStruct(tokens.shape, f32),
        compiler_params=vmem_limit(16),
        cost_estimate=pl.CostEstimate(
            flops=20 * tokens.size, bytes_accessed=16 * tokens.size, transcendentals=0
        ),
        name="rows_stage",
    )(place, *given)


def output_kernel(context_ref, token_ref, gain_ref, *refs):
    weights, (residual_ref, normed_ref) = refs[:-2], refs[-2:]
    seqs, local_rows, model = token_ref.shape
    groups = context_ref.shape[0] // seqs
    part = context_ref.shape[1]
    for seq in range(seqs):
        rows = slice(seq * local_rows, (seq + 1) * local_rows)
        for p, weight_ref in enumerate(weights):
            lanes = slice(p * PANEL, (p + 1) * PANEL)
            weight = weight_ref[...].reshape(model, PANEL)
            total = token_ref[seq, :, lanes].astype(f32)
            for group in range(groups):
                total = total + lax.dot_general(
                    context_ref[seq * groups + group],
                    weight[group * part : (group + 1) * part],
                    (((0,), (0,)), ((), ())),
                    preferred_element_type=f32,
                )
            residual_ref[rows, lanes] = total
    normed_ref[...] = rms_scale(residual_ref[...], gain_ref[...]).astype(bf16)


def output_stage(context, tokens, gain_row, everything, shape):
    seqs, local_rows, model = tokens.shape
    whole = lambda array: pl.BlockSpec(array.shape, lambda i: (0,) * array.ndim)
    return pl.pallas_call(
        output_kernel,
        grid=(1,),
        in_specs=[whole(context), whole(tokens), whole(gain_row)] + shape.output_specs(),
        out_specs=[pl.BlockSpec((seqs * local_rows, model), lambda i: (0, 0))] * 2,
        out_shape=[
            jax.ShapeDtypeStruct((seqs * local_rows, model), f32),
            jax.ShapeDtypeStruct((seqs * local_rows, model), bf16),
        ],
        compiler_params=vmem_limit(40),
        cost_estimate=pl.CostEstimate(
            flops=2 * seqs * local_rows * model * model,
            bytes_accessed=2 * model * model,
            transcendentals=0,
        ),
        name="output_stage",
    )(context, tokens, gain_row, *[everything] * shape.panels)


def hidden_kernel(shape, normed_own, normed_other, down_own, down_other, gate_w, upper_w, *refs):
    panels = shape.panels
    down_w = refs[:panels]
    norm_own, norm_other, hidden_ref, gate_ref, upper_ref = refs[panels : panels + 5]
    normed, downs, lows, sides, pres = refs[panels + 5 :]
    step = pl.program_id(0)
    half = normed_own.shape[0]

    @pl.when(step == 0)
    def gather():
        normed[:half] = normed_own[...]
        normed[half:] = normed_other[...]
        downs[:half] = down_own[...]
        downs[half:] = down_other[...]

    across = (((1,), (1,)), ((), ()))
    weights = []
    for side, weight_ref in enumerate((gate_w, upper_w)):
        weight = weight_ref[...].reshape(shape.model, PANEL)
        sides[side, step] = weight
        pres[side] = jnp.dot(normed[...], weight, preferred_element_type=f32)
    down = jnp.concatenate([ref[...].reshape(PANEL, PANEL) for ref in down_w], axis=1)
    pres[2] = lax.dot_general(downs[...], down, across, preferred_element_type=f32)
    slope = 0.7978845608028654
    tile = 64

    def bend_rows(k, carried):
        rows = pl.ds(pl.multiple_of(k * tile, tile), tile)
        gate_pre, up_pre, hidden_grad = pres[0, rows], pres[1, rows], pres[2, rows]
        square = gate_pre * gate_pre
        bend = jnp.tanh(slope * gate_pre * (1.0 + 0.044715 * square))
        share = 0.5 * (1.0 + bend)
        curved = gate_pre * share
        steep = share + 0.5 * gate_pre * (1.0 - bend * bend) * (
            slope * (1.0 + 3.0 * 0.044715 * square)
        )
        hidden_ref[rows] = (curved * up_pre).astype(bf16)
        gate_low = (hidden_grad * up_pre * steep).astype(bf16)
        up_low = (hidden_grad * curved).astype(bf16)
        gate_ref[rows], upper_ref[rows] = gate_low, up_low
        lows[0, step, rows], lows[1, step, rows] = gate_low, up_low
        return carried

    lax.fori_loop(0, 2 * half // tile, bend_rows, 0)

    @pl.when(step == shape.steps - 1)
    def finish():
        for rows, ref in ((slice(0, half), norm_own), (slice(half, 2 * half), norm_other)):
            total = None
            for side in range(2):
                for k in range(shape.steps):
                    more = lax.dot_general(
                        lows[side, k, rows], sides[side, k], across, preferred_element_type=f32
                    )
                    total = more if total is None else total + more
            ref[...] = total.astype(ref.dtype)


def hidden_back_kernel(
    shape,
    place_ref,
    normed_own,
    normed_other,
    down_own,
    down_other,
    hidden_ref,
    gate_ref,
    upper_ref,
    output_ref,
    *refs,
):
    panels = shape.panels
    down_w = refs[:panels]
    out_own, out_other = refs[panels : panels + 2]
    grad_refs, (turned, downs, outs) = refs[panels + 2 : -3], refs[-3:]
    step = pl.program_id(0)
    x, dp = place_ref[0], place_ref[1]
    half = normed_own.shape[0]

    @pl.when(step == 0)
    def gather():
        turned[:, :half] = normed_own[...].T
        turned[:, half:] = normed_other[...].T
        downs[:half] = down_own[...]
        downs[half:] = down_other[...]
        shape.store_output(grad_refs, output_ref, x)

    hidden = hidden_ref[...]
    down = jnp.concatenate([ref[...].reshape(PANEL, PANEL) for ref in down_w], axis=1)
    product = jnp.dot(hidden, down, preferred_element_type=f32)

    @pl.when(step == 0)
    def first_out():
        outs[...] = product

    @pl.when(step != 0)
    def later_out():
        outs[...] += product

    for side, ref in enumerate((gate_ref, upper_ref)):
        grad = jnp.dot(turned[...], ref[...], preferred_element_type=f32)
        shape.store_side(grad_refs, step, side, grad, x, dp)
    grad = jnp.dot(hidden.T, downs[...], preferred_element_type=f32)
    for p in range(panels):
        shape.store_down(grad_refs, step, p, grad[:, p * PANEL : (p + 1) * PANEL], x, dp)

    @pl.when(step == shape.steps - 1)
    def finish():
        out_own[...] = outs[:half]
        out_other[...] = outs[half:].astype(bf16)


class PackedWeights:
    def __init__(self, model, hidden_half, pieces):
        self.model, self.pieces = model, pieces
        self.side = model // pieces
        self.deep = hidden_half // pieces
        self.steps = hidden_half // PANEL
        self.panels = model // PANEL
        self.side_rows = 2 * self.steps * self.side
        self.grad_rows = self.side_rows + self.panels * self.deep

    def side_spec(self, shift):
        return pl.BlockSpec((self.pieces, self.side, PANEL), lambda j: (0, j + shift, 0))

    def down_specs(self):
        if self.pieces == 1:
            first = self.side_rows // PANEL
            each = self.deep // PANEL
            return [
                pl.BlockSpec((1, PANEL, PANEL), lambda j, p=p: (0, first + p * each + j, 0))
                for p in range(self.panels)
            ]
        first = self.side_rows // self.deep
        some = self.pieces // self.steps
        return [
            pl.BlockSpec((some, self.deep, PANEL), lambda j, p=p: (j, first + p, 0))
            for p in range(self.panels)
        ]

    def output_specs(self):
        first = self.grad_rows // self.side
        return [
            pl.BlockSpec((self.pieces, self.side, PANEL), lambda j, p=p: (0, first + p, 0))
            for p in range(self.panels)
        ]

    def grad_shapes(self):
        if self.pieces == 1:
            return [(1, self.grad_rows, PANEL)]
        side = self.steps * self.side
        first = (self.pieces // 2, side + self.deep + self.panels * 32, PANEL)
        second = (self.pieces // 2, side + (self.panels - 1) * self.deep, PANEL)
        return [first, first, second, second]

    def store_output(self, refs, output_ref, x):
        if self.pieces == 1:
            return
        owners, rows, model = output_ref.shape
        pairs = output_ref[...].reshape(owners // 2, 2, rows, model)
        start = self.steps * self.side + self.deep
        short = jnp.zeros((owners // 2, 32 - rows, PANEL), bf16)
        for k in range(2):

            @pl.when(x == k)
            def store():
                for p in range(self.panels):
                    lanes = slice(p * PANEL, (p + 1) * PANEL)
                    at = slice(start + 32 * p, start + 32 * (p + 1))
                    for slot, side in ((0, k), (1, 1 - k)):
                        refs[slot][:, at, :] = jnp.concatenate(
                            [pairs[:, side, :, lanes], short], axis=1
                        )

    def store_side(self, refs, step, side, value, x, dp):
        low = value.astype(bf16).reshape(self.pieces, self.side, PANEL)
        if self.pieces == 1:
            start = pl.multiple_of((step + side * self.steps) * self.side, 16)
            refs[0][:, pl.ds(start, self.side), :] = low
            return
        rows = pl.ds(pl.multiple_of(step * self.side, 16), self.side)
        half = self.pieces // 2
        if side:
            for k in range(2):

                @pl.when(dp == k)
                def store_upper():
                    refs[2][:, rows, :] = low[k * half : (k + 1) * half]
                    refs[3][:, rows, :] = low[(1 - k) * half : (2 - k) * half]
        else:
            pairs = low.reshape(half, 2, self.side, PANEL)
            for k in range(2):

                @pl.when(x == k)
                def store_gate():
                    refs[0][:, rows, :] = pairs[:, k]
                    refs[1][:, rows, :] = pairs[:, 1 - k]

    def store_down(self, refs, step, p, value, x, dp):
        low = value.astype(bf16)
        if self.pieces == 1:
            start = pl.multiple_of(self.side_rows + p * self.deep + step * PANEL, PANEL)
            refs[0][0, pl.ds(start, PANEL), :] = low
            return
        some = self.pieces // self.steps
        first = self.steps * self.side
        if p == 0:
            pairs = low.reshape(some // 2, 2, self.deep, PANEL)
            spots = pl.ds(step * (some // 2), some // 2)
            for k in range(2):

                @pl.when(x == k)
                def store_first():
                    refs[0][spots, first : first + self.deep, :] = pairs[:, k]
                    refs[1][spots, first : first + self.deep, :] = pairs[:, 1 - k]
        else:
            pieces = low.reshape(some, self.deep, PANEL)
            per_half = self.steps // 2
            spots = pl.ds((step % per_half) * some, some)
            first += (p - 1) * self.deep
            for slot, mine in ((2, step // per_half == dp), (3, step // per_half != dp)):

                @pl.when(mine)
                def store_other():
                    refs[slot][spots, first : first + self.deep, :] = pieces


def hidden_stage(normed, normed_other, down, down_other, everything, shape):
    half, model = normed.shape
    whole = pl.BlockSpec((half, model), lambda j: (0, 0))
    panel = pl.BlockSpec((2 * half, PANEL), lambda j: (0, j))
    units = shape.steps * PANEL
    return pl.pallas_call(
        functools.partial(hidden_kernel, shape),
        grid=(shape.steps,),
        in_specs=[whole] * 4
        + [shape.side_spec(0), shape.side_spec(shape.steps)]
        + shape.down_specs(),
        out_specs=[whole] * 2 + [panel] * 3,
        out_shape=[
            jax.ShapeDtypeStruct((half, model), f32),
            jax.ShapeDtypeStruct((half, model), bf16),
        ]
        + [jax.ShapeDtypeStruct((2 * half, units), bf16)] * 3,
        scratch_shapes=[
            pltpu.VMEM((2 * half, model), bf16),
            pltpu.VMEM((2 * half, model), bf16),
            pltpu.VMEM((2, shape.steps, 2 * half, PANEL), bf16),
            pltpu.VMEM((2, shape.steps, model, PANEL), bf16),
            pltpu.VMEM((3, 2 * half, PANEL), f32),
        ],
        compiler_params=vmem_limit(40),
        cost_estimate=pl.CostEstimate(
            flops=10 * 2 * half * model * units, bytes_accessed=12 * model * units, transcendentals=0
        ),
        name="hidden_stage",
    )(normed, normed_other, down, down_other, *[everything] * (2 + shape.panels))


def hidden_back(place, normed, normed_other, down, down_other, lows, output, everything, shape):
    half, model = normed.shape
    whole = pl.BlockSpec((half, model), lambda j, s: (0, 0))
    panel = pl.BlockSpec((2 * half, PANEL), lambda j, s: (0, j))
    with_place = lambda spec: pl.BlockSpec(
        spec.block_shape, lambda j, s, spec=spec: spec.index_map(j)
    )
    grads = shape.grad_shapes()
    units = shape.steps * PANEL
    return pl.pallas_call(
        functools.partial(hidden_back_kernel, shape),
        grid_spec=pltpu.PrefetchScalarGridSpec(
            num_scalar_prefetch=1,
            grid=(shape.steps,),
            in_specs=[whole] * 4
            + [panel] * 3
            + [pl.BlockSpec(output.shape, lambda j, s: (0, 0, 0))]
            + [with_place(spec) for spec in shape.down_specs()],
            out_specs=[whole] * 2 + [pl.BlockSpec(size, lambda j, s: (0, 0, 0)) for size in grads],
            scratch_shapes=[
                pltpu.VMEM((model, 2 * half), bf16),
                pltpu.VMEM((2 * half, model), bf16),
                pltpu.VMEM((2 * half, model), f32),
            ],
        ),
        out_shape=[
            jax.ShapeDtypeStruct((half, model), f32),
            jax.ShapeDtypeStruct((half, model), bf16),
        ]
        + [jax.ShapeDtypeStruct(size, bf16) for size in grads],
        compiler_params=vmem_limit(40),
        cost_estimate=pl.CostEstimate(
            flops=8 * 2 * half * model * units, bytes_accessed=12 * model * units, transcendentals=0
        ),
        name="hidden_back",
    )(
        place, normed, normed_other, down, down_other, *lows, output, *[everything] * shape.panels
    )


def output_back_kernel(norm_own, norm_other, residual_ref, down_ref, gain_ref, context_ref, *refs):
    weights = refs[:-4]
    rows_ref, gain_grad_ref, context_grad_ref, weight_grad_ref = refs[-4:]
    residual, gain = residual_ref[...], gain_ref[...]
    norm_grad = norm_own[...] + norm_other[...].astype(f32)
    scale = lax.rsqrt(jnp.mean(residual * residual, axis=-1, keepdims=True) + epsilon)
    gain_grad_ref[...] = jnp.sum(norm_grad * (residual * scale), axis=0, keepdims=True)
    weighted = norm_grad * gain
    inner = jnp.mean(weighted * residual, axis=-1, keepdims=True)
    rows_grad = (
        down_ref[...].astype(f32)
        + scale * weighted
        - residual * (scale * scale * scale * inner)
    )
    rows_ref[...] = rows_grad
    low = rows_grad.astype(bf16)
    blocks, part, local_rows = context_ref.shape
    seqs = rows_grad.shape[0] // local_rows
    groups = blocks // seqs
    model = residual.shape[1]
    for group in range(groups):
        columns = slice(group * part, (group + 1) * part)
        product = None
        for p, weight_ref in enumerate(weights):
            more = lax.dot_general(
                weight_ref[...].reshape(model, PANEL)[columns],
                low[:, p * PANEL : (p + 1) * PANEL],
                (((1,), (1,)), ((), ())),
                preferred_element_type=f32,
            )
            product = more if product is None else product + more
        turned = product.astype(bf16)
        total = None
        for seq in range(seqs):
            rows = slice(seq * local_rows, (seq + 1) * local_rows)
            context_grad_ref[seq * groups + group] = turned[:, rows]
            more = jnp.dot(
                context_ref[seq * groups + group], low[rows], preferred_element_type=f32
            )
            total = more if total is None else total + more
        weight_grad_ref[columns, :] = total.astype(bf16)


def output_back(norm_own, norm_other, residual, down, gain_row, context, everything, shape):
    rows, model = residual.shape
    whole = lambda array: pl.BlockSpec(array.shape, lambda i: (0,) * array.ndim)
    given = (norm_own, norm_other, residual, down, gain_row, context)
    out_shape = [
        jax.ShapeDtypeStruct((rows, model), f32),
        jax.ShapeDtypeStruct((1, model), f32),
        jax.ShapeDtypeStruct(context.shape, bf16),
        jax.ShapeDtypeStruct((model, model), bf16),
    ]
    return pl.pallas_call(
        output_back_kernel,
        grid=(1,),
        in_specs=[whole(array) for array in given] + shape.output_specs(),
        out_specs=[whole(array) for array in out_shape],
        out_shape=out_shape,
        compiler_params=vmem_limit(40),
        cost_estimate=pl.CostEstimate(
            flops=4 * rows * model * model, bytes_accessed=4 * model * model, transcendentals=0
        ),
        name="output_back",
    )(*given, *[everything] * shape.panels)


def owned_kernel(part, term_ref, *refs):
    groups, rows, columns = term_ref.shape
    extras = None
    for group in range(groups):
        term = term_ref[group].astype(f32)
        for k in range(3):
            refs[k][:, group * part : (group + 1) * part] = term[:, k * part : (k + 1) * part]
        more = term[:, 3 * part :]
        extras = more if extras is None else extras + more
    short = jnp.zeros((BLOCK - rows, BLOCK), f32)
    refs[3][...] = jnp.concatenate([extras, short], axis=0).T[:8]


def owned_stage(terms, model, part):
    groups, rows, columns = terms.shape
    whole = lambda array: pl.BlockSpec(array.shape, lambda i: (0,) * array.ndim)
    out_shape = [jax.ShapeDtypeStruct((rows, model), f32)] * 3 + [
        jax.ShapeDtypeStruct((8, BLOCK), f32)
    ]
    return pl.pallas_call(
        functools.partial(owned_kernel, part),
        grid=(1,),
        in_specs=[whole(terms)],
        out_specs=[whole(array) for array in out_shape],
        out_shape=out_shape,
        compiler_params=vmem_limit(16),
        cost_estimate=pl.CostEstimate(
            flops=terms.size, bytes_accessed=4 * terms.size, transcendentals=0
        ),
        name="owned_stage",
    )(terms)


def swap(value, axis):
    return lax.ppermute(value, axis, [(0, 1), (1, 0)])


def after(value, gate):
    return lax.optimization_barrier((value, gate))[0]


def pick(pair, index, axis):
    return lax.dynamic_index_in_dim(pair, index, axis, keepdims=False)


def in_order(mine, theirs, index, axis):
    return jnp.where(
        index == 0, jnp.stack([mine, theirs], axis), jnp.stack([theirs, mine], axis)
    )


def plus(mine, came):
    return (mine.astype(f32) + came.astype(f32)).astype(bf16)


def halve(value, index, name, axis):
    return plus(pick(value, index, axis), swap(pick(value, 1 - index, axis), name))


def columns_in_panels(weight):
    rows, cols = weight.shape
    return jnp.transpose(weight.reshape(rows, cols // PANEL, PANEL), (1, 0, 2)).reshape(
        rows * cols // PANEL, PANEL
    )


def own_half(weight, each, c):
    rows, cols = weight.shape
    return pick(weight.reshape(rows, cols // (2 * each), 2, each), c, 2).reshape(rows, cols // 2)


def body(
    inputs,
    w_query,
    w_key,
    w_value,
    w_output,
    w_gate,
    w_upper,
    w_down,
    gain_one,
    gain_two,
    bias_table,
    buckets,
    cotangent,
    sizes,
):
    along_dp, along_a = sizes
    dp, a, x, c = (lax.axis_index(name) for name in ("dp", "a", "x", "c"))
    zh, zl = lax.axis_index("zh"), lax.axis_index("zl")
    z, group = 2 * zh + zl, 2 * zl + x
    depth = 4
    seqs, local_rows, model = inputs.shape
    length = buckets.shape[0] // 2 + 1
    width = model // H
    heads = H // GROUPS
    part = heads * width
    weight_rows, hidden_units = w_gate.shape
    each = w_down.shape[0]
    own_count = depth * 2 * local_rows
    token_count = seqs * local_rows

    near = in_order(pick(inputs, zh, 0), swap(pick(inputs, 1 - zh, 0), "zh"), zh, 0)
    column = in_order(near, swap(near, "zl"), zl, 1)
    tokens_own = in_order(column, swap(column, "x"), x, 2).reshape(own_count, model)

    blocks = [
        jnp.transpose(w.reshape(weight_rows, GROUPS, part), (1, 0, 2))
        for w in (w_query, w_key, w_value)
    ]
    table_column = jnp.pad(bias_table, (0, weight_rows - bias_table.shape[0]))
    extra = jnp.stack([gain_one, gain_two, table_column], axis=1)
    extra = jnp.pad(extra, ((0, 0), (0, BLOCK - extra.shape[1])))
    extra = jnp.broadcast_to(extra[None], (GROUPS, weight_rows, BLOCK))
    columns = lax.all_to_all(
        jnp.concatenate([*blocks, extra], axis=2), ("zl", "x"), 0, 0, tiled=True
    )
    columns = in_order(columns, swap(columns, "zh"), zh, 0)
    if along_a > 1:
        columns = lax.all_gather(columns, "a", axis=0)
    columns = in_order(columns, swap(columns, "dp"), dp, 0)
    columns = in_order(columns, swap(columns, "c"), c, columns.ndim - 2)
    columns = columns.reshape(model, 3 * part + BLOCK)
    gain_a = columns[:, 3 * part].astype(f32).reshape(1, model)
    gain_b = columns[:, 3 * part + 1].astype(f32).reshape(1, model)
    table = columns[:, 3 * part + 2].reshape(model // weight_rows, weight_rows)
    table = table[:, : bias_table.shape[0]].reshape(BUCKETS, H)
    padded = jnp.pad(buckets, (0, 1), constant_values=BLOCK)
    hot = (padded[:, None] == jnp.arange(BLOCK, dtype=jnp.int32)[None, :]).astype(bf16)
    own_table = lax.dynamic_slice_in_dim(table, group * heads, heads, 1)
    own_table = jnp.pad(own_table, ((0, BLOCK - BUCKETS), (0, 0)))
    ahead = jnp.pad(buckets, (1, 0), constant_values=BLOCK)
    hot_ahead = (ahead[None, :] == jnp.arange(BLOCK, dtype=jnp.int32)[:, None]).astype(bf16)
    vectors = lax.dot_general(
        own_table, hot_ahead, (((0,), (0,)), ((), ())), preferred_element_type=f32
    ).reshape(heads, 1, 2 * length)

    if along_a == 1:
        sent = [own_half(w, each, 1 - c) for w in (w_gate, w_upper)] + [w_output]
        came = swap(jnp.concatenate(sent, axis=1), "c")
        kept = [own_half(w, each, c) for w in (w_gate, w_upper)] + [w_output]
        both = in_order(jnp.concatenate(kept, axis=1), came, c, 0).reshape(2 * weight_rows, -1)
        packed = jnp.concatenate(
            [
                columns_in_panels(both[:, :hidden_units]),
                columns_in_panels(w_down),
                columns_in_panels(both[:, hidden_units:]),
            ],
            axis=0,
        )
        pieces = along_dp * depth * 2
        everything = lax.all_gather(packed, chips, axis=0, tiled=True)
        everything = everything.reshape(pieces, packed.shape[0], PANEL)
    else:
        pieces = 1
        gate_all, upper_all, down_all, output_all = (
            lax.all_gather(w, everyone, axis=0, tiled=True)
            for w in (w_gate, w_upper, w_down, w_output)
        )
        down_half = pick(down_all.reshape(-1, 2, each, model), c, 1).reshape(-1, model)
        everything = jnp.concatenate(
            [
                columns_in_panels(own_half(gate_all, each, c)),
                columns_in_panels(own_half(upper_all, each, c)),
                columns_in_panels(down_half),
                columns_in_panels(output_all),
            ],
            axis=0,
        )[None]
    shape = PackedWeights(model, hidden_units // 2, pieces)

    if along_a > 1:
        tokens_all = lax.all_gather(tokens_own, "a", axis=0, tiled=True)
    else:
        tokens_all = tokens_own
    normed, query, own = project(tokens_all, gain_a, columns, heads, width)
    if along_a > 1:
        query = lax.dynamic_slice_in_dim(query, a * own_count, own_count, 1)
        normed = lax.dynamic_slice_in_dim(normed, a * own_count, own_count, 0)
    other = swap(own, "c")
    biases = skew(vectors)
    place = jnp.stack([a * (own_count // BLOCK), c]).astype(jnp.int32)
    place = after(place, hot)
    context_own, probs, kept, inverse = attend(place, query, own, other, biases)
    owners = ("zh", "zl", "x")
    context = lax.all_to_all(context_own, owners, 0, 0, tiled=True)

    down_grad = cotangent.reshape(token_count, model)
    down_other = swap(down_grad, "c")
    residual, second = output_stage(context, inputs, gain_b, everything, shape)
    second_other = swap(second, "c")
    sides_place = jnp.stack([x, dp]).astype(jnp.int32)
    norm_own, norm_other, *lows = hidden_stage(
        second, second_other, down_grad, down_other, everything, shape
    )
    norm_came = swap(norm_other, "c")
    residual_grad, gain_b_grad, context_sent, output_grad = output_back(
        norm_own, norm_came, residual, down_grad, gain_b, context, everything, shape
    )
    *lows, output_grad, context_sent = lax.optimization_barrier(
        (*lows, output_grad, context_sent)
    )
    context_grad = lax.all_to_all(context_sent, owners, 0, 0, tiled=True)
    output_terms = halve(
        output_grad.reshape(model // (2 * weight_rows), CORES, weight_rows, model), c, "c", 1
    )
    out_own, out_other, *big_grads = hidden_back(
        sides_place,
        second,
        second_other,
        down_grad,
        down_other,
        lows,
        output_terms,
        everything,
        shape,
    )
    out_came = swap(out_other, "c")
    outputs = (residual + out_own + out_came.astype(f32)).astype(bf16)

    if along_a == 1:
        first_terms, first_sent, second_terms, second_sent = big_grads
        first_came = swap(first_sent, "x")
        second_came = swap(second_sent, "dp")
    query_grad, own_grad, other_grad, bucket_sums = attend_back(
        place, context_grad, kept, inverse, probs, query, own, other, hot
    )
    if along_a > 1:
        own_grad, other_grad = (
            lax.psum_scatter(value, "a", scatter_dimension=2, tiled=True)
            for value in (own_grad, other_grad)
        )
    else:
        first_came, second_came, query_grad, own_grad, other_grad, bucket_sums = (
            lax.optimization_barrier(
                (first_came, second_came, query_grad, own_grad, other_grad, bucket_sums)
            )
        )
        first_terms = plus(first_terms, first_came).reshape(along_dp, depth, -1, PANEL)
        second_terms = plus(second_terms, second_came).reshape(depth, 2, -1, PANEL)
        first_terms, second_terms, query_grad = lax.optimization_barrier(
            (first_terms, second_terms, query_grad)
        )
        first_came = swap(pick(first_terms, 1 - dp, 0), "dp")
        second_came = swap(pick(second_terms, 1 - x, 1), "x")
    came = swap(other_grad, "c")

    per_owner = bias_table.shape[0]
    bucket_sums = bucket_sums[:, 0, :BUCKETS]
    spot = jnp.arange(model, dtype=jnp.int32)
    entry = spot // weight_rows * per_owner + spot % weight_rows
    entry = jnp.where(spot % weight_rows < per_owner, entry, -1)
    spread = (entry[None, :] // H == jnp.arange(BUCKETS, dtype=jnp.int32)[:, None]).astype(bf16)
    table_rows = jnp.dot(bucket_sums.astype(bf16), spread, preferred_element_type=f32)
    own_heads = group * heads + jnp.arange(heads, dtype=jnp.int32)
    table_row = jnp.sum(
        jnp.where(entry[None, :] % H == own_heads[:, None], table_rows, 0.0), axis=0
    )
    extra = jnp.stack(
        [jnp.zeros((model,), f32), gain_b_grad.reshape(model), table_row, gain_a.reshape(model)]
        + [jnp.zeros((model,), f32)] * 4
    )
    core_place = jnp.stack([x, c]).astype(jnp.int32)
    *rows_grads, mixed, sent_c = project_back(
        core_place, query_grad, own_grad, came, normed, columns, extra, weight_rows
    )
    if along_a == 1:
        first_came, second_came = (
            after(value, sent_c) for value in (first_came, second_came)
        )

    by_owner = (along_dp, along_a, 2, GROUPS, weight_rows, mixed.shape[2])
    mixed, sent_c = mixed.reshape(by_owner), sent_c.reshape(by_owner)
    came_x = swap(rows_grads[1], "x")
    mixed = plus(mixed, swap(sent_c, "c"))
    if along_a == 1:
        terms = jnp.concatenate(
            [
                plus(pick(first_terms, dp, 0), first_came),
                plus(pick(second_terms, x, 1), second_came),
            ],
            axis=1,
        )
        terms = terms.reshape(2, 2, -1, PANEL)
        column_came = swap(pick(terms, 1 - zl, 1), "zl")
    came_dp = swap(pick(mixed, 1 - dp, 0), "dp")
    mixed = plus(pick(mixed, dp, 0), came_dp)
    came_zh = swap(pick(mixed, 1 - zh, 1), "zh")
    share = plus(rows_grads[0], came_x).reshape(2, 2, local_rows, model)
    share, sent = pick(share, zl, 1), pick(share, 1 - zl, 1)
    came_zl = swap(sent, "zl")
    if along_a == 1:
        column_came = after(column_came, sent)
        terms = plus(pick(terms, zl, 1), column_came)
        sent = pick(terms, 1 - zh, 0)
        column_came = swap(sent, "zh")
    share = plus(share, after(came_zl, sent))
    rows_own, sent = pick(share, zh, 0), pick(share, 1 - zh, 0)
    rows_came = swap(sent, "zh")
    came_zh = after(came_zh, sent)
    mixed = plus(pick(mixed, zh, 1), came_zh)
    if along_a > 1:
        mixed = lax.psum_scatter(mixed, "a", scatter_dimension=0, tiled=True)
    terms_owned = lax.all_to_all(mixed[0], ("zl", "x"), 0, 0, tiled=True)
    input_grad = rows_stage(
        zh.astype(jnp.int32)[None], inputs, residual_grad, gain_a, rows_own, rows_came
    )

    if along_a == 1:
        column_came = after(column_came, mixed)
        total = pick(terms, zh, 0).astype(f32) + column_came.astype(f32)
        side, deep = shape.steps * shape.side, shape.deep
        rest = total[side + deep + shape.panels * 32 :]
        output_owned = jnp.transpose(
            total[side + deep : side + deep + shape.panels * 32].reshape(shape.panels, 32, PANEL)[
                :, :weight_rows
            ],
            (1, 0, 2),
        ).reshape(weight_rows, model)
        sides = jnp.concatenate([total[:side], rest[:side]], axis=0)
        sides = sides.astype(bf16).reshape(-1, 2, weight_rows, PANEL)
        sides = in_order(pick(sides, c, 1), swap(pick(sides, 1 - c, 1), "c"), c, 0)
        sides = sides.reshape(2, 2, shape.steps, weight_rows, PANEL)
        sides = jnp.transpose(
            sides.reshape(2, 2, shape.steps, weight_rows, PANEL // each, each), (1, 3, 2, 4, 0, 5)
        ).reshape(2, weight_rows, hidden_units)
        gate_owned, upper_owned = sides[0].astype(f32), sides[1].astype(f32)
        down_owned = jnp.transpose(
            jnp.concatenate([total[side : side + deep], rest[side:]], axis=0).reshape(
                shape.panels, each, PANEL
            ),
            (1, 0, 2),
        ).reshape(each, model)
    else:
        side = shape.steps * model
        gate_half, upper_half = (
            jnp.transpose(
                big_grads[0][0, k * side : (k + 1) * side].reshape(shape.steps, model, PANEL),
                (1, 0, 2),
            ).reshape(model, -1, 1, each)
            for k in range(2)
        )
        down_half = jnp.transpose(
            big_grads[0][0, 2 * side :].reshape(shape.panels, -1, PANEL), (1, 0, 2)
        ).reshape(-1, 1, each, model)
        zero = jnp.zeros_like
        output_owned = lax.psum_scatter(
            in_order(output_terms, zero(output_terms), c, 1).reshape(model, model),
            everyone,
            scatter_dimension=0,
            tiled=True,
        ).astype(f32)
        gate_owned, upper_owned = (
            lax.psum_scatter(
                in_order(half, zero(half), c, 2).reshape(model, hidden_units),
                everyone,
                scatter_dimension=0,
                tiled=True,
            ).astype(f32)
            for half in (gate_half, upper_half)
        )
        down_owned = lax.psum_scatter(
            in_order(down_half, zero(down_half), c, 1).reshape(hidden_units, model),
            everyone,
            scatter_dimension=0,
            tiled=True,
        ).astype(f32)

    *owned, extras = owned_stage(terms_owned, model, part)
    return (
        outputs.reshape(seqs, local_rows, model),
        input_grad,
        *owned,
        output_owned,
        gate_owned,
        upper_owned,
        down_owned,
        extras[0, :weight_rows],
        extras[1, :weight_rows],
        extras[2, :per_owner],
    )


def solution(mesh):
    along_dp, along_ctx = mesh.shape["dp"], mesh.shape["ctx"]
    along_a = along_ctx // (4 * 2 * CORES)
    fine = Mesh(mesh.devices.reshape(along_dp, along_a, 2, 2, 2, CORES), everyone)
    rows = P("dp", ("a", "zh", "zl", "x", "c"), None)
    owned = P(everyone, None)
    vector = P(everyone)
    in_specs = (rows, *[owned] * 7, *[vector] * 3, P(), rows)
    out_specs = (rows, rows, *[owned] * 7, *[vector] * 3)
    return jax.shard_map(
        functools.partial(body, sizes=(along_dp, along_a)),
        mesh=fine,
        in_specs=in_specs,
        out_specs=out_specs,
        check_vma=False,
    )
```

```python
import functools

import jax
import jax.numpy as jnp
from jax import lax
from jax.experimental import pallas as pl
from jax.experimental.pallas import tpu as pltpu
from jax.sharding import Mesh
from jax.sharding import PartitionSpec as P

H = 12
BUCKETS = 32
GROUPS = 4
CORES = 2
BLOCK = 128

epsilon = 1e-06
exactly = lax.Precision.HIGHEST
bf16 = jnp.bfloat16
f32 = jnp.float32
everyone = ("dp", "a", "zh", "zl", "x", "c")
chips = ("dp", "zh", "zl", "x")
PANEL = 256


def rms_scale(values, gain_vec):
    return (
        values * lax.rsqrt(jnp.mean(values * values, axis=-1, keepdims=True) + epsilon) * gain_vec
    )


def vmem_limit(mib):
    return pltpu.CompilerParams(vmem_limit_bytes=mib * 1024 * 1024)


def project_kernel(heads, token_ref, gain_ref, weight_ref, normed_ref, query_ref, pair_ref):
    rows = token_ref[...].astype(f32)
    scale = lax.rsqrt(jnp.mean(rows * rows, axis=-1, keepdims=True) + epsilon)
    normed = (rows * scale * gain_ref[...]).astype(bf16)
    normed_ref[...] = normed
    width = query_ref.shape[2]
    mixed = jnp.dot(
        normed, weight_ref[:, : 3 * heads * width], preferred_element_type=f32
    ).astype(bf16)
    for k in range(heads):
        query_ref[k] = mixed[:, k * width : (k + 1) * width]
        for side in range(2):
            first = (heads * (side + 1) + k) * width
            pair_ref[k, :, side * width : (side + 1) * width] = mixed[:, first : first + width]


def project(tokens, gain_row, weight, heads, width):
    rows, model = tokens.shape
    tile = 256
    return pl.pallas_call(
        functools.partial(project_kernel, heads),
        grid=(rows // tile,),
        in_specs=[
            pl.BlockSpec((tile, model), lambda i: (i, 0)),
            pl.BlockSpec((1, model), lambda i: (0, 0)),
            pl.BlockSpec(weight.shape, lambda i: (0, 0)),
        ],
        out_specs=[
            pl.BlockSpec((tile, model), lambda i: (i, 0)),
            pl.BlockSpec((heads, tile, width), lambda i: (0, i, 0)),
            pl.BlockSpec((heads, tile, 2 * width), lambda i: (0, i, 0)),
        ],
        out_shape=[
            jax.ShapeDtypeStruct((rows, model), bf16),
            jax.ShapeDtypeStruct((heads, rows, width), bf16),
            jax.ShapeDtypeStruct((heads, rows, 2 * width), bf16),
        ],
        compiler_params=vmem_limit(12),
        cost_estimate=pl.CostEstimate(
            flops=2 * rows * model * 3 * heads * width,
            bytes_accessed=8 * rows * model,
            transcendentals=0,
        ),
        name="project",
    )(tokens, gain_row, weight)


def skew_kernel(vector_ref, table_ref, row_scratch):
    span = vector_ref.shape[-1]
    for r in range(8):
        row_scratch[r : r + 1, :] = pltpu.roll(vector_ref[0], r, 1) if r else vector_ref[0]
    eight = row_scratch[...]
    rows = []
    for group in range(BLOCK // 8):
        turned = pltpu.roll(eight, 8 * group, 1) if group else eight
        rows.append(turned[:, BLOCK:span])
    for pair in range(BLOCK // 16):
        both = jnp.concatenate(rows[2 * pair : 2 * pair + 2], axis=0)
        table_ref[0, 16 * pair : 16 * pair + 16, :] = both.astype(bf16)


def skew(vectors):
    heads, unused, span = vectors.shape
    return pl.pallas_call(
        skew_kernel,
        grid=(heads,),
        in_specs=[pl.BlockSpec((1, 1, span), lambda h: (h, 0, 0))],
        out_specs=pl.BlockSpec((1, BLOCK, span - BLOCK), lambda h: (h, 0, 0)),
        out_shape=jax.ShapeDtypeStruct((heads, BLOCK, span - BLOCK), bf16),
        scratch_shapes=[pltpu.VMEM((8, span), f32)],
        compiler_params=vmem_limit(10),
        cost_estimate=pl.CostEstimate(
            flops=0, bytes_accessed=2 * heads * BLOCK * span, transcendentals=0
        ),
        name="skew",
    )(vectors)


def interleave(keys, values, own_ref, other_ref, parity, fill):
    width = keys.shape[1]
    for k in range(own_ref.shape[1] // BLOCK):
        rows = slice(k * BLOCK, (k + 1) * BLOCK)
        for source, spot in ((own_ref, parity), (other_ref, 1 - parity)):
            into = pl.ds(pl.multiple_of((2 * k + spot) * BLOCK, BLOCK), BLOCK)
            keys[into, :] = source[0, rows, :width]
            values[into, :width] = source[0, rows, width:]
            if fill:
                values[into, width:] = jnp.ones((BLOCK, width), bf16)


def table_starts(tile, step, first_block, parity, blocks):
    starts = []
    for sub in range(tile // BLOCK):
        block = 2 * (first_block + step * (tile // BLOCK) + sub) + parity
        starts.append((blocks - 1 - block) * BLOCK)
    return starts


def attend_kernel(
    tile,
    chunk,
    place_ref,
    query_ref,
    pair_own,
    pair_other,
    table,
    context_ref,
    probs_ref,
    kept_ref,
    inverse_ref,
    keys,
    values,
    scores,
):
    head, step = pl.program_id(0), pl.program_id(1)
    first_block, parity = place_ref[0], place_ref[1]
    key_count, width = keys.shape
    blocks = key_count // BLOCK
    subs = tile // BLOCK
    table = table.at[0]

    @pl.when(step == 0)
    def prepare():
        interleave(keys, values, pair_own, pair_other, parity, True)

    query = query_ref[0]
    starts = table_starts(tile, step, first_block, parity, blocks)
    lane_max = None
    for part in range(key_count // chunk):
        cols = slice(part * chunk, (part + 1) * chunk)
        product = lax.dot_general(
            query, keys[cols, :], (((1,), (1,)), ((), ())), preferred_element_type=f32
        )
        pieces = []
        for sub in range(subs):
            rows = slice(sub * BLOCK, (sub + 1) * BLOCK)
            offset = pl.multiple_of(starts[sub] + part * chunk, BLOCK)
            piece = product[rows] + table[:, pl.ds(offset, chunk)].astype(f32)
            scores[rows, cols] = piece
            for k in range(chunk // BLOCK):
                lanes = piece[:, k * BLOCK : (k + 1) * BLOCK]
                top = lanes if k == 0 else jnp.maximum(top, lanes)
            pieces.append(top)
        pieces = jnp.concatenate(pieces, axis=0)
        lane_max = pieces if lane_max is None else jnp.maximum(lane_max, pieces)
    row_max = jnp.max(lane_max, axis=-1, keepdims=True)
    total = jnp.zeros((tile, 2 * width), f32)
    for part in range(key_count // chunk):
        cols = slice(part * chunk, (part + 1) * chunk)
        low = jnp.exp(scores[:, cols] - row_max).astype(bf16)
        probs_ref[0, :, cols] = low
        total = total + jnp.dot(low, values[cols, :], preferred_element_type=f32)
    inverse = 1.0 / total[:, width:]
    value = total[:, :width] * inverse
    kept_ref[0, :, :width] = value
    kept_ref[0, :, width:] = inverse
    turned = value.T.astype(bf16)
    inverse_turned = inverse.T
    for sub in range(subs):
        lanes = slice(sub * BLOCK, (sub + 1) * BLOCK)
        rows = pl.ds(pl.multiple_of(head * width, width), width)
        context_ref[step * subs + sub, rows, :] = turned[:, lanes]
        inverse_ref[0, sub] = inverse_turned[0:1, lanes]


def attend(place, query, own, other, table):
    heads, rows, width = query.shape
    own_rows = own.shape[1]
    key_count = 2 * own_rows
    tile, chunk = 256, 512
    pairs = pl.BlockSpec((1, own_rows, 2 * width), lambda h, i, s: (h, 0, 0))
    return pl.pallas_call(
        functools.partial(attend_kernel, tile, chunk),
        grid_spec=pltpu.PrefetchScalarGridSpec(
            num_scalar_prefetch=1,
            grid=(heads, rows // tile),
            in_specs=[
                pl.BlockSpec((1, tile, width), lambda h, i, s: (h, i, 0)),
                pairs,
                pairs,
                pl.BlockSpec((1, *table.shape[1:]), lambda h, i, s: (h, 0, 0)),
            ],
            out_specs=[
                pl.BlockSpec((rows // BLOCK, heads * width, BLOCK), lambda h, i, s: (0, 0, 0)),
                pl.BlockSpec((1, tile, key_count), lambda h, i, s: (h, i, 0)),
                pl.BlockSpec((1, tile, 2 * width), lambda h, i, s: (h, i, 0)),
                pl.BlockSpec((1, tile // BLOCK, 1, BLOCK), lambda h, i, s: (h, i, 0, 0)),
            ],
            scratch_shapes=[
                pltpu.VMEM((key_count, width), bf16),
                pltpu.VMEM((key_count, 2 * width), bf16),
                pltpu.VMEM((tile, key_count), f32),
            ],
        ),
        out_shape=[
            jax.ShapeDtypeStruct((rows // BLOCK, heads * width, BLOCK), bf16),
            jax.ShapeDtypeStruct((heads, rows, key_count), bf16),
            jax.ShapeDtypeStruct((heads, rows, 2 * width), f32),
            jax.ShapeDtypeStruct((heads, rows // BLOCK, 1, BLOCK), f32),
        ],
        compiler_params=vmem_limit(54),
        cost_estimate=pl.CostEstimate(
            flops=16 * heads * rows * key_count * width,
            bytes_accessed=2 * heads * rows * key_count,
            transcendentals=heads * rows * key_count,
        ),
        name="attend",
    )(place, query, own, other, table)


def attend_back_kernel(
    tile,
    chunk,
    place_ref,
    grad_ref,
    kept_ref,
    inverse_ref,
    probs_ref,
    query_ref,
    pair_own,
    pair_other,
    hot_ref,
    query_grad_ref,
    own_grad_ref,
    other_grad_ref,
    offset_ref,
    keys,
    values,
    diagonals,
    key_sums,
    value_sums,
):
    step = pl.program_id(1)
    first_block, parity = place_ref[0], place_ref[1]
    key_count, width = keys.shape
    blocks = key_count // BLOCK
    subs = tile // BLOCK

    @pl.when(step == 0)
    def prepare():
        interleave(keys, values, pair_own, pair_other, parity, False)
        diagonals[...] = jnp.zeros_like(diagonals)
        key_sums[...] = jnp.zeros_like(key_sums)
        value_sums[...] = jnp.zeros_like(value_sums)

    turned = jnp.concatenate(
        [grad_ref[sub].astype(f32) * inverse_ref[0, sub] for sub in range(subs)], axis=1
    )
    grad_turned = turned.astype(bf16)
    scaled = grad_turned.astype(f32).T
    delta = jnp.sum(scaled * kept_ref[0, :, :width], axis=-1, keepdims=True)
    scaled = scaled.astype(bf16)
    query_turned = query_ref[0].astype(f32).T.astype(bf16)
    starts = table_starts(tile, step, first_block, parity, blocks)
    query_grad = jnp.zeros((tile, width), f32)
    for part in range(key_count // chunk):
        cols = slice(part * chunk, (part + 1) * chunk)
        prob_grad = lax.dot_general(
            scaled, values[cols, :], (((1,), (1,)), ((), ())), preferred_element_type=f32
        )
        low = probs_ref[0, :, cols]
        score_grad = low.astype(f32) * (prob_grad - delta)
        for sub in range(subs):
            rows = slice(sub * BLOCK, (sub + 1) * BLOCK)
            offset = pl.multiple_of(starts[sub] + part * chunk, BLOCK)
            diagonals[:, pl.ds(offset, chunk)] += score_grad[rows]
        score_low = score_grad.astype(bf16)
        query_grad = query_grad + jnp.dot(score_low, keys[cols, :], preferred_element_type=f32)
        key_sums[:, cols] += jnp.dot(query_turned, score_low, preferred_element_type=f32)
        value_sums[:, cols] += jnp.dot(grad_turned, low, preferred_element_type=f32)
    query_grad_ref[0] = query_grad.astype(bf16)

    @pl.when(step == pl.num_programs(1) - 1)
    def finish():
        span = diagonals.shape[1]
        eight = diagonals[0:8, :]
        for group in range(1, BLOCK // 8):
            eight = eight + pltpu.roll(
                diagonals[8 * group : 8 * group + 8, :], span - 8 * group, 1
            )
        total = eight[0:1, :]
        for r in range(1, 8):
            total = total + pltpu.roll(eight[r : r + 1, :], span - r, 1)
        total = pltpu.roll(total, BLOCK - 1, 1)
        bucket_sums = None
        for unused in range(3):
            low = total.astype(bf16)
            total = total - low.astype(f32)
            more = jnp.dot(low, hot_ref[...], preferred_element_type=f32)
            bucket_sums = more if bucket_sums is None else bucket_sums + more
        offset_ref[0] = bucket_sums
        for sums, rows in ((key_sums, slice(0, width)), (value_sums, slice(width, 2 * width))):
            for b in range(blocks // 2):
                near = pl.multiple_of((2 * b + parity) * BLOCK, BLOCK)
                far = pl.multiple_of((2 * b + 1 - parity) * BLOCK, BLOCK)
                lanes = slice(b * BLOCK, (b + 1) * BLOCK)
                own_grad_ref[0, rows, lanes] = sums[:, pl.ds(near, BLOCK)].astype(bf16)
                other_grad_ref[0, rows, lanes] = sums[:, pl.ds(far, BLOCK)].astype(bf16)


def attend_back(place, grad, kept, inverse, probs, query, own, other, hot):
    count, rows, width = query.shape
    own_rows = own.shape[1]
    key_count = 2 * own_rows
    span = key_count * 2
    tile, chunk = 512, 512
    pairs = pl.BlockSpec((1, own_rows, 2 * width), lambda h, i, s: (h, 0, 0))
    return pl.pallas_call(
        functools.partial(attend_back_kernel, tile, chunk),
        grid_spec=pltpu.PrefetchScalarGridSpec(
            num_scalar_prefetch=1,
            grid=(count, rows // tile),
            in_specs=[
                pl.BlockSpec(
                    (tile // BLOCK, width, BLOCK), lambda h, i, s: (i, h, 0)
                ),
                pl.BlockSpec((1, tile, 2 * width), lambda h, i, s: (h, i, 0)),
                pl.BlockSpec((1, tile // BLOCK, 1, BLOCK), lambda h, i, s: (h, i, 0, 0)),
                pl.BlockSpec((1, tile, key_count), lambda h, i, s: (h, i, 0)),
                pl.BlockSpec((1, tile, width), lambda h, i, s: (h, i, 0)),
                pairs,
                pairs,
                pl.BlockSpec(hot.shape, lambda h, i, s: (0, 0)),
            ],
            out_specs=[
                pl.BlockSpec((1, tile, width), lambda h, i, s: (h, i, 0)),
                pl.BlockSpec((1, 2 * width, own_rows), lambda h, i, s: (h, 0, 0)),
                pl.BlockSpec((1, 2 * width, own_rows), lambda h, i, s: (h, 0, 0)),
                pl.BlockSpec((1, 1, hot.shape[1]), lambda h, i, s: (h, 0, 0)),
            ],
            scratch_shapes=[
                pltpu.VMEM((key_count, width), bf16),
                pltpu.VMEM((key_count, width), bf16),
                pltpu.VMEM((BLOCK, span), f32),
                pltpu.VMEM((width, key_count), f32),
                pltpu.VMEM((width, key_count), f32),
            ],
        ),
        out_shape=[
            jax.ShapeDtypeStruct((count, rows, width), bf16),
            jax.ShapeDtypeStruct((count, 2 * width, own_rows), bf16),
            jax.ShapeDtypeStruct((count, 2 * width, own_rows), bf16),
            jax.ShapeDtypeStruct((count, 1, hot.shape[1]), f32),
        ],
        compiler_params=vmem_limit(54),
        cost_estimate=pl.CostEstimate(
            flops=32 * count * rows * key_count * width,
            bytes_accessed=2 * count * rows * key_count,
            transcendentals=0,
        ),
        name="attend_back",
    )(place, grad, kept, inverse, probs, query, own, other, hot)


def project_back_kernel(
    place_ref,
    normed_ref,
    weight_ref,
    extra_ref,
    query_grad_ref,
    own_ref,
    came_ref,
    kept_rows,
    sent_rows,
    kept_ref,
    sent_ref,
    turned,
    sums,
    gains,
):
    step = pl.program_id(0)
    heads, unused, width = query_grad_ref.shape
    part = heads * width
    for head in range(heads):
        turned[head * width : (head + 1) * width, :] = query_grad_ref[head].T
        both = (own_ref[head].astype(f32) + came_ref[head].astype(f32)).astype(bf16)
        for side in range(2):
            at = part * (side + 1) + head * width
            turned[at : at + width, :] = both[side * width : (side + 1) * width]
    grads = turned[...]
    normed_grad = lax.dot_general(
        grads,
        weight_ref[:, : 3 * part],
        (((0,), (1,)), ((), ())),
        preferred_element_type=f32,
    )
    low = normed_grad.astype(bf16)
    half = low.shape[0] // 2
    for k in range(2):

        @pl.when(place_ref[0] == k)
        def store():
            kept_rows[0] = low[k * half : (k + 1) * half]
            sent_rows[0] = low[(1 - k) * half : (2 - k) * half]

    gain = jnp.sum(normed_grad * normed_ref[...].astype(f32), axis=0, keepdims=True)
    update = jnp.dot(grads, normed_ref[...], preferred_element_type=f32)

    @pl.when(step == 0)
    def start():
        sums[...] = update
        gains[...] = extra_ref[...]

    @pl.when(step != 0)
    def more():
        sums[...] += update

    gains[0:1, :] += gain / extra_ref[3:4, :]

    @pl.when(step == pl.num_programs(0) - 1)
    def finish():
        update = sums[...].T
        model = update.shape[0]
        extras = jnp.concatenate(
            [gains[...], jnp.zeros((BLOCK - gains.shape[0], model), f32)], axis=0
        ).T
        owners, rows, columns = kept_ref.shape
        for k in range(2):

            @pl.when(place_ref[1] == k)
            def pack():
                for owner in range(owners):
                    for ref, core in ((kept_ref, k), (sent_ref, 1 - k)):
                        at = slice((2 * owner + core) * rows, (2 * owner + core + 1) * rows)
                        ref[owner, :, : 3 * part] = update[at].astype(bf16)
                        ref[owner, :, 3 * part :] = extras[at].astype(bf16)


def project_back(place, query_grad, own, came, normed, weight, extra, weight_rows):
    rows, model = normed.shape
    heads, unused, width = query_grad.shape
    part = heads * width
    tile = 2 * BLOCK
    steps = rows // tile
    whole = lambda shape: pl.BlockSpec(shape, lambda i, s: (0, 0))
    pairs = pl.BlockSpec((heads, 2 * width, tile), lambda i, s: (0, 0, i))
    share = pl.BlockSpec((1, BLOCK, model), lambda i, s: (i, 0, 0))
    packed = (model // (2 * weight_rows), weight_rows, 3 * part + BLOCK)
    return pl.pallas_call(
        project_back_kernel,
        grid_spec=pltpu.PrefetchScalarGridSpec(
            num_scalar_prefetch=1,
            grid=(steps,),
            in_specs=[
                pl.BlockSpec((tile, model), lambda i, s: (i, 0)),
                whole(weight.shape),
                whole(extra.shape),
                pl.BlockSpec((heads, tile, width), lambda i, s: (0, i, 0)),
                pairs,
                pairs,
            ],
            out_specs=[share] * 2 + [pl.BlockSpec(packed, lambda i, s: (0, 0, 0))] * 2,
            scratch_shapes=[
                pltpu.VMEM((3 * part, tile), bf16),
                pltpu.VMEM((3 * part, model), f32),
                pltpu.VMEM(extra.shape, f32),
            ],
        ),
        out_shape=[jax.ShapeDtypeStruct((steps, BLOCK, model), bf16)] * 2
        + [jax.ShapeDtypeStruct(packed, bf16)] * 2,
        compiler_params=vmem_limit(60),
        cost_estimate=pl.CostEstimate(
            flops=12 * rows * model * part, bytes_accessed=12 * rows * model, transcendentals=0
        ),
        name="project_back",
    )(place, normed, weight, extra, query_grad, own, came)


def rows_kernel(place_ref, token_ref, residual_ref, gain_ref, own_ref, other_ref, grad_ref):
    seqs, local_rows, model = token_ref.shape
    for k, normed_ref in enumerate((own_ref, other_ref)):
        seq = place_ref[0] ^ k
        weighted = normed_ref[...].astype(f32) * gain_ref[...]
        tokens = token_ref[seq].astype(f32)
        scale = lax.rsqrt(jnp.mean(tokens * tokens, axis=-1, keepdims=True) + epsilon)
        inner = jnp.mean(weighted * tokens, axis=-1, keepdims=True)
        rows = pl.ds(pl.multiple_of(seq * local_rows, local_rows), local_rows)
        grad_ref[seq] = (
            residual_ref[rows] + scale * weighted - tokens * (scale * scale * scale * inner)
        )


def rows_stage(place, tokens, residual_grad, gain_row, own, other):
    whole = lambda array: pl.BlockSpec(array.shape, lambda i, s: (0,) * array.ndim)
    given = (tokens, residual_grad, gain_row, own, other)
    return pl.pallas_call(
        rows_kernel,
        grid_spec=pltpu.PrefetchScalarGridSpec(
            num_scalar_prefetch=1,
            grid=(1,),
            in_specs=[whole(array) for array in given],
            out_specs=whole(tokens),
        ),
        out_shape=jax.ShapeDtypeStruct(tokens.shape, f32),
        compiler_params=vmem_limit(16),
        cost_estimate=pl.CostEstimate(
            flops=20 * tokens.size, bytes_accessed=16 * tokens.size, transcendentals=0
        ),
        name="rows_stage",
    )(place, *given)


def output_kernel(context_ref, token_ref, gain_ref, *refs):
    weights, (residual_ref, normed_ref) = refs[:-2], refs[-2:]
    seqs, local_rows, model = token_ref.shape
    groups = context_ref.shape[0] // seqs
    part = context_ref.shape[1]
    for seq in range(seqs):
        rows = slice(seq * local_rows, (seq + 1) * local_rows)
        for p, weight_ref in enumerate(weights):
            lanes = slice(p * PANEL, (p + 1) * PANEL)
            weight = weight_ref[...].reshape(model, PANEL)
            total = token_ref[seq, :, lanes].astype(f32)
            for group in range(groups):
                total = total + lax.dot_general(
                    context_ref[seq * groups + group],
                    weight[group * part : (group + 1) * part],
                    (((0,), (0,)), ((), ())),
                    preferred_element_type=f32,
                )
            residual_ref[rows, lanes] = total
    normed_ref[...] = rms_scale(residual_ref[...], gain_ref[...]).astype(bf16)


def output_stage(context, tokens, gain_row, everything, shape):
    seqs, local_rows, model = tokens.shape
    whole = lambda array: pl.BlockSpec(array.shape, lambda i: (0,) * array.ndim)
    return pl.pallas_call(
        output_kernel,
        grid=(1,),
        in_specs=[whole(context), whole(tokens), whole(gain_row)] + shape.output_specs(),
        out_specs=[pl.BlockSpec((seqs * local_rows, model), lambda i: (0, 0))] * 2,
        out_shape=[
            jax.ShapeDtypeStruct((seqs * local_rows, model), f32),
            jax.ShapeDtypeStruct((seqs * local_rows, model), bf16),
        ],
        compiler_params=vmem_limit(40),
        cost_estimate=pl.CostEstimate(
            flops=2 * seqs * local_rows * model * model,
            bytes_accessed=2 * model * model,
            transcendentals=0,
        ),
        name="output_stage",
    )(context, tokens, gain_row, *[everything] * shape.panels)


def hidden_kernel(shape, normed_own, normed_other, down_own, down_other, gate_w, upper_w, *refs):
    panels = shape.panels
    down_w = refs[:panels]
    norm_own, norm_other, hidden_ref, gate_ref, upper_ref = refs[panels : panels + 5]
    normed, downs, lows, sides, pres = refs[panels + 5 :]
    step = pl.program_id(0)
    half = normed_own.shape[0]

    @pl.when(step == 0)
    def gather():
        normed[:half] = normed_own[...]
        normed[half:] = normed_other[...]
        downs[:half] = down_own[...]
        downs[half:] = down_other[...]

    across = (((1,), (1,)), ((), ()))
    weights = []
    for side, weight_ref in enumerate((gate_w, upper_w)):
        weight = weight_ref[...].reshape(shape.model, PANEL)
        sides[side, step] = weight
        pres[side] = jnp.dot(normed[...], weight, preferred_element_type=f32)
    down = jnp.concatenate([ref[...].reshape(PANEL, PANEL) for ref in down_w], axis=1)
    pres[2] = lax.dot_general(downs[...], down, across, preferred_element_type=f32)
    slope = 0.7978845608028654
    tile = 64

    def bend_rows(k, carried):
        rows = pl.ds(pl.multiple_of(k * tile, tile), tile)
        gate_pre, up_pre, hidden_grad = pres[0, rows], pres[1, rows], pres[2, rows]
        square = gate_pre * gate_pre
        bend = jnp.tanh(slope * gate_pre * (1.0 + 0.044715 * square))
        share = 0.5 * (1.0 + bend)
        curved = gate_pre * share
        steep = share + 0.5 * gate_pre * (1.0 - bend * bend) * (
            slope * (1.0 + 3.0 * 0.044715 * square)
        )
        hidden_ref[rows] = (curved * up_pre).astype(bf16)
        gate_low = (hidden_grad * up_pre * steep).astype(bf16)
        up_low = (hidden_grad * curved).astype(bf16)
        gate_ref[rows], upper_ref[rows] = gate_low, up_low
        lows[0, step, rows], lows[1, step, rows] = gate_low, up_low
        return carried

    lax.fori_loop(0, 2 * half // tile, bend_rows, 0)

    @pl.when(step == shape.steps - 1)
    def finish():
        for rows, ref in ((slice(0, half), norm_own), (slice(half, 2 * half), norm_other)):
            total = None
            for side in range(2):
                for k in range(shape.steps):
                    more = lax.dot_general(
                        lows[side, k, rows], sides[side, k], across, preferred_element_type=f32
                    )
                    total = more if total is None else total + more
            ref[...] = total.astype(ref.dtype)


def hidden_back_kernel(
    shape,
    place_ref,
    normed_own,
    normed_other,
    down_own,
    down_other,
    hidden_ref,
    gate_ref,
    upper_ref,
    output_ref,
    *refs,
):
    panels = shape.panels
    down_w = refs[:panels]
    out_own, out_other = refs[panels : panels + 2]
    grad_refs, (turned, downs, outs) = refs[panels + 2 : -3], refs[-3:]
    step = pl.program_id(0)
    x, dp = place_ref[0], place_ref[1]
    half = normed_own.shape[0]

    @pl.when(step == 0)
    def gather():
        turned[:, :half] = normed_own[...].T
        turned[:, half:] = normed_other[...].T
        downs[:half] = down_own[...]
        downs[half:] = down_other[...]
        shape.store_output(grad_refs, output_ref, x)

    hidden = hidden_ref[...]
    down = jnp.concatenate([ref[...].reshape(PANEL, PANEL) for ref in down_w], axis=1)
    product = jnp.dot(hidden, down, preferred_element_type=f32)

    @pl.when(step == 0)
    def first_out():
        outs[...] = product

    @pl.when(step != 0)
    def later_out():
        outs[...] += product

    for side, ref in enumerate((gate_ref, upper_ref)):
        grad = jnp.dot(turned[...], ref[...], preferred_element_type=f32)
        shape.store_side(grad_refs, step, side, grad, x, dp)
    grad = jnp.dot(hidden.T, downs[...], preferred_element_type=f32)
    for p in range(panels):
        shape.store_down(grad_refs, step, p, grad[:, p * PANEL : (p + 1) * PANEL], x, dp)

    @pl.when(step == shape.steps - 1)
    def finish():
        out_own[...] = outs[:half]
        out_other[...] = outs[half:].astype(bf16)


class PackedWeights:
    def __init__(self, model, hidden_half, pieces):
        self.model, self.pieces = model, pieces
        self.side = model // pieces
        self.deep = hidden_half // pieces
        self.steps = hidden_half // PANEL
        self.panels = model // PANEL
        self.side_rows = 2 * self.steps * self.side
        self.grad_rows = self.side_rows + self.panels * self.deep

    def side_spec(self, shift):
        return pl.BlockSpec((self.pieces, self.side, PANEL), lambda j: (0, j + shift, 0))

    def down_specs(self):
        if self.pieces == 1:
            first = self.side_rows // PANEL
            each = self.deep // PANEL
            return [
                pl.BlockSpec((1, PANEL, PANEL), lambda j, p=p: (0, first + p * each + j, 0))
                for p in range(self.panels)
            ]
        first = self.side_rows // self.deep
        some = self.pieces // self.steps
        return [
            pl.BlockSpec((some, self.deep, PANEL), lambda j, p=p: (j, first + p, 0))
            for p in range(self.panels)
        ]

    def output_specs(self):
        first = self.grad_rows // self.side
        return [
            pl.BlockSpec((self.pieces, self.side, PANEL), lambda j, p=p: (0, first + p, 0))
            for p in range(self.panels)
        ]

    def grad_shapes(self):
        if self.pieces == 1:
            return [(1, self.grad_rows, PANEL)]
        side = self.steps * self.side
        first = (self.pieces // 2, side + self.deep + self.panels * 32, PANEL)
        second = (self.pieces // 2, side + (self.panels - 1) * self.deep, PANEL)
        return [first, first, second, second]

    def store_output(self, refs, output_ref, x):
        if self.pieces == 1:
            return
        owners, rows, model = output_ref.shape
        pairs = output_ref[...].reshape(owners // 2, 2, rows, model)
        start = self.steps * self.side + self.deep
        short = jnp.zeros((owners // 2, 32 - rows, PANEL), bf16)
        for k in range(2):

            @pl.when(x == k)
            def store():
                for p in range(self.panels):
                    lanes = slice(p * PANEL, (p + 1) * PANEL)
                    at = slice(start + 32 * p, start + 32 * (p + 1))
                    for slot, side in ((0, k), (1, 1 - k)):
                        refs[slot][:, at, :] = jnp.concatenate(
                            [pairs[:, side, :, lanes], short], axis=1
                        )

    def store_side(self, refs, step, side, value, x, dp):
        low = value.astype(bf16).reshape(self.pieces, self.side, PANEL)
        if self.pieces == 1:
            start = pl.multiple_of((step + side * self.steps) * self.side, 16)
            refs[0][:, pl.ds(start, self.side), :] = low
            return
        rows = pl.ds(pl.multiple_of(step * self.side, 16), self.side)
        half = self.pieces // 2
        if side:
            for k in range(2):

                @pl.when(dp == k)
                def store_upper():
                    refs[2][:, rows, :] = low[k * half : (k + 1) * half]
                    refs[3][:, rows, :] = low[(1 - k) * half : (2 - k) * half]
        else:
            pairs = low.reshape(half, 2, self.side, PANEL)
            for k in range(2):

                @pl.when(x == k)
                def store_gate():
                    refs[0][:, rows, :] = pairs[:, k]
                    refs[1][:, rows, :] = pairs[:, 1 - k]

    def store_down(self, refs, step, p, value, x, dp):
        low = value.astype(bf16)
        if self.pieces == 1:
            start = pl.multiple_of(self.side_rows + p * self.deep + step * PANEL, PANEL)
            refs[0][0, pl.ds(start, PANEL), :] = low
            return
        some = self.pieces // self.steps
        first = self.steps * self.side
        if p == 0:
            pairs = low.reshape(some // 2, 2, self.deep, PANEL)
            spots = pl.ds(step * (some // 2), some // 2)
            for k in range(2):

                @pl.when(x == k)
                def store_first():
                    refs[0][spots, first : first + self.deep, :] = pairs[:, k]
                    refs[1][spots, first : first + self.deep, :] = pairs[:, 1 - k]
        else:
            pieces = low.reshape(some, self.deep, PANEL)
            per_half = self.steps // 2
            spots = pl.ds((step % per_half) * some, some)
            first += (p - 1) * self.deep
            for slot, mine in ((2, step // per_half == dp), (3, step // per_half != dp)):

                @pl.when(mine)
                def store_other():
                    refs[slot][spots, first : first + self.deep, :] = pieces


def hidden_stage(normed, normed_other, down, down_other, everything, shape):
    half, model = normed.shape
    whole = pl.BlockSpec((half, model), lambda j: (0, 0))
    panel = pl.BlockSpec((2 * half, PANEL), lambda j: (0, j))
    units = shape.steps * PANEL
    return pl.pallas_call(
        functools.partial(hidden_kernel, shape),
        grid=(shape.steps,),
        in_specs=[whole] * 4
        + [shape.side_spec(0), shape.side_spec(shape.steps)]
        + shape.down_specs(),
        out_specs=[whole] * 2 + [panel] * 3,
        out_shape=[
            jax.ShapeDtypeStruct((half, model), f32),
            jax.ShapeDtypeStruct((half, model), bf16),
        ]
        + [jax.ShapeDtypeStruct((2 * half, units), bf16)] * 3,
        scratch_shapes=[
            pltpu.VMEM((2 * half, model), bf16),
            pltpu.VMEM((2 * half, model), bf16),
            pltpu.VMEM((2, shape.steps, 2 * half, PANEL), bf16),
            pltpu.VMEM((2, shape.steps, model, PANEL), bf16),
            pltpu.VMEM((3, 2 * half, PANEL), f32),
        ],
        compiler_params=vmem_limit(40),
        cost_estimate=pl.CostEstimate(
            flops=10 * 2 * half * model * units, bytes_accessed=12 * model * units, transcendentals=0
        ),
        name="hidden_stage",
    )(normed, normed_other, down, down_other, *[everything] * (2 + shape.panels))


def hidden_back(place, normed, normed_other, down, down_other, lows, output, everything, shape):
    half, model = normed.shape
    whole = pl.BlockSpec((half, model), lambda j, s: (0, 0))
    panel = pl.BlockSpec((2 * half, PANEL), lambda j, s: (0, j))
    with_place = lambda spec: pl.BlockSpec(
        spec.block_shape, lambda j, s, spec=spec: spec.index_map(j)
    )
    grads = shape.grad_shapes()
    units = shape.steps * PANEL
    return pl.pallas_call(
        functools.partial(hidden_back_kernel, shape),
        grid_spec=pltpu.PrefetchScalarGridSpec(
            num_scalar_prefetch=1,
            grid=(shape.steps,),
            in_specs=[whole] * 4
            + [panel] * 3
            + [pl.BlockSpec(output.shape, lambda j, s: (0, 0, 0))]
            + [with_place(spec) for spec in shape.down_specs()],
            out_specs=[whole] * 2 + [pl.BlockSpec(size, lambda j, s: (0, 0, 0)) for size in grads],
            scratch_shapes=[
                pltpu.VMEM((model, 2 * half), bf16),
                pltpu.VMEM((2 * half, model), bf16),
                pltpu.VMEM((2 * half, model), f32),
            ],
        ),
        out_shape=[
            jax.ShapeDtypeStruct((half, model), f32),
            jax.ShapeDtypeStruct((half, model), bf16),
        ]
        + [jax.ShapeDtypeStruct(size, bf16) for size in grads],
        compiler_params=vmem_limit(60),
        cost_estimate=pl.CostEstimate(
            flops=8 * 2 * half * model * units, bytes_accessed=12 * model * units, transcendentals=0
        ),
        name="hidden_back",
    )(
        place, normed, normed_other, down, down_other, *lows, output, *[everything] * shape.panels
    )


def output_back_kernel(norm_own, norm_other, residual_ref, down_ref, gain_ref, context_ref, *refs):
    weights = refs[:-4]
    rows_ref, gain_grad_ref, context_grad_ref, weight_grad_ref = refs[-4:]
    residual, gain = residual_ref[...], gain_ref[...]
    norm_grad = norm_own[...] + norm_other[...].astype(f32)
    scale = lax.rsqrt(jnp.mean(residual * residual, axis=-1, keepdims=True) + epsilon)
    gain_grad_ref[...] = jnp.sum(norm_grad * (residual * scale), axis=0, keepdims=True)
    weighted = norm_grad * gain
    inner = jnp.mean(weighted * residual, axis=-1, keepdims=True)
    rows_grad = (
        down_ref[...].astype(f32)
        + scale * weighted
        - residual * (scale * scale * scale * inner)
    )
    rows_ref[...] = rows_grad
    low = rows_grad.astype(bf16)
    blocks, part, local_rows = context_ref.shape
    seqs = rows_grad.shape[0] // local_rows
    groups = blocks // seqs
    model = residual.shape[1]
    for group in range(groups):
        columns = slice(group * part, (group + 1) * part)
        product = None
        for p, weight_ref in enumerate(weights):
            more = lax.dot_general(
                weight_ref[...].reshape(model, PANEL)[columns],
                low[:, p * PANEL : (p + 1) * PANEL],
                (((1,), (1,)), ((), ())),
                preferred_element_type=f32,
            )
            product = more if product is None else product + more
        turned = product.astype(bf16)
        total = None
        for seq in range(seqs):
            rows = slice(seq * local_rows, (seq + 1) * local_rows)
            context_grad_ref[seq * groups + group] = turned[:, rows]
            more = jnp.dot(
                context_ref[seq * groups + group], low[rows], preferred_element_type=f32
            )
            total = more if total is None else total + more
        weight_grad_ref[columns, :] = total.astype(bf16)


def output_back(norm_own, norm_other, residual, down, gain_row, context, everything, shape):
    rows, model = residual.shape
    whole = lambda array: pl.BlockSpec(array.shape, lambda i: (0,) * array.ndim)
    given = (norm_own, norm_other, residual, down, gain_row, context)
    out_shape = [
        jax.ShapeDtypeStruct((rows, model), f32),
        jax.ShapeDtypeStruct((1, model), f32),
        jax.ShapeDtypeStruct(context.shape, bf16),
        jax.ShapeDtypeStruct((model, model), bf16),
    ]
    return pl.pallas_call(
        output_back_kernel,
        grid=(1,),
        in_specs=[whole(array) for array in given] + shape.output_specs(),
        out_specs=[whole(array) for array in out_shape],
        out_shape=out_shape,
        compiler_params=vmem_limit(40),
        cost_estimate=pl.CostEstimate(
            flops=4 * rows * model * model, bytes_accessed=4 * model * model, transcendentals=0
        ),
        name="output_back",
    )(*given, *[everything] * shape.panels)


def owned_kernel(part, term_ref, *refs):
    groups, rows, columns = term_ref.shape
    extras = None
    for group in range(groups):
        term = term_ref[group].astype(f32)
        for k in range(3):
            refs[k][:, group * part : (group + 1) * part] = term[:, k * part : (k + 1) * part]
        more = term[:, 3 * part :]
        extras = more if extras is None else extras + more
    short = jnp.zeros((BLOCK - rows, BLOCK), f32)
    refs[3][...] = jnp.concatenate([extras, short], axis=0).T[:8]


def owned_stage(terms, model, part):
    groups, rows, columns = terms.shape
    whole = lambda array: pl.BlockSpec(array.shape, lambda i: (0,) * array.ndim)
    out_shape = [jax.ShapeDtypeStruct((rows, model), f32)] * 3 + [
        jax.ShapeDtypeStruct((8, BLOCK), f32)
    ]
    return pl.pallas_call(
        functools.partial(owned_kernel, part),
        grid=(1,),
        in_specs=[whole(terms)],
        out_specs=[whole(array) for array in out_shape],
        out_shape=out_shape,
        compiler_params=vmem_limit(16),
        cost_estimate=pl.CostEstimate(
            flops=terms.size, bytes_accessed=4 * terms.size, transcendentals=0
        ),
        name="owned_stage",
    )(terms)


def swap(value, axis):
    return lax.ppermute(value, axis, [(0, 1), (1, 0)])


def after(value, gate):
    return lax.optimization_barrier((value, gate))[0]


def pick(pair, index, axis):
    return lax.dynamic_index_in_dim(pair, index, axis, keepdims=False)


def in_order(mine, theirs, index, axis):
    return jnp.where(
        index == 0, jnp.stack([mine, theirs], axis), jnp.stack([theirs, mine], axis)
    )


def plus(mine, came):
    return (mine.astype(f32) + came.astype(f32)).astype(bf16)


def halve(value, index, name, axis):
    return plus(pick(value, index, axis), swap(pick(value, 1 - index, axis), name))


def columns_in_panels(weight):
    rows, cols = weight.shape
    return jnp.transpose(weight.reshape(rows, cols // PANEL, PANEL), (1, 0, 2)).reshape(
        rows * cols // PANEL, PANEL
    )


def own_half(weight, each, c):
    rows, cols = weight.shape
    return pick(weight.reshape(rows, cols // (2 * each), 2, each), c, 2).reshape(rows, cols // 2)


def body(
    inputs,
    w_query,
    w_key,
    w_value,
    w_output,
    w_gate,
    w_upper,
    w_down,
    gain_one,
    gain_two,
    bias_table,
    buckets,
    cotangent,
    sizes,
):
    along_dp, along_a = sizes
    dp, a, x, c = (lax.axis_index(name) for name in ("dp", "a", "x", "c"))
    zh, zl = lax.axis_index("zh"), lax.axis_index("zl")
    z, group = 2 * zh + zl, 2 * zl + x
    depth = 4
    seqs, local_rows, model = inputs.shape
    length = buckets.shape[0] // 2 + 1
    width = model // H
    heads = H // GROUPS
    part = heads * width
    weight_rows, hidden_units = w_gate.shape
    each = w_down.shape[0]
    own_count = depth * 2 * local_rows
    token_count = seqs * local_rows

    near = in_order(pick(inputs, zh, 0), swap(pick(inputs, 1 - zh, 0), "zh"), zh, 0)
    column = in_order(near, swap(near, "zl"), zl, 1)
    tokens_own = in_order(column, swap(column, "x"), x, 2).reshape(own_count, model)

    blocks = [
        jnp.transpose(w.reshape(weight_rows, GROUPS, part), (1, 0, 2))
        for w in (w_query, w_key, w_value)
    ]
    table_column = jnp.pad(bias_table, (0, weight_rows - bias_table.shape[0]))
    extra = jnp.stack([gain_one, gain_two, table_column], axis=1)
    extra = jnp.pad(extra, ((0, 0), (0, BLOCK - extra.shape[1])))
    extra = jnp.broadcast_to(extra[None], (GROUPS, weight_rows, BLOCK))
    columns = lax.all_to_all(
        jnp.concatenate([*blocks, extra], axis=2), ("zl", "x"), 0, 0, tiled=True
    )
    columns = in_order(columns, swap(columns, "zh"), zh, 0)
    if along_a > 1:
        columns = lax.all_gather(columns, "a", axis=0)
    columns = in_order(columns, swap(columns, "dp"), dp, 0)
    columns = in_order(columns, swap(columns, "c"), c, columns.ndim - 2)
    columns = columns.reshape(model, 3 * part + BLOCK)
    gain_a = columns[:, 3 * part].astype(f32).reshape(1, model)
    gain_b = columns[:, 3 * part + 1].astype(f32).reshape(1, model)
    table = columns[:, 3 * part + 2].reshape(model // weight_rows, weight_rows)
    table = table[:, : bias_table.shape[0]].reshape(BUCKETS, H)
    padded = jnp.pad(buckets, (0, 1), constant_values=BLOCK)
    hot = (padded[:, None] == jnp.arange(BLOCK, dtype=jnp.int32)[None, :]).astype(bf16)
    own_table = lax.dynamic_slice_in_dim(table, group * heads, heads, 1)
    own_table = jnp.pad(own_table, ((0, BLOCK - BUCKETS), (0, 0)))
    ahead = jnp.pad(buckets, (1, 0), constant_values=BLOCK)
    hot_ahead = (ahead[None, :] == jnp.arange(BLOCK, dtype=jnp.int32)[:, None]).astype(bf16)
    vectors = lax.dot_general(
        own_table, hot_ahead, (((0,), (0,)), ((), ())), preferred_element_type=f32
    ).reshape(heads, 1, 2 * length)

    if along_a == 1:
        sent = [own_half(w, each, 1 - c) for w in (w_gate, w_upper)] + [w_output]
        came = swap(jnp.concatenate(sent, axis=1), "c")
        kept = [own_half(w, each, c) for w in (w_gate, w_upper)] + [w_output]
        both = in_order(jnp.concatenate(kept, axis=1), came, c, 0).reshape(2 * weight_rows, -1)
        packed = jnp.concatenate(
            [
                columns_in_panels(both[:, :hidden_units]),
                columns_in_panels(w_down),
                columns_in_panels(both[:, hidden_units:]),
            ],
            axis=0,
        )
        pieces = along_dp * depth * 2
        everything = lax.all_gather(packed, chips, axis=0, tiled=True)
        everything = everything.reshape(pieces, packed.shape[0], PANEL)
    else:
        pieces = 1
        gate_all, upper_all, down_all, output_all = (
            lax.all_gather(w, everyone, axis=0, tiled=True)
            for w in (w_gate, w_upper, w_down, w_output)
        )
        down_half = pick(down_all.reshape(-1, 2, each, model), c, 1).reshape(-1, model)
        everything = jnp.concatenate(
            [
                columns_in_panels(own_half(gate_all, each, c)),
                columns_in_panels(own_half(upper_all, each, c)),
                columns_in_panels(down_half),
                columns_in_panels(output_all),
            ],
            axis=0,
        )[None]
    shape = PackedWeights(model, hidden_units // 2, pieces)

    if along_a > 1:
        tokens_all = lax.all_gather(tokens_own, "a", axis=0, tiled=True)
    else:
        tokens_all = tokens_own
    normed, query, own = project(tokens_all, gain_a, columns, heads, width)
    if along_a > 1:
        query = lax.dynamic_slice_in_dim(query, a * own_count, own_count, 1)
        normed = lax.dynamic_slice_in_dim(normed, a * own_count, own_count, 0)
    other = swap(own, "c")
    biases = skew(vectors)
    place = jnp.stack([a * (own_count // BLOCK), c]).astype(jnp.int32)
    place = after(place, hot)
    context_own, probs, kept, inverse = attend(place, query, own, other, biases)
    owners = ("zh", "zl", "x")
    context = lax.all_to_all(context_own, owners, 0, 0, tiled=True)

    down_grad = cotangent.reshape(token_count, model)
    down_other = swap(down_grad, "c")
    residual, second = output_stage(context, inputs, gain_b, everything, shape)
    second_other = swap(second, "c")
    sides_place = jnp.stack([x, dp]).astype(jnp.int32)
    norm_own, norm_other, *lows = hidden_stage(
        second, second_other, down_grad, down_other, everything, shape
    )
    norm_came = swap(norm_other, "c")
    residual_grad, gain_b_grad, context_sent, output_grad = output_back(
        norm_own, norm_came, residual, down_grad, gain_b, context, everything, shape
    )
    *lows, output_grad, context_sent = lax.optimization_barrier(
        (*lows, output_grad, context_sent)
    )
    context_grad = lax.all_to_all(context_sent, owners, 0, 0, tiled=True)
    output_terms = halve(
        output_grad.reshape(model // (2 * weight_rows), CORES, weight_rows, model), c, "c", 1
    )
    out_own, out_other, *big_grads = hidden_back(
        sides_place,
        second,
        second_other,
        down_grad,
        down_other,
        lows,
        output_terms,
        everything,
        shape,
    )
    out_came = swap(out_other, "c")
    outputs = (residual + out_own + out_came.astype(f32)).astype(bf16)

    if along_a == 1:
        first_terms, first_sent, second_terms, second_sent = big_grads
        first_came = swap(first_sent, "x")
        second_came = swap(second_sent, "dp")
    query_grad, own_grad, other_grad, bucket_sums = attend_back(
        place, context_grad, kept, inverse, probs, query, own, other, hot
    )
    if along_a > 1:
        own_grad, other_grad = (
            lax.psum_scatter(value, "a", scatter_dimension=2, tiled=True)
            for value in (own_grad, other_grad)
        )
    else:
        first_came, second_came, query_grad, own_grad, other_grad, bucket_sums = (
            lax.optimization_barrier(
                (first_came, second_came, query_grad, own_grad, other_grad, bucket_sums)
            )
        )
        first_terms = plus(first_terms, first_came).reshape(along_dp, depth, -1, PANEL)
        second_terms = plus(second_terms, second_came).reshape(depth, 2, -1, PANEL)
        first_terms, second_terms, query_grad = lax.optimization_barrier(
            (first_terms, second_terms, query_grad)
        )
        first_came = swap(pick(first_terms, 1 - dp, 0), "dp")
        second_came = swap(pick(second_terms, 1 - x, 1), "x")
    came = swap(other_grad, "c")

    per_owner = bias_table.shape[0]
    bucket_sums = bucket_sums[:, 0, :BUCKETS]
    spot = jnp.arange(model, dtype=jnp.int32)
    entry = spot // weight_rows * per_owner + spot % weight_rows
    entry = jnp.where(spot % weight_rows < per_owner, entry, -1)
    spread = (entry[None, :] // H == jnp.arange(BUCKETS, dtype=jnp.int32)[:, None]).astype(bf16)
    table_rows = jnp.dot(bucket_sums.astype(bf16), spread, preferred_element_type=f32)
    own_heads = group * heads + jnp.arange(heads, dtype=jnp.int32)
    table_row = jnp.sum(
        jnp.where(entry[None, :] % H == own_heads[:, None], table_rows, 0.0), axis=0
    )
    extra = jnp.stack(
        [jnp.zeros((model,), f32), gain_b_grad.reshape(model), table_row, gain_a.reshape(model)]
        + [jnp.zeros((model,), f32)] * 4
    )
    core_place = jnp.stack([x, c]).astype(jnp.int32)
    *rows_grads, mixed, sent_c = project_back(
        core_place, query_grad, own_grad, came, normed, columns, extra, weight_rows
    )
    if along_a == 1:
        first_came, second_came = (
            after(value, sent_c) for value in (first_came, second_came)
        )

    by_owner = (along_dp, along_a, 2, GROUPS, weight_rows, mixed.shape[2])
    mixed, sent_c = mixed.reshape(by_owner), sent_c.reshape(by_owner)
    came_x = swap(rows_grads[1], "x")
    mixed = plus(mixed, swap(sent_c, "c"))
    if along_a == 1:
        terms = jnp.concatenate(
            [
                plus(pick(first_terms, dp, 0), first_came),
                plus(pick(second_terms, x, 1), second_came),
            ],
            axis=1,
        )
        terms = terms.reshape(2, 2, -1, PANEL)
        column_came = swap(pick(terms, 1 - zl, 1), "zl")
    came_dp = swap(pick(mixed, 1 - dp, 0), "dp")
    mixed = plus(pick(mixed, dp, 0), came_dp)
    came_zh = swap(pick(mixed, 1 - zh, 1), "zh")
    share = plus(rows_grads[0], came_x).reshape(2, 2, local_rows, model)
    share, sent = pick(share, zl, 1), pick(share, 1 - zl, 1)
    came_zl = swap(sent, "zl")
    if along_a == 1:
        column_came = after(column_came, sent)
        terms = plus(pick(terms, zl, 1), column_came)
        sent = pick(terms, 1 - zh, 0)
        column_came = swap(sent, "zh")
    share = plus(share, after(came_zl, sent))
    rows_own, sent = pick(share, zh, 0), pick(share, 1 - zh, 0)
    rows_came = swap(sent, "zh")
    came_zh = after(came_zh, sent)
    mixed = plus(pick(mixed, zh, 1), came_zh)
    if along_a > 1:
        mixed = lax.psum_scatter(mixed, "a", scatter_dimension=0, tiled=True)
    terms_owned = lax.all_to_all(mixed[0], ("zl", "x"), 0, 0, tiled=True)
    input_grad = rows_stage(
        zh.astype(jnp.int32)[None], inputs, residual_grad, gain_a, rows_own, rows_came
    )

    if along_a == 1:
        column_came = after(column_came, mixed)
        total = pick(terms, zh, 0).astype(f32) + column_came.astype(f32)
        side, deep = shape.steps * shape.side, shape.deep
        rest = total[side + deep + shape.panels * 32 :]
        output_owned = jnp.transpose(
            total[side + deep : side + deep + shape.panels * 32].reshape(shape.panels, 32, PANEL)[
                :, :weight_rows
            ],
            (1, 0, 2),
        ).reshape(weight_rows, model)
        sides = jnp.concatenate([total[:side], rest[:side]], axis=0)
        sides = sides.astype(bf16).reshape(-1, 2, weight_rows, PANEL)
        sides = in_order(pick(sides, c, 1), swap(pick(sides, 1 - c, 1), "c"), c, 0)
        sides = sides.reshape(2, 2, shape.steps, weight_rows, PANEL)
        sides = jnp.transpose(
            sides.reshape(2, 2, shape.steps, weight_rows, PANEL // each, each), (1, 3, 2, 4, 0, 5)
        ).reshape(2, weight_rows, hidden_units)
        gate_owned, upper_owned = sides[0].astype(f32), sides[1].astype(f32)
        down_owned = jnp.transpose(
            jnp.concatenate([total[side : side + deep], rest[side:]], axis=0).reshape(
                shape.panels, each, PANEL
            ),
            (1, 0, 2),
        ).reshape(each, model)
    else:
        side = shape.steps * model
        gate_half, upper_half = (
            jnp.transpose(
                big_grads[0][0, k * side : (k + 1) * side].reshape(shape.steps, model, PANEL),
                (1, 0, 2),
            ).reshape(model, -1, 1, each)
            for k in range(2)
        )
        down_half = jnp.transpose(
            big_grads[0][0, 2 * side :].reshape(shape.panels, -1, PANEL), (1, 0, 2)
        ).reshape(-1, 1, each, model)
        zero = jnp.zeros_like
        output_owned = lax.psum_scatter(
            in_order(output_terms, zero(output_terms), c, 1).reshape(model, model),
            everyone,
            scatter_dimension=0,
            tiled=True,
        ).astype(f32)
        gate_owned, upper_owned = (
            lax.psum_scatter(
                in_order(half, zero(half), c, 2).reshape(model, hidden_units),
                everyone,
                scatter_dimension=0,
                tiled=True,
            ).astype(f32)
            for half in (gate_half, upper_half)
        )
        down_owned = lax.psum_scatter(
            in_order(down_half, zero(down_half), c, 1).reshape(hidden_units, model),
            everyone,
            scatter_dimension=0,
            tiled=True,
        ).astype(f32)

    *owned, extras = owned_stage(terms_owned, model, part)
    return (
        outputs.reshape(seqs, local_rows, model),
        input_grad,
        *owned,
        output_owned,
        gate_owned,
        upper_owned,
        down_owned,
        extras[0, :weight_rows],
        extras[1, :weight_rows],
        extras[2, :per_owner],
    )


def solution(mesh):
    along_dp, along_ctx = mesh.shape["dp"], mesh.shape["ctx"]
    along_a = along_ctx // (4 * 2 * CORES)
    fine = Mesh(mesh.devices.reshape(along_dp, along_a, 2, 2, 2, CORES), everyone)
    rows = P("dp", ("a", "zh", "zl", "x", "c"), None)
    owned = P(everyone, None)
    vector = P(everyone)
    in_specs = (rows, *[owned] * 7, *[vector] * 3, P(), rows)
    out_specs = (rows, rows, *[owned] * 7, *[vector] * 3)
    return jax.shard_map(
        functools.partial(body, sizes=(along_dp, along_a)),
        mesh=fine,
        in_specs=in_specs,
        out_specs=out_specs,
        check_vma=False,
    )
```

```python
import functools

import jax
import jax.numpy as jnp
from jax import lax
from jax.experimental import pallas as pl
from jax.experimental.pallas import tpu as pltpu
from jax.sharding import Mesh
from jax.sharding import PartitionSpec as P

H = 12
BUCKETS = 32
GROUPS = 4
CORES = 2
BLOCK = 128

epsilon = 1e-06
exactly = lax.Precision.HIGHEST
bf16 = jnp.bfloat16
f32 = jnp.float32
everyone = ("dp", "a", "zh", "zl", "x", "c")
chips = ("dp", "zh", "zl", "x")
PANEL = 256


def rms_scale(values, gain_vec):
    return (
        values * lax.rsqrt(jnp.mean(values * values, axis=-1, keepdims=True) + epsilon) * gain_vec
    )


def vmem_limit(mib):
    return pltpu.CompilerParams(vmem_limit_bytes=mib * 1024 * 1024)


def project_kernel(heads, token_ref, gain_ref, weight_ref, normed_ref, query_ref, pair_ref):
    rows = token_ref[...].astype(f32)
    scale = lax.rsqrt(jnp.mean(rows * rows, axis=-1, keepdims=True) + epsilon)
    normed = (rows * scale * gain_ref[...]).astype(bf16)
    normed_ref[...] = normed
    width = query_ref.shape[2]
    mixed = jnp.dot(
        normed, weight_ref[:, : 3 * heads * width], preferred_element_type=f32
    ).astype(bf16)
    for k in range(heads):
        query_ref[k] = mixed[:, k * width : (k + 1) * width]
        for side in range(2):
            first = (heads * (side + 1) + k) * width
            pair_ref[k, :, side * width : (side + 1) * width] = mixed[:, first : first + width]


def project(tokens, gain_row, weight, heads, width):
    rows, model = tokens.shape
    tile = 256
    return pl.pallas_call(
        functools.partial(project_kernel, heads),
        grid=(rows // tile,),
        in_specs=[
            pl.BlockSpec((tile, model), lambda i: (i, 0)),
            pl.BlockSpec((1, model), lambda i: (0, 0)),
            pl.BlockSpec(weight.shape, lambda i: (0, 0)),
        ],
        out_specs=[
            pl.BlockSpec((tile, model), lambda i: (i, 0)),
            pl.BlockSpec((heads, tile, width), lambda i: (0, i, 0)),
            pl.BlockSpec((heads, tile, 2 * width), lambda i: (0, i, 0)),
        ],
        out_shape=[
            jax.ShapeDtypeStruct((rows, model), bf16),
            jax.ShapeDtypeStruct((heads, rows, width), bf16),
            jax.ShapeDtypeStruct((heads, rows, 2 * width), bf16),
        ],
        compiler_params=vmem_limit(12),
        cost_estimate=pl.CostEstimate(
            flops=2 * rows * model * 3 * heads * width,
            bytes_accessed=8 * rows * model,
            transcendentals=0,
        ),
        name="project",
    )(tokens, gain_row, weight)


def skew_kernel(vector_ref, table_ref, row_scratch):
    span = vector_ref.shape[-1]
    for r in range(8):
        row_scratch[r : r + 1, :] = pltpu.roll(vector_ref[0], r, 1) if r else vector_ref[0]
    eight = row_scratch[...]
    rows = []
    for group in range(BLOCK // 8):
        turned = pltpu.roll(eight, 8 * group, 1) if group else eight
        rows.append(turned[:, BLOCK:span])
    for pair in range(BLOCK // 16):
        both = jnp.concatenate(rows[2 * pair : 2 * pair + 2], axis=0)
        table_ref[0, 16 * pair : 16 * pair + 16, :] = both.astype(bf16)


def skew(vectors):
    heads, unused, span = vectors.shape
    return pl.pallas_call(
        skew_kernel,
        grid=(heads,),
        in_specs=[pl.BlockSpec((1, 1, span), lambda h: (h, 0, 0))],
        out_specs=pl.BlockSpec((1, BLOCK, span - BLOCK), lambda h: (h, 0, 0)),
        out_shape=jax.ShapeDtypeStruct((heads, BLOCK, span - BLOCK), bf16),
        scratch_shapes=[pltpu.VMEM((8, span), f32)],
        compiler_params=vmem_limit(10),
        cost_estimate=pl.CostEstimate(
            flops=0, bytes_accessed=2 * heads * BLOCK * span, transcendentals=0
        ),
        name="skew",
    )(vectors)


def interleave(keys, values, own_ref, other_ref, parity, fill):
    width = keys.shape[1]
    for k in range(own_ref.shape[1] // BLOCK):
        rows = slice(k * BLOCK, (k + 1) * BLOCK)
        for source, spot in ((own_ref, parity), (other_ref, 1 - parity)):
            into = pl.ds(pl.multiple_of((2 * k + spot) * BLOCK, BLOCK), BLOCK)
            keys[into, :] = source[0, rows, :width]
            values[into, :width] = source[0, rows, width:]
            if fill:
                values[into, width:] = jnp.ones((BLOCK, width), bf16)


def table_starts(tile, step, first_block, parity, blocks):
    starts = []
    for sub in range(tile // BLOCK):
        block = 2 * (first_block + step * (tile // BLOCK) + sub) + parity
        starts.append((blocks - 1 - block) * BLOCK)
    return starts


def attend_kernel(
    tile,
    chunk,
    place_ref,
    query_ref,
    pair_own,
    pair_other,
    table,
    context_ref,
    probs_ref,
    kept_ref,
    inverse_ref,
    keys,
    values,
    scores,
):
    head, step = pl.program_id(0), pl.program_id(1)
    first_block, parity = place_ref[0], place_ref[1]
    key_count, width = keys.shape
    blocks = key_count // BLOCK
    subs = tile // BLOCK
    table = table.at[0]

    @pl.when(step == 0)
    def prepare():
        interleave(keys, values, pair_own, pair_other, parity, True)

    query = query_ref[0]
    starts = table_starts(tile, step, first_block, parity, blocks)
    lane_max = None
    for part in range(key_count // chunk):
        cols = slice(part * chunk, (part + 1) * chunk)
        product = lax.dot_general(
            query, keys[cols, :], (((1,), (1,)), ((), ())), preferred_element_type=f32
        )
        pieces = []
        for sub in range(subs):
            rows = slice(sub * BLOCK, (sub + 1) * BLOCK)
            offset = pl.multiple_of(starts[sub] + part * chunk, BLOCK)
            piece = product[rows] + table[:, pl.ds(offset, chunk)].astype(f32)
            scores[rows, cols] = piece
            for k in range(chunk // BLOCK):
                lanes = piece[:, k * BLOCK : (k + 1) * BLOCK]
                top = lanes if k == 0 else jnp.maximum(top, lanes)
            pieces.append(top)
        pieces = jnp.concatenate(pieces, axis=0)
        lane_max = pieces if lane_max is None else jnp.maximum(lane_max, pieces)
    row_max = jnp.max(lane_max, axis=-1, keepdims=True)
    total = jnp.zeros((tile, 2 * width), f32)
    for part in range(key_count // chunk):
        cols = slice(part * chunk, (part + 1) * chunk)
        low = jnp.exp(scores[:, cols] - row_max).astype(bf16)
        probs_ref[0, :, cols] = low
        total = total + jnp.dot(low, values[cols, :], preferred_element_type=f32)
    inverse = 1.0 / total[:, width:]
    value = total[:, :width] * inverse
    kept_ref[0, :, :width] = value
    kept_ref[0, :, width:] = inverse
    turned = value.T.astype(bf16)
    inverse_turned = inverse.T
    for sub in range(subs):
        lanes = slice(sub * BLOCK, (sub + 1) * BLOCK)
        rows = pl.ds(pl.multiple_of(head * width, width), width)
        context_ref[step * subs + sub, rows, :] = turned[:, lanes]
        inverse_ref[0, sub] = inverse_turned[0:1, lanes]


def attend(place, query, own, other, table):
    heads, rows, width = query.shape
    own_rows = own.shape[1]
    key_count = 2 * own_rows
    tile, chunk = 256, 512
    pairs = pl.BlockSpec((1, own_rows, 2 * width), lambda h, i, s: (h, 0, 0))
    return pl.pallas_call(
        functools.partial(attend_kernel, tile, chunk),
        grid_spec=pltpu.PrefetchScalarGridSpec(
            num_scalar_prefetch=1,
            grid=(heads, rows // tile),
            in_specs=[
                pl.BlockSpec((1, tile, width), lambda h, i, s: (h, i, 0)),
                pairs,
                pairs,
                pl.BlockSpec((1, *table.shape[1:]), lambda h, i, s: (h, 0, 0)),
            ],
            out_specs=[
                pl.BlockSpec((rows // BLOCK, heads * width, BLOCK), lambda h, i, s: (0, 0, 0)),
                pl.BlockSpec((1, tile, key_count), lambda h, i, s: (h, i, 0)),
                pl.BlockSpec((1, tile, 2 * width), lambda h, i, s: (h, i, 0)),
                pl.BlockSpec((1, tile // BLOCK, 1, BLOCK), lambda h, i, s: (h, i, 0, 0)),
            ],
            scratch_shapes=[
                pltpu.VMEM((key_count, width), bf16),
                pltpu.VMEM((key_count, 2 * width), bf16),
                pltpu.VMEM((tile, key_count), f32),
            ],
        ),
        out_shape=[
            jax.ShapeDtypeStruct((rows // BLOCK, heads * width, BLOCK), bf16),
            jax.ShapeDtypeStruct((heads, rows, key_count), bf16),
            jax.ShapeDtypeStruct((heads, rows, 2 * width), f32),
            jax.ShapeDtypeStruct((heads, rows // BLOCK, 1, BLOCK), f32),
        ],
        compiler_params=vmem_limit(54),
        cost_estimate=pl.CostEstimate(
            flops=16 * heads * rows * key_count * width,
            bytes_accessed=2 * heads * rows * key_count,
            transcendentals=heads * rows * key_count,
        ),
        name="attend",
    )(place, query, own, other, table)


def attend_back_kernel(
    tile,
    chunk,
    place_ref,
    grad_ref,
    kept_ref,
    inverse_ref,
    probs_ref,
    query_ref,
    pair_own,
    pair_other,
    hot_ref,
    query_grad_ref,
    own_grad_ref,
    other_grad_ref,
    offset_ref,
    keys,
    values,
    diagonals,
    key_sums,
    value_sums,
):
    step = pl.program_id(1)
    first_block, parity = place_ref[0], place_ref[1]
    key_count, width = keys.shape
    blocks = key_count // BLOCK
    subs = tile // BLOCK

    @pl.when(step == 0)
    def prepare():
        interleave(keys, values, pair_own, pair_other, parity, False)
        diagonals[...] = jnp.zeros_like(diagonals)
        key_sums[...] = jnp.zeros_like(key_sums)
        value_sums[...] = jnp.zeros_like(value_sums)

    turned = jnp.concatenate(
        [grad_ref[sub].astype(f32) * inverse_ref[0, sub] for sub in range(subs)], axis=1
    )
    grad_turned = turned.astype(bf16)
    scaled = grad_turned.astype(f32).T
    delta = jnp.sum(scaled * kept_ref[0, :, :width], axis=-1, keepdims=True)
    scaled = scaled.astype(bf16)
    query_turned = query_ref[0].astype(f32).T.astype(bf16)
    starts = table_starts(tile, step, first_block, parity, blocks)
    query_grad = jnp.zeros((tile, width), f32)
    for part in range(key_count // chunk):
        cols = slice(part * chunk, (part + 1) * chunk)
        prob_grad = lax.dot_general(
            scaled, values[cols, :], (((1,), (1,)), ((), ())), preferred_element_type=f32
        )
        low = probs_ref[0, :, cols]
        score_grad = low.astype(f32) * (prob_grad - delta)
        for sub in range(subs):
            rows = slice(sub * BLOCK, (sub + 1) * BLOCK)
            offset = pl.multiple_of(starts[sub] + part * chunk, BLOCK)
            diagonals[:, pl.ds(offset, chunk)] += score_grad[rows]
        score_low = score_grad.astype(bf16)
        query_grad = query_grad + jnp.dot(score_low, keys[cols, :], preferred_element_type=f32)
        key_sums[:, cols] += jnp.dot(query_turned, score_low, preferred_element_type=f32)
        value_sums[:, cols] += jnp.dot(grad_turned, low, preferred_element_type=f32)
    query_grad_ref[0] = query_grad.astype(bf16)

    @pl.when(step == pl.num_programs(1) - 1)
    def finish():
        span = diagonals.shape[1]
        eight = diagonals[0:8, :]
        for group in range(1, BLOCK // 8):
            eight = eight + pltpu.roll(
                diagonals[8 * group : 8 * group + 8, :], span - 8 * group, 1
            )
        total = eight[0:1, :]
        for r in range(1, 8):
            total = total + pltpu.roll(eight[r : r + 1, :], span - r, 1)
        total = pltpu.roll(total, BLOCK - 1, 1)
        bucket_sums = None
        for unused in range(3):
            low = total.astype(bf16)
            total = total - low.astype(f32)
            more = jnp.dot(low, hot_ref[...], preferred_element_type=f32)
            bucket_sums = more if bucket_sums is None else bucket_sums + more
        offset_ref[0] = bucket_sums
        for sums, rows in ((key_sums, slice(0, width)), (value_sums, slice(width, 2 * width))):
            for b in range(blocks // 2):
                near = pl.multiple_of((2 * b + parity) * BLOCK, BLOCK)
                far = pl.multiple_of((2 * b + 1 - parity) * BLOCK, BLOCK)
                lanes = slice(b * BLOCK, (b + 1) * BLOCK)
                own_grad_ref[0, rows, lanes] = sums[:, pl.ds(near, BLOCK)].astype(bf16)
                other_grad_ref[0, rows, lanes] = sums[:, pl.ds(far, BLOCK)].astype(bf16)


def attend_back(place, grad, kept, inverse, probs, query, own, other, hot):
    count, rows, width = query.shape
    own_rows = own.shape[1]
    key_count = 2 * own_rows
    span = key_count * 2
    tile, chunk = 512, 512
    pairs = pl.BlockSpec((1, own_rows, 2 * width), lambda h, i, s: (h, 0, 0))
    return pl.pallas_call(
        functools.partial(attend_back_kernel, tile, chunk),
        grid_spec=pltpu.PrefetchScalarGridSpec(
            num_scalar_prefetch=1,
            grid=(count, rows // tile),
            in_specs=[
                pl.BlockSpec(
                    (tile // BLOCK, width, BLOCK), lambda h, i, s: (i, h, 0)
                ),
                pl.BlockSpec((1, tile, 2 * width), lambda h, i, s: (h, i, 0)),
                pl.BlockSpec((1, tile // BLOCK, 1, BLOCK), lambda h, i, s: (h, i, 0, 0)),
                pl.BlockSpec((1, tile, key_count), lambda h, i, s: (h, i, 0)),
                pl.BlockSpec((1, tile, width), lambda h, i, s: (h, i, 0)),
                pairs,
                pairs,
                pl.BlockSpec(hot.shape, lambda h, i, s: (0, 0)),
            ],
            out_specs=[
                pl.BlockSpec((1, tile, width), lambda h, i, s: (h, i, 0)),
                pl.BlockSpec((1, 2 * width, own_rows), lambda h, i, s: (h, 0, 0)),
                pl.BlockSpec((1, 2 * width, own_rows), lambda h, i, s: (h, 0, 0)),
                pl.BlockSpec((1, 1, hot.shape[1]), lambda h, i, s: (h, 0, 0)),
            ],
            scratch_shapes=[
                pltpu.VMEM((key_count, width), bf16),
                pltpu.VMEM((key_count, width), bf16),
                pltpu.VMEM((BLOCK, span), f32),
                pltpu.VMEM((width, key_count), f32),
                pltpu.VMEM((width, key_count), f32),
            ],
        ),
        out_shape=[
            jax.ShapeDtypeStruct((count, rows, width), bf16),
            jax.ShapeDtypeStruct((count, 2 * width, own_rows), bf16),
            jax.ShapeDtypeStruct((count, 2 * width, own_rows), bf16),
            jax.ShapeDtypeStruct((count, 1, hot.shape[1]), f32),
        ],
        compiler_params=vmem_limit(54),
        cost_estimate=pl.CostEstimate(
            flops=32 * count * rows * key_count * width,
            bytes_accessed=2 * count * rows * key_count,
            transcendentals=0,
        ),
        name="attend_back",
    )(place, grad, kept, inverse, probs, query, own, other, hot)


def project_back_kernel(
    place_ref,
    normed_ref,
    weight_ref,
    extra_ref,
    query_grad_ref,
    own_ref,
    came_ref,
    kept_rows,
    sent_rows,
    kept_ref,
    sent_ref,
    turned,
    sums,
    gains,
):
    step = pl.program_id(0)
    heads, unused, width = query_grad_ref.shape
    part = heads * width
    for head in range(heads):
        turned[head * width : (head + 1) * width, :] = query_grad_ref[head].T
        both = (own_ref[head].astype(f32) + came_ref[head].astype(f32)).astype(bf16)
        for side in range(2):
            at = part * (side + 1) + head * width
            turned[at : at + width, :] = both[side * width : (side + 1) * width]
    grads = turned[...]
    normed_grad = lax.dot_general(
        grads,
        weight_ref[:, : 3 * part],
        (((0,), (1,)), ((), ())),
        preferred_element_type=f32,
    )
    low = normed_grad.astype(bf16)
    half = low.shape[0] // 2
    for k in range(2):

        @pl.when(place_ref[0] == k)
        def store():
            kept_rows[0] = low[k * half : (k + 1) * half]
            sent_rows[0] = low[(1 - k) * half : (2 - k) * half]

    gain = jnp.sum(normed_grad * normed_ref[...].astype(f32), axis=0, keepdims=True)
    update = jnp.dot(grads, normed_ref[...], preferred_element_type=f32)

    @pl.when(step == 0)
    def start():
        sums[...] = update
        gains[...] = extra_ref[...]

    @pl.when(step != 0)
    def more():
        sums[...] += update

    gains[0:1, :] += gain / extra_ref[3:4, :]

    @pl.when(step == pl.num_programs(0) - 1)
    def finish():
        update = sums[...].T
        model = update.shape[0]
        extras = jnp.concatenate(
            [gains[...], jnp.zeros((BLOCK - gains.shape[0], model), f32)], axis=0
        ).T
        owners, rows, columns = kept_ref.shape
        for k in range(2):

            @pl.when(place_ref[1] == k)
            def pack():
                for owner in range(owners):
                    for ref, core in ((kept_ref, k), (sent_ref, 1 - k)):
                        at = slice((2 * owner + core) * rows, (2 * owner + core + 1) * rows)
                        ref[owner, :, : 3 * part] = update[at].astype(bf16)
                        ref[owner, :, 3 * part :] = extras[at].astype(bf16)


def project_back(place, query_grad, own, came, normed, weight, extra, weight_rows):
    rows, model = normed.shape
    heads, unused, width = query_grad.shape
    part = heads * width
    tile = 2 * BLOCK
    steps = rows // tile
    whole = lambda shape: pl.BlockSpec(shape, lambda i, s: (0, 0))
    pairs = pl.BlockSpec((heads, 2 * width, tile), lambda i, s: (0, 0, i))
    share = pl.BlockSpec((1, BLOCK, model), lambda i, s: (i, 0, 0))
    packed = (model // (2 * weight_rows), weight_rows, 3 * part + BLOCK)
    return pl.pallas_call(
        project_back_kernel,
        grid_spec=pltpu.PrefetchScalarGridSpec(
            num_scalar_prefetch=1,
            grid=(steps,),
            in_specs=[
                pl.BlockSpec((tile, model), lambda i, s: (i, 0)),
                whole(weight.shape),
                whole(extra.shape),
                pl.BlockSpec((heads, tile, width), lambda i, s: (0, i, 0)),
                pairs,
                pairs,
            ],
            out_specs=[share] * 2 + [pl.BlockSpec(packed, lambda i, s: (0, 0, 0))] * 2,
            scratch_shapes=[
                pltpu.VMEM((3 * part, tile), bf16),
                pltpu.VMEM((3 * part, model), f32),
                pltpu.VMEM(extra.shape, f32),
            ],
        ),
        out_shape=[jax.ShapeDtypeStruct((steps, BLOCK, model), bf16)] * 2
        + [jax.ShapeDtypeStruct(packed, bf16)] * 2,
        compiler_params=vmem_limit(60),
        cost_estimate=pl.CostEstimate(
            flops=12 * rows * model * part, bytes_accessed=12 * rows * model, transcendentals=0
        ),
        name="project_back",
    )(place, normed, weight, extra, query_grad, own, came)


def rows_kernel(place_ref, token_ref, residual_ref, gain_ref, own_ref, other_ref, grad_ref):
    seqs, local_rows, model = token_ref.shape
    for k, normed_ref in enumerate((own_ref, other_ref)):
        seq = place_ref[0] ^ k
        weighted = normed_ref[...].astype(f32) * gain_ref[...]
        tokens = token_ref[seq].astype(f32)
        scale = lax.rsqrt(jnp.mean(tokens * tokens, axis=-1, keepdims=True) + epsilon)
        inner = jnp.mean(weighted * tokens, axis=-1, keepdims=True)
        rows = pl.ds(pl.multiple_of(seq * local_rows, local_rows), local_rows)
        grad_ref[seq] = (
            residual_ref[rows] + scale * weighted - tokens * (scale * scale * scale * inner)
        )


def rows_stage(place, tokens, residual_grad, gain_row, own, other):
    whole = lambda array: pl.BlockSpec(array.shape, lambda i, s: (0,) * array.ndim)
    given = (tokens, residual_grad, gain_row, own, other)
    return pl.pallas_call(
        rows_kernel,
        grid_spec=pltpu.PrefetchScalarGridSpec(
            num_scalar_prefetch=1,
            grid=(1,),
            in_specs=[whole(array) for array in given],
            out_specs=whole(tokens),
        ),
        out_shape=jax.ShapeDtypeStruct(tokens.shape, f32),
        compiler_params=vmem_limit(16),
        cost_estimate=pl.CostEstimate(
            flops=20 * tokens.size, bytes_accessed=16 * tokens.size, transcendentals=0
        ),
        name="rows_stage",
    )(place, *given)


def output_kernel(context_ref, token_ref, gain_ref, *refs):
    weights, (residual_ref, normed_ref) = refs[:-2], refs[-2:]
    seqs, local_rows, model = token_ref.shape
    groups = context_ref.shape[0] // seqs
    part = context_ref.shape[1]
    for seq in range(seqs):
        rows = slice(seq * local_rows, (seq + 1) * local_rows)
        for p, weight_ref in enumerate(weights):
            lanes = slice(p * PANEL, (p + 1) * PANEL)
            weight = weight_ref[...].reshape(model, PANEL)
            total = token_ref[seq, :, lanes].astype(f32)
            for group in range(groups):
                total = total + lax.dot_general(
                    context_ref[seq * groups + group],
                    weight[group * part : (group + 1) * part],
                    (((0,), (0,)), ((), ())),
                    preferred_element_type=f32,
                )
            residual_ref[rows, lanes] = total
    normed_ref[...] = rms_scale(residual_ref[...], gain_ref[...]).astype(bf16)


def output_stage(context, tokens, gain_row, everything, shape):
    seqs, local_rows, model = tokens.shape
    whole = lambda array: pl.BlockSpec(array.shape, lambda i: (0,) * array.ndim)
    return pl.pallas_call(
        output_kernel,
        grid=(1,),
        in_specs=[whole(context), whole(tokens), whole(gain_row)] + shape.output_specs(),
        out_specs=[pl.BlockSpec((seqs * local_rows, model), lambda i: (0, 0))] * 2,
        out_shape=[
            jax.ShapeDtypeStruct((seqs * local_rows, model), f32),
            jax.ShapeDtypeStruct((seqs * local_rows, model), bf16),
        ],
        compiler_params=vmem_limit(16),
        cost_estimate=pl.CostEstimate(
            flops=2 * seqs * local_rows * model * model,
            bytes_accessed=2 * model * model,
            transcendentals=0,
        ),
        name="output_stage",
    )(context, tokens, gain_row, *[everything] * shape.panels)


def hidden_kernel(shape, normed_own, normed_other, down_own, down_other, gate_w, upper_w, *refs):
    panels = shape.panels
    down_w = refs[:panels]
    norm_own, norm_other, hidden_ref, gate_ref, upper_ref = refs[panels : panels + 5]
    normed, downs, lows, sides, pres = refs[panels + 5 :]
    step = pl.program_id(0)
    half = normed_own.shape[0]

    @pl.when(step == 0)
    def gather():
        normed[:half] = normed_own[...]
        normed[half:] = normed_other[...]
        downs[:half] = down_own[...]
        downs[half:] = down_other[...]

    across = (((1,), (1,)), ((), ()))
    weights = []
    for side, weight_ref in enumerate((gate_w, upper_w)):
        weight = weight_ref[...].reshape(shape.model, PANEL)
        sides[side, step] = weight
        pres[side] = jnp.dot(normed[...], weight, preferred_element_type=f32)
    down = jnp.concatenate([ref[...].reshape(PANEL, PANEL) for ref in down_w], axis=1)
    pres[2] = lax.dot_general(downs[...], down, across, preferred_element_type=f32)
    slope = 0.7978845608028654
    tile = 64

    def bend_rows(k, carried):
        rows = pl.ds(pl.multiple_of(k * tile, tile), tile)
        gate_pre, up_pre, hidden_grad = pres[0, rows], pres[1, rows], pres[2, rows]
        square = gate_pre * gate_pre
        bend = jnp.tanh(slope * gate_pre * (1.0 + 0.044715 * square))
        share = 0.5 * (1.0 + bend)
        curved = gate_pre * share
        steep = share + 0.5 * gate_pre * (1.0 - bend * bend) * (
            slope * (1.0 + 3.0 * 0.044715 * square)
        )
        hidden_ref[rows] = (curved * up_pre).astype(bf16)
        gate_low = (hidden_grad * up_pre * steep).astype(bf16)
        up_low = (hidden_grad * curved).astype(bf16)
        gate_ref[rows], upper_ref[rows] = gate_low, up_low
        lows[0, step, rows], lows[1, step, rows] = gate_low, up_low
        return carried

    lax.fori_loop(0, 2 * half // tile, bend_rows, 0)

    @pl.when(step == shape.steps - 1)
    def finish():
        for rows, ref in ((slice(0, half), norm_own), (slice(half, 2 * half), norm_other)):
            total = None
            for side in range(2):
                for k in range(shape.steps):
                    more = lax.dot_general(
                        lows[side, k, rows], sides[side, k], across, preferred_element_type=f32
                    )
                    total = more if total is None else total + more
            ref[...] = total.astype(ref.dtype)


def hidden_back_kernel(
    shape,
    place_ref,
    normed_own,
    normed_other,
    down_own,
    down_other,
    hidden_ref,
    gate_ref,
    upper_ref,
    output_ref,
    *refs,
):
    panels = shape.panels
    down_w = refs[:panels]
    out_own, out_other = refs[panels : panels + 2]
    grad_refs, (turned, downs, outs) = refs[panels + 2 : -3], refs[-3:]
    step = pl.program_id(0)
    x, dp = place_ref[0], place_ref[1]
    half = normed_own.shape[0]

    @pl.when(step == 0)
    def gather():
        turned[:, :half] = normed_own[...].T
        turned[:, half:] = normed_other[...].T
        downs[:half] = down_own[...]
        downs[half:] = down_other[...]
        shape.store_output(grad_refs, output_ref, x)

    hidden = hidden_ref[...]
    down = jnp.concatenate([ref[...].reshape(PANEL, PANEL) for ref in down_w], axis=1)
    product = jnp.dot(hidden, down, preferred_element_type=f32)

    @pl.when(step == 0)
    def first_out():
        outs[...] = product

    @pl.when(step != 0)
    def later_out():
        outs[...] += product

    for side, ref in enumerate((gate_ref, upper_ref)):
        grad = jnp.dot(turned[...], ref[...], preferred_element_type=f32)
        shape.store_side(grad_refs, step, side, grad, x, dp)
    grad = jnp.dot(hidden.T, downs[...], preferred_element_type=f32)
    for p in range(panels):
        shape.store_down(grad_refs, step, p, grad[:, p * PANEL : (p + 1) * PANEL], x, dp)

    @pl.when(step == shape.steps - 1)
    def finish():
        out_own[...] = outs[:half]
        out_other[...] = outs[half:].astype(bf16)


class PackedWeights:
    def __init__(self, model, hidden_half, pieces):
        self.model, self.pieces = model, pieces
        self.side = model // pieces
        self.deep = hidden_half // pieces
        self.steps = hidden_half // PANEL
        self.panels = model // PANEL
        self.side_rows = 2 * self.steps * self.side
        self.grad_rows = self.side_rows + self.panels * self.deep

    def side_spec(self, shift):
        return pl.BlockSpec((self.pieces, self.side, PANEL), lambda j: (0, j + shift, 0))

    def down_specs(self):
        if self.pieces == 1:
            first = self.side_rows // PANEL
            each = self.deep // PANEL
            return [
                pl.BlockSpec((1, PANEL, PANEL), lambda j, p=p: (0, first + p * each + j, 0))
                for p in range(self.panels)
            ]
        first = self.side_rows // self.deep
        some = self.pieces // self.steps
        return [
            pl.BlockSpec((some, self.deep, PANEL), lambda j, p=p: (j, first + p, 0))
            for p in range(self.panels)
        ]

    def output_specs(self):
        first = self.grad_rows // self.side
        return [
            pl.BlockSpec((self.pieces, self.side, PANEL), lambda j, p=p: (0, first + p, 0))
            for p in range(self.panels)
        ]

    def grad_shapes(self):
        if self.pieces == 1:
            return [(1, self.grad_rows, PANEL)]
        side = self.steps * self.side
        first = (self.pieces // 2, side + self.deep + self.panels * 32, PANEL)
        second = (self.pieces // 2, side + (self.panels - 1) * self.deep, PANEL)
        return [first, first, second, second]

    def store_output(self, refs, output_ref, x):
        if self.pieces == 1:
            return
        owners, rows, model = output_ref.shape
        pairs = output_ref[...].reshape(owners // 2, 2, rows, model)
        start = self.steps * self.side + self.deep
        short = jnp.zeros((owners // 2, 32 - rows, PANEL), bf16)
        for k in range(2):

            @pl.when(x == k)
            def store():
                for p in range(self.panels):
                    lanes = slice(p * PANEL, (p + 1) * PANEL)
                    at = slice(start + 32 * p, start + 32 * (p + 1))
                    for slot, side in ((0, k), (1, 1 - k)):
                        refs[slot][:, at, :] = jnp.concatenate(
                            [pairs[:, side, :, lanes], short], axis=1
                        )

    def store_side(self, refs, step, side, value, x, dp):
        low = value.astype(bf16).reshape(self.pieces, self.side, PANEL)
        if self.pieces == 1:
            start = pl.multiple_of((step + side * self.steps) * self.side, 16)
            refs[0][:, pl.ds(start, self.side), :] = low
            return
        rows = pl.ds(pl.multiple_of(step * self.side, 16), self.side)
        half = self.pieces // 2
        if side:
            for k in range(2):

                @pl.when(dp == k)
                def store_upper():
                    refs[2][:, rows, :] = low[k * half : (k + 1) * half]
                    refs[3][:, rows, :] = low[(1 - k) * half : (2 - k) * half]
        else:
            pairs = low.reshape(half, 2, self.side, PANEL)
            for k in range(2):

                @pl.when(x == k)
                def store_gate():
                    refs[0][:, rows, :] = pairs[:, k]
                    refs[1][:, rows, :] = pairs[:, 1 - k]

    def store_down(self, refs, step, p, value, x, dp):
        low = value.astype(bf16)
        if self.pieces == 1:
            start = pl.multiple_of(self.side_rows + p * self.deep + step * PANEL, PANEL)
            refs[0][0, pl.ds(start, PANEL), :] = low
            return
        some = self.pieces // self.steps
        first = self.steps * self.side
        if p == 0:
            pairs = low.reshape(some // 2, 2, self.deep, PANEL)
            spots = pl.ds(step * (some // 2), some // 2)
            for k in range(2):

                @pl.when(x == k)
                def store_first():
                    refs[0][spots, first : first + self.deep, :] = pairs[:, k]
                    refs[1][spots, first : first + self.deep, :] = pairs[:, 1 - k]
        else:
            pieces = low.reshape(some, self.deep, PANEL)
            per_half = self.steps // 2
            spots = pl.ds((step % per_half) * some, some)
            first += (p - 1) * self.deep
            for slot, mine in ((2, step // per_half == dp), (3, step // per_half != dp)):

                @pl.when(mine)
                def store_other():
                    refs[slot][spots, first : first + self.deep, :] = pieces


def hidden_stage(normed, normed_other, down, down_other, everything, shape):
    half, model = normed.shape
    whole = pl.BlockSpec((half, model), lambda j: (0, 0))
    panel = pl.BlockSpec((2 * half, PANEL), lambda j: (0, j))
    units = shape.steps * PANEL
    return pl.pallas_call(
        functools.partial(hidden_kernel, shape),
        grid=(shape.steps,),
        in_specs=[whole] * 4
        + [shape.side_spec(0), shape.side_spec(shape.steps)]
        + shape.down_specs(),
        out_specs=[whole] * 2 + [panel] * 3,
        out_shape=[
            jax.ShapeDtypeStruct((half, model), f32),
            jax.ShapeDtypeStruct((half, model), bf16),
        ]
        + [jax.ShapeDtypeStruct((2 * half, units), bf16)] * 3,
        scratch_shapes=[
            pltpu.VMEM((2 * half, model), bf16),
            pltpu.VMEM((2 * half, model), bf16),
            pltpu.VMEM((2, shape.steps, 2 * half, PANEL), bf16),
            pltpu.VMEM((2, shape.steps, model, PANEL), bf16),
            pltpu.VMEM((3, 2 * half, PANEL), f32),
        ],
        compiler_params=vmem_limit(26),
        cost_estimate=pl.CostEstimate(
            flops=10 * 2 * half * model * units, bytes_accessed=12 * model * units, transcendentals=0
        ),
        name="hidden_stage",
    )(normed, normed_other, down, down_other, *[everything] * (2 + shape.panels))


def hidden_back(place, normed, normed_other, down, down_other, lows, output, everything, shape):
    half, model = normed.shape
    whole = pl.BlockSpec((half, model), lambda j, s: (0, 0))
    panel = pl.BlockSpec((2 * half, PANEL), lambda j, s: (0, j))
    with_place = lambda spec: pl.BlockSpec(
        spec.block_shape, lambda j, s, spec=spec: spec.index_map(j)
    )
    grads = shape.grad_shapes()
    units = shape.steps * PANEL
    return pl.pallas_call(
        functools.partial(hidden_back_kernel, shape),
        grid_spec=pltpu.PrefetchScalarGridSpec(
            num_scalar_prefetch=1,
            grid=(shape.steps,),
            in_specs=[whole] * 4
            + [panel] * 3
            + [pl.BlockSpec(output.shape, lambda j, s: (0, 0, 0))]
            + [with_place(spec) for spec in shape.down_specs()],
            out_specs=[whole] * 2 + [pl.BlockSpec(size, lambda j, s: (0, 0, 0)) for size in grads],
            scratch_shapes=[
                pltpu.VMEM((model, 2 * half), bf16),
                pltpu.VMEM((2 * half, model), bf16),
                pltpu.VMEM((2 * half, model), f32),
            ],
        ),
        out_shape=[
            jax.ShapeDtypeStruct((half, model), f32),
            jax.ShapeDtypeStruct((half, model), bf16),
        ]
        + [jax.ShapeDtypeStruct(size, bf16) for size in grads],
        compiler_params=vmem_limit(60),
        cost_estimate=pl.CostEstimate(
            flops=8 * 2 * half * model * units, bytes_accessed=12 * model * units, transcendentals=0
        ),
        name="hidden_back",
    )(
        place, normed, normed_other, down, down_other, *lows, output, *[everything] * shape.panels
    )


def output_back_kernel(norm_own, norm_other, residual_ref, down_ref, gain_ref, context_ref, *refs):
    weights = refs[:-4]
    rows_ref, gain_grad_ref, context_grad_ref, weight_grad_ref = refs[-4:]
    residual, gain = residual_ref[...], gain_ref[...]
    norm_grad = norm_own[...] + norm_other[...].astype(f32)
    scale = lax.rsqrt(jnp.mean(residual * residual, axis=-1, keepdims=True) + epsilon)
    gain_grad_ref[...] = jnp.sum(norm_grad * (residual * scale), axis=0, keepdims=True)
    weighted = norm_grad * gain
    inner = jnp.mean(weighted * residual, axis=-1, keepdims=True)
    rows_grad = (
        down_ref[...].astype(f32)
        + scale * weighted
        - residual * (scale * scale * scale * inner)
    )
    rows_ref[...] = rows_grad
    low = rows_grad.astype(bf16)
    blocks, part, local_rows = context_ref.shape
    seqs = rows_grad.shape[0] // local_rows
    groups = blocks // seqs
    model = residual.shape[1]
    for group in range(groups):
        columns = slice(group * part, (group + 1) * part)
        product = None
        for p, weight_ref in enumerate(weights):
            more = lax.dot_general(
                weight_ref[...].reshape(model, PANEL)[columns],
                low[:, p * PANEL : (p + 1) * PANEL],
                (((1,), (1,)), ((), ())),
                preferred_element_type=f32,
            )
            product = more if product is None else product + more
        turned = product.astype(bf16)
        total = None
        for seq in range(seqs):
            rows = slice(seq * local_rows, (seq + 1) * local_rows)
            context_grad_ref[seq * groups + group] = turned[:, rows]
            more = jnp.dot(
                context_ref[seq * groups + group], low[rows], preferred_element_type=f32
            )
            total = more if total is None else total + more
        weight_grad_ref[columns, :] = total.astype(bf16)


def output_back(norm_own, norm_other, residual, down, gain_row, context, everything, shape):
    rows, model = residual.shape
    whole = lambda array: pl.BlockSpec(array.shape, lambda i: (0,) * array.ndim)
    given = (norm_own, norm_other, residual, down, gain_row, context)
    out_shape = [
        jax.ShapeDtypeStruct((rows, model), f32),
        jax.ShapeDtypeStruct((1, model), f32),
        jax.ShapeDtypeStruct(context.shape, bf16),
        jax.ShapeDtypeStruct((model, model), bf16),
    ]
    return pl.pallas_call(
        output_back_kernel,
        grid=(1,),
        in_specs=[whole(array) for array in given] + shape.output_specs(),
        out_specs=[whole(array) for array in out_shape],
        out_shape=out_shape,
        compiler_params=vmem_limit(16),
        cost_estimate=pl.CostEstimate(
            flops=4 * rows * model * model, bytes_accessed=4 * model * model, transcendentals=0
        ),
        name="output_back",
    )(*given, *[everything] * shape.panels)


def owned_kernel(part, term_ref, *refs):
    groups, rows, columns = term_ref.shape
    extras = None
    for group in range(groups):
        term = term_ref[group].astype(f32)
        for k in range(3):
            refs[k][:, group * part : (group + 1) * part] = term[:, k * part : (k + 1) * part]
        more = term[:, 3 * part :]
        extras = more if extras is None else extras + more
    short = jnp.zeros((BLOCK - rows, BLOCK), f32)
    refs[3][...] = jnp.concatenate([extras, short], axis=0).T[:8]


def owned_stage(terms, model, part):
    groups, rows, columns = terms.shape
    whole = lambda array: pl.BlockSpec(array.shape, lambda i: (0,) * array.ndim)
    out_shape = [jax.ShapeDtypeStruct((rows, model), f32)] * 3 + [
        jax.ShapeDtypeStruct((8, BLOCK), f32)
    ]
    return pl.pallas_call(
        functools.partial(owned_kernel, part),
        grid=(1,),
        in_specs=[whole(terms)],
        out_specs=[whole(array) for array in out_shape],
        out_shape=out_shape,
        compiler_params=vmem_limit(16),
        cost_estimate=pl.CostEstimate(
            flops=terms.size, bytes_accessed=4 * terms.size, transcendentals=0
        ),
        name="owned_stage",
    )(terms)


def swap(value, axis):
    return lax.ppermute(value, axis, [(0, 1), (1, 0)])


def after(value, gate):
    return lax.optimization_barrier((value, gate))[0]


def pick(pair, index, axis):
    return lax.dynamic_index_in_dim(pair, index, axis, keepdims=False)


def in_order(mine, theirs, index, axis):
    return jnp.where(
        index == 0, jnp.stack([mine, theirs], axis), jnp.stack([theirs, mine], axis)
    )


def plus(mine, came):
    return (mine.astype(f32) + came.astype(f32)).astype(bf16)


def halve(value, index, name, axis):
    return plus(pick(value, index, axis), swap(pick(value, 1 - index, axis), name))


def columns_in_panels(weight):
    rows, cols = weight.shape
    return jnp.transpose(weight.reshape(rows, cols // PANEL, PANEL), (1, 0, 2)).reshape(
        rows * cols // PANEL, PANEL
    )


def own_half(weight, each, c):
    rows, cols = weight.shape
    return pick(weight.reshape(rows, cols // (2 * each), 2, each), c, 2).reshape(rows, cols // 2)


def body(
    inputs,
    w_query,
    w_key,
    w_value,
    w_output,
    w_gate,
    w_upper,
    w_down,
    gain_one,
    gain_two,
    bias_table,
    buckets,
    cotangent,
    sizes,
):
    along_dp, along_a = sizes
    dp, a, x, c = (lax.axis_index(name) for name in ("dp", "a", "x", "c"))
    zh, zl = lax.axis_index("zh"), lax.axis_index("zl")
    z, group = 2 * zh + zl, 2 * zl + x
    depth = 4
    seqs, local_rows, model = inputs.shape
    length = buckets.shape[0] // 2 + 1
    width = model // H
    heads = H // GROUPS
    part = heads * width
    weight_rows, hidden_units = w_gate.shape
    each = w_down.shape[0]
    own_count = depth * 2 * local_rows
    token_count = seqs * local_rows

    near = in_order(pick(inputs, zh, 0), swap(pick(inputs, 1 - zh, 0), "zh"), zh, 0)
    column = in_order(near, swap(near, "zl"), zl, 1)
    tokens_own = in_order(column, swap(column, "x"), x, 2).reshape(own_count, model)

    blocks = [
        jnp.transpose(w.reshape(weight_rows, GROUPS, part), (1, 0, 2))
        for w in (w_query, w_key, w_value)
    ]
    table_column = jnp.pad(bias_table, (0, weight_rows - bias_table.shape[0]))
    extra = jnp.stack([gain_one, gain_two, table_column], axis=1)
    extra = jnp.pad(extra, ((0, 0), (0, BLOCK - extra.shape[1])))
    extra = jnp.broadcast_to(extra[None], (GROUPS, weight_rows, BLOCK))
    columns = lax.all_to_all(
        jnp.concatenate([*blocks, extra], axis=2), ("zl", "x"), 0, 0, tiled=True
    )
    columns = in_order(columns, swap(columns, "zh"), zh, 0)
    if along_a > 1:
        columns = lax.all_gather(columns, "a", axis=0)
    columns = in_order(columns, swap(columns, "dp"), dp, 0)
    columns = in_order(columns, swap(columns, "c"), c, columns.ndim - 2)
    columns = columns.reshape(model, 3 * part + BLOCK)
    gain_a = columns[:, 3 * part].astype(f32).reshape(1, model)
    gain_b = columns[:, 3 * part + 1].astype(f32).reshape(1, model)
    table = columns[:, 3 * part + 2].reshape(model // weight_rows, weight_rows)
    table = table[:, : bias_table.shape[0]].reshape(BUCKETS, H)
    padded = jnp.pad(buckets, (0, 1), constant_values=BLOCK)
    hot = (padded[:, None] == jnp.arange(BLOCK, dtype=jnp.int32)[None, :]).astype(bf16)
    own_table = lax.dynamic_slice_in_dim(table, group * heads, heads, 1)
    own_table = jnp.pad(own_table, ((0, BLOCK - BUCKETS), (0, 0)))
    ahead = jnp.pad(buckets, (1, 0), constant_values=BLOCK)
    hot_ahead = (ahead[None, :] == jnp.arange(BLOCK, dtype=jnp.int32)[:, None]).astype(bf16)
    vectors = lax.dot_general(
        own_table, hot_ahead, (((0,), (0,)), ((), ())), preferred_element_type=f32
    ).reshape(heads, 1, 2 * length)

    if along_a == 1:
        sent = [own_half(w, each, 1 - c) for w in (w_gate, w_upper)] + [w_output]
        came = swap(jnp.concatenate(sent, axis=1), "c")
        kept = [own_half(w, each, c) for w in (w_gate, w_upper)] + [w_output]
        both = in_order(jnp.concatenate(kept, axis=1), came, c, 0).reshape(2 * weight_rows, -1)
        packed = jnp.concatenate(
            [
                columns_in_panels(both[:, :hidden_units]),
                columns_in_panels(w_down),
                columns_in_panels(both[:, hidden_units:]),
            ],
            axis=0,
        )
        pieces = along_dp * depth * 2
        everything = lax.all_gather(packed, chips, axis=0, tiled=True)
        everything = everything.reshape(pieces, packed.shape[0], PANEL)
    else:
        pieces = 1
        gate_all, upper_all, down_all, output_all = (
            lax.all_gather(w, everyone, axis=0, tiled=True)
            for w in (w_gate, w_upper, w_down, w_output)
        )
        down_half = pick(down_all.reshape(-1, 2, each, model), c, 1).reshape(-1, model)
        everything = jnp.concatenate(
            [
                columns_in_panels(own_half(gate_all, each, c)),
                columns_in_panels(own_half(upper_all, each, c)),
                columns_in_panels(down_half),
                columns_in_panels(output_all),
            ],
            axis=0,
        )[None]
    shape = PackedWeights(model, hidden_units // 2, pieces)

    if along_a > 1:
        tokens_all = lax.all_gather(tokens_own, "a", axis=0, tiled=True)
    else:
        tokens_all = tokens_own
    normed, query, own = project(tokens_all, gain_a, columns, heads, width)
    if along_a > 1:
        query = lax.dynamic_slice_in_dim(query, a * own_count, own_count, 1)
        normed = lax.dynamic_slice_in_dim(normed, a * own_count, own_count, 0)
    other = swap(own, "c")
    biases = skew(vectors)
    place = jnp.stack([a * (own_count // BLOCK), c]).astype(jnp.int32)
    place = after(place, hot)
    context_own, probs, kept, inverse = attend(place, query, own, other, biases)
    owners = ("zh", "zl", "x")
    context = lax.all_to_all(context_own, owners, 0, 0, tiled=True)

    down_grad = cotangent.reshape(token_count, model)
    down_other = swap(down_grad, "c")
    residual, second = output_stage(context, inputs, gain_b, everything, shape)
    second_other = swap(second, "c")
    sides_place = jnp.stack([x, dp]).astype(jnp.int32)
    norm_own, norm_other, *lows = hidden_stage(
        second, second_other, down_grad, down_other, everything, shape
    )
    norm_came = swap(norm_other, "c")
    residual_grad, gain_b_grad, context_sent, output_grad = output_back(
        norm_own, norm_came, residual, down_grad, gain_b, context, everything, shape
    )
    *lows, output_grad, context_sent = lax.optimization_barrier(
        (*lows, output_grad, context_sent)
    )
    context_grad = lax.all_to_all(context_sent, owners, 0, 0, tiled=True)
    output_terms = halve(
        output_grad.reshape(model // (2 * weight_rows), CORES, weight_rows, model), c, "c", 1
    )
    out_own, out_other, *big_grads = hidden_back(
        sides_place,
        second,
        second_other,
        down_grad,
        down_other,
        lows,
        output_terms,
        everything,
        shape,
    )
    out_came = swap(out_other, "c")
    outputs = (residual + out_own + out_came.astype(f32)).astype(bf16)

    if along_a == 1:
        first_terms, first_sent, second_terms, second_sent = big_grads
        first_came = swap(first_sent, "x")
        second_came = swap(second_sent, "dp")
    query_grad, own_grad, other_grad, bucket_sums = attend_back(
        place, context_grad, kept, inverse, probs, query, own, other, hot
    )
    if along_a > 1:
        own_grad, other_grad = (
            lax.psum_scatter(value, "a", scatter_dimension=2, tiled=True)
            for value in (own_grad, other_grad)
        )
    else:
        first_came, second_came, query_grad, own_grad, other_grad, bucket_sums = (
            lax.optimization_barrier(
                (first_came, second_came, query_grad, own_grad, other_grad, bucket_sums)
            )
        )
        first_terms = plus(first_terms, first_came).reshape(along_dp, depth, -1, PANEL)
        second_terms = plus(second_terms, second_came).reshape(depth, 2, -1, PANEL)
        first_terms, second_terms, query_grad = lax.optimization_barrier(
            (first_terms, second_terms, query_grad)
        )
        first_came = swap(pick(first_terms, 1 - dp, 0), "dp")
        second_came = swap(pick(second_terms, 1 - x, 1), "x")
    came = swap(other_grad, "c")

    per_owner = bias_table.shape[0]
    bucket_sums = bucket_sums[:, 0, :BUCKETS]
    spot = jnp.arange(model, dtype=jnp.int32)
    entry = spot // weight_rows * per_owner + spot % weight_rows
    entry = jnp.where(spot % weight_rows < per_owner, entry, -1)
    spread = (entry[None, :] // H == jnp.arange(BUCKETS, dtype=jnp.int32)[:, None]).astype(bf16)
    table_rows = jnp.dot(bucket_sums.astype(bf16), spread, preferred_element_type=f32)
    own_heads = group * heads + jnp.arange(heads, dtype=jnp.int32)
    table_row = jnp.sum(
        jnp.where(entry[None, :] % H == own_heads[:, None], table_rows, 0.0), axis=0
    )
    extra = jnp.stack(
        [jnp.zeros((model,), f32), gain_b_grad.reshape(model), table_row, gain_a.reshape(model)]
        + [jnp.zeros((model,), f32)] * 4
    )
    core_place = jnp.stack([x, c]).astype(jnp.int32)
    *rows_grads, mixed, sent_c = project_back(
        core_place, query_grad, own_grad, came, normed, columns, extra, weight_rows
    )
    if along_a == 1:
        first_came, second_came = (
            after(value, sent_c) for value in (first_came, second_came)
        )

    by_owner = (along_dp, along_a, 2, GROUPS, weight_rows, mixed.shape[2])
    mixed, sent_c = mixed.reshape(by_owner), sent_c.reshape(by_owner)
    came_x = swap(rows_grads[1], "x")
    mixed = plus(mixed, swap(sent_c, "c"))
    if along_a == 1:
        terms = jnp.concatenate(
            [
                plus(pick(first_terms, dp, 0), first_came),
                plus(pick(second_terms, x, 1), second_came),
            ],
            axis=1,
        )
        terms = terms.reshape(2, 2, -1, PANEL)
        column_came = swap(pick(terms, 1 - zl, 1), "zl")
    came_dp = swap(pick(mixed, 1 - dp, 0), "dp")
    mixed = plus(pick(mixed, dp, 0), came_dp)
    came_zh = swap(pick(mixed, 1 - zh, 1), "zh")
    share = plus(rows_grads[0], came_x).reshape(2, 2, local_rows, model)
    share, sent = pick(share, zl, 1), pick(share, 1 - zl, 1)
    came_zl = swap(sent, "zl")
    if along_a == 1:
        column_came = after(column_came, sent)
        terms = plus(pick(terms, zl, 1), column_came)
        sent = pick(terms, 1 - zh, 0)
        column_came = swap(sent, "zh")
    share = plus(share, after(came_zl, sent))
    rows_own, sent = pick(share, zh, 0), pick(share, 1 - zh, 0)
    rows_came = swap(sent, "zh")
    came_zh = after(came_zh, sent)
    mixed = plus(pick(mixed, zh, 1), came_zh)
    if along_a > 1:
        mixed = lax.psum_scatter(mixed, "a", scatter_dimension=0, tiled=True)
    terms_owned = lax.all_to_all(mixed[0], ("zl", "x"), 0, 0, tiled=True)
    input_grad = rows_stage(
        zh.astype(jnp.int32)[None], inputs, residual_grad, gain_a, rows_own, rows_came
    )

    if along_a == 1:
        column_came = after(column_came, mixed)
        total = pick(terms, zh, 0).astype(f32) + column_came.astype(f32)
        side, deep = shape.steps * shape.side, shape.deep
        rest = total[side + deep + shape.panels * 32 :]
        output_owned = jnp.transpose(
            total[side + deep : side + deep + shape.panels * 32].reshape(shape.panels, 32, PANEL)[
                :, :weight_rows
            ],
            (1, 0, 2),
        ).reshape(weight_rows, model)
        sides = jnp.concatenate([total[:side], rest[:side]], axis=0)
        sides = sides.astype(bf16).reshape(-1, 2, weight_rows, PANEL)
        sides = in_order(pick(sides, c, 1), swap(pick(sides, 1 - c, 1), "c"), c, 0)
        sides = sides.reshape(2, 2, shape.steps, weight_rows, PANEL)
        sides = jnp.transpose(
            sides.reshape(2, 2, shape.steps, weight_rows, PANEL // each, each), (1, 3, 2, 4, 0, 5)
        ).reshape(2, weight_rows, hidden_units)
        gate_owned, upper_owned = sides[0].astype(f32), sides[1].astype(f32)
        down_owned = jnp.transpose(
            jnp.concatenate([total[side : side + deep], rest[side:]], axis=0).reshape(
                shape.panels, each, PANEL
            ),
            (1, 0, 2),
        ).reshape(each, model)
    else:
        side = shape.steps * model
        gate_half, upper_half = (
            jnp.transpose(
                big_grads[0][0, k * side : (k + 1) * side].reshape(shape.steps, model, PANEL),
                (1, 0, 2),
            ).reshape(model, -1, 1, each)
            for k in range(2)
        )
        down_half = jnp.transpose(
            big_grads[0][0, 2 * side :].reshape(shape.panels, -1, PANEL), (1, 0, 2)
        ).reshape(-1, 1, each, model)
        zero = jnp.zeros_like
        output_owned = lax.psum_scatter(
            in_order(output_terms, zero(output_terms), c, 1).reshape(model, model),
            everyone,
            scatter_dimension=0,
            tiled=True,
        ).astype(f32)
        gate_owned, upper_owned = (
            lax.psum_scatter(
                in_order(half, zero(half), c, 2).reshape(model, hidden_units),
                everyone,
                scatter_dimension=0,
                tiled=True,
            ).astype(f32)
            for half in (gate_half, upper_half)
        )
        down_owned = lax.psum_scatter(
            in_order(down_half, zero(down_half), c, 1).reshape(hidden_units, model),
            everyone,
            scatter_dimension=0,
            tiled=True,
        ).astype(f32)

    *owned, extras = owned_stage(terms_owned, model, part)
    return (
        outputs.reshape(seqs, local_rows, model),
        input_grad,
        *owned,
        output_owned,
        gate_owned,
        upper_owned,
        down_owned,
        extras[0, :weight_rows],
        extras[1, :weight_rows],
        extras[2, :per_owner],
    )


def solution(mesh):
    along_dp, along_ctx = mesh.shape["dp"], mesh.shape["ctx"]
    along_a = along_ctx // (4 * 2 * CORES)
    fine = Mesh(mesh.devices.reshape(along_dp, along_a, 2, 2, 2, CORES), everyone)
    rows = P("dp", ("a", "zh", "zl", "x", "c"), None)
    owned = P(everyone, None)
    vector = P(everyone)
    in_specs = (rows, *[owned] * 7, *[vector] * 3, P(), rows)
    out_specs = (rows, rows, *[owned] * 7, *[vector] * 3)
    return jax.shard_map(
        functools.partial(body, sizes=(along_dp, along_a)),
        mesh=fine,
        in_specs=in_specs,
        out_specs=out_specs,
        check_vma=False,
    )
```
